32 devices in a mesh: wide: 8 (over z, core), narrow: 4 (over y, x).
Axes of the slice: x: 2, y: 2, z: 4, core: 2. Of those that a mesh axis runs over, the one named last changes fastest.
Arguments:
- block_input: bfloat16 [16384, 1536], P(('wide', 'narrow')), may hold values from -23 to 23
- routes: int32 [16384, 2], P('wide'), may hold values from 0 to 15, all different within a row
- first_gain: bfloat16 [1536], P('narrow'), may hold values from 0.099609375 to 1.8984375
- query_key_value_weight: bfloat16 [1536, 2560], P('wide', 'narrow'), may hold values from -0.15625 to 0.15625
- output_weight: bfloat16 [1536, 1536], P('narrow', 'wide'), may hold values from -4 to 4
- second_gain: bfloat16 [1536], P('narrow'), may hold values from 0.099609375 to 1.8984375
- router_weight: bfloat16 [1536, 16], P('wide'), may hold values from -0.109375 to 0.109375
- gate_weight: bfloat16 [16, 1536, 1024], P(None, 'wide', 'narrow'), may hold values from -0.15625 to 0.15625
- up_weight: bfloat16 [16, 1536, 1024], P(None, 'wide', 'narrow'), may hold values from -0.15625 to 0.15625
- down_weight: bfloat16 [16, 1536, 1024], P(None, 'wide', 'narrow'), may hold values from -0.375 to 0.375
- cotangent: bfloat16 [16384, 1536], P(('wide', 'narrow')), may hold values from -6 to 6
Outputs:
- block_output: bfloat16 [16384, 1536], P(('wide', 'narrow'))
- input_grad: float32 [16384, 1536], P(('wide', 'narrow'))
- first_gain_grad: float32 [1536], P('narrow')
- input_weight_grad: float32 [1536, 2560], P('wide', 'narrow')
- output_weight_grad: float32 [1536, 1536], P('narrow', 'wide')
- second_gain_grad: float32 [1536], P('narrow')
- router_weight_grad: float32 [1536, 16], P('wide')
- gate_weight_grad: float32 [16, 1536, 1024], P(None, 'wide', 'narrow')
- up_weight_grad: float32 [16, 1536, 1024], P(None, 'wide', 'narrow')
- down_weight_grad: float32 [16, 1536, 1024], P(None, 'wide', 'narrow')
The draws below stay inside these ranges and needn't reach their ends.
All inputs are finite; a program needn't handle non-finite values.
Results may differ from the reference program's by a relative error of at most 0.015.
The reference program's roundings to bfloat16 on the way count: a program that leaves them out, or rounds other values in their place, can miss the bound.
Values may be sent and summed in bfloat16 or wider, within the bound.
A program may use at most 576 MiB of HBM per device.

```python
import jax
import jax.numpy as jnp
from jax import lax

MODEL_WIDTH = 1536
QUERY_HEADS = 24
KEY_VALUE_HEADS = 8
HEAD_SIZE = 64
E = 16
F = 1024
TOPK = 2
SEQUENCE_LENGTH = 2048
QBLK = 512
BLOCK = 256
TOKENS = 16384


def draw_block_input(key, part):
    keys = jax.random.split(key, 3)
    row_scale = jnp.exp(jax.random.uniform(keys[0], (TOKENS, 1), jnp.float32, -1.15, 1.15))
    column_scale = jnp.exp(jax.random.uniform(keys[1], (1, MODEL_WIDTH), jnp.float32, -1.15, 1.15))
    base = jnp.clip(jax.random.normal(keys[2], (TOKENS, MODEL_WIDTH), jnp.float32), -4.5, 4.5)
    return (base * row_scale * column_scale * 0.5).astype(jnp.bfloat16)


def level_of(stream_key, dims, pieces, least, top_value):
    factor_of = 1.0
    for position, shards_of in pieces:
        heights = jax.random.uniform(jax.random.fold_in(jax.random.fold_in(stream_key, 6), position), (shards_of,), jnp.float32, least / len(pieces), top_value / len(pieces))
        factor_of = factor_of * jnp.repeat(jnp.exp(heights), dims[position] // shards_of).reshape((-1,) + (1,) * (len(dims) - 1 - position))
    return factor_of


def distinct(stream_key, rows, amount, top, lift):
    sequence = jax.random.permutation(jax.random.fold_in(stream_key, 1), amount)
    pull = sequence
    for power in range(3):
        pull = pull * pull // amount
    pull = pull * lift // amount
    lots = jax.random.randint(jax.random.fold_in(stream_key, 2), (rows, amount), 0, 4096) + pull
    sure = jax.random.permutation(jax.random.fold_in(stream_key, 3), rows)[jnp.arange(amount) % rows]
    lots = jnp.where(jnp.arange(rows)[:, None] == sure[None, :], 1 << 14, lots)
    score = lots * amount + jnp.arange(amount)
    return lax.top_k(score.astype(jnp.int32), top)[1].astype(jnp.int32)


def scatter_about(key, extent, spread, limit, cuts=(), kind=jnp.bfloat16):
    values = spread * jax.random.normal(key, extent, jnp.float32)
    if cuts:
        values = values * level_of(key, extent, cuts, -0.22, 0.18)
    return jnp.clip(values, -limit, limit).astype(kind)


def setup_inputs(seed: int = 0) -> dict:
    streams_of = jax.random.split(jax.random.key(seed), 12)
    block_input = draw_block_input(jax.random.fold_in(streams_of[11], 71), 0)
    routes = distinct(streams_of[1], TOKENS, E, TOPK, 1024)
    first_gain = jnp.clip(1.0 + 0.18 * jax.random.normal(streams_of[2], (MODEL_WIDTH,), jnp.float32), 0.099609375, 1.8984375).astype(jnp.bfloat16)
    query_key_value_weight = scatter_about(streams_of[3], (MODEL_WIDTH, (QUERY_HEADS + 2 * KEY_VALUE_HEADS) * HEAD_SIZE), MODEL_WIDTH ** -0.5, 0.15625, ((0, 8), (1, 4)))
    output_weight = scatter_about(streams_of[4], (QUERY_HEADS * HEAD_SIZE, MODEL_WIDTH), 2 ** -0.5, 4.0, ((0, 4), (1, 8)))
    second_gain = jnp.clip(1.0 + 0.18 * jax.random.normal(streams_of[5], (MODEL_WIDTH,), jnp.float32), 0.099609375, 1.8984375).astype(jnp.bfloat16)
    router_weight = scatter_about(streams_of[6], (MODEL_WIDTH, E), (2 * MODEL_WIDTH) ** -0.5, 0.109375, ((0, 8),))
    gate_weight = scatter_about(streams_of[7], (E, MODEL_WIDTH, F), MODEL_WIDTH ** -0.5, 0.15625, ((1, 8), (2, 4)))
    up_weight = scatter_about(streams_of[8], (E, MODEL_WIDTH, F), MODEL_WIDTH ** -0.5, 0.15625, ((1, 8), (2, 4)))
    down_weight = scatter_about(streams_of[9], (E, MODEL_WIDTH, F), (F // 4) ** -0.5, 0.375, ((1, 8), (2, 4)))
    cotangent = scatter_about(streams_of[10], (TOKENS, MODEL_WIDTH), 1.0, 6.0, ((0, 32),))
    return dict(block_input=block_input, routes=routes, first_gain=first_gain, query_key_value_weight=query_key_value_weight, output_weight=output_weight, second_gain=second_gain, router_weight=router_weight, gate_weight=gate_weight, up_weight=up_weight, down_weight=down_weight, cotangent=cotangent)


EPSILON = 1e-05
HIGH = lax.Precision.HIGHEST

@jax.custom_vjp
def low(v):
    return lax.optimization_barrier(v.astype(jnp.bfloat16)).astype(jnp.float32)

@jax.custom_vjp
def low_back(v):
    return v

def low_keep(v):
    return (low(v), None)

def low_pass(kept, grad):
    return (grad,)

def back_keep(v):
    return (v, None)

def back_low(kept, grad):
    return (low(grad),)
low.defvjp(low_keep, low_pass)
low_back.defvjp(back_keep, back_low)

def product(left, right):
    return jnp.dot(left, right, precision=HIGH, preferred_element_type=jnp.float32)

def arrange(experts_of):
    assigned = experts_of.shape[0] * experts_of.shape[1]
    flat_ids = experts_of.reshape(assigned).astype(jnp.int32)
    one_hot = (flat_ids[:, None] == jnp.arange(E, dtype=jnp.int32)[None, :]).astype(jnp.int32)
    expert_rows = lax.optimization_barrier(jnp.sum(one_hot, axis=0, dtype=jnp.int32))
    padded = (expert_rows + BLOCK - 1) // BLOCK * BLOCK
    block_ends = jnp.cumsum(padded, dtype=jnp.int32)
    starts = block_ends - padded
    before = jnp.cumsum(one_hot, axis=0, dtype=jnp.int32) - one_hot
    slot_of = lax.optimization_barrier(jnp.sum((before + starts[None, :]) * one_hot, axis=1, dtype=jnp.int32))
    buffer_rows = assigned + E * BLOCK
    row_owner = jnp.zeros((buffer_rows,), jnp.int32).at[slot_of].set(jnp.arange(assigned, dtype=jnp.int32))
    row_live = jnp.zeros((buffer_rows,), jnp.int32).at[slot_of].set(jnp.ones((assigned,), jnp.int32))
    firsts = jnp.arange(buffer_rows // BLOCK, dtype=jnp.int32) * BLOCK
    later = (firsts[:, None] >= block_ends[None, :]).astype(jnp.int32)
    block_expert = jnp.minimum(lax.optimization_barrier(jnp.sum(later, axis=1, dtype=jnp.int32)), E - 1)
    return (slot_of, row_owner, row_live, block_expert)

def attend(projected_rows):
    head_group = QUERY_HEADS // KEY_VALUE_HEADS
    weight_pieces = projected_rows.reshape(SEQUENCE_LENGTH, KEY_VALUE_HEADS, head_group + 2, HEAD_SIZE)
    queries = weight_pieces[:, :, :head_group, :]
    key_rows = weight_pieces[:, :, head_group, :]
    value_rows = weight_pieces[:, :, head_group + 1, :]
    positions = jnp.arange(SEQUENCE_LENGTH, dtype=jnp.int32)

    def block_out(start):
        query_rows = lax.dynamic_slice_in_dim(queries, start, QBLK, 0)
        scores = jnp.einsum('qgrd,kgd->grqk', query_rows, key_rows, precision=HIGH) * 0.125
        visible = (start + jnp.arange(QBLK, dtype=jnp.int32))[:, None] >= positions[None, :]
        scores = low_back(jnp.where(visible, scores, -1e+30))
        attn_probs = low(jax.nn.softmax(scores, axis=-1))
        return jnp.einsum('grqk,kgd->qgrd', attn_probs, value_rows, precision=HIGH)
    starts = jnp.arange(SEQUENCE_LENGTH // QBLK, dtype=jnp.int32) * QBLK
    blocks = lax.map(jax.checkpoint(block_out), starts)
    return blocks.reshape(SEQUENCE_LENGTH, QUERY_HEADS * HEAD_SIZE)

def experts(normed, experts_of, gates, gate_weight, up_weight, down_weight):
    slot_of, row_owner, row_live, block_expert = arrange(experts_of)
    token_of = row_owner // TOPK
    alive = row_live.astype(jnp.float32)
    rows_in = normed[token_of] * alive[:, None]
    row_gate = gates.reshape(-1)[row_owner] * alive
    block_count = block_expert.shape[0]

    def block_out(item):
        block_rows, expert = item
        gate_val = low_back(product(block_rows, gate_weight[expert]))
        up_val = low_back(product(block_rows, up_weight[expert]))
        active = low(jax.nn.silu(gate_val) * up_val)
        return low_back(product(active, down_weight[expert].T))
    outputs = lax.map(jax.checkpoint(block_out), (rows_in.reshape(block_count, BLOCK, MODEL_WIDTH), block_expert))
    weighted = outputs.reshape(block_count * BLOCK, MODEL_WIDTH) * row_gate[:, None]
    return jnp.zeros((experts_of.shape[0], MODEL_WIDTH), jnp.float32).at[token_of].add(weighted)

def layer(inputs, experts_of, first_gain, query_key_value_weight, output_weight, second_gain, router_weight, gate_weight, up_weight, down_weight):
    first_scale = lax.rsqrt(lax.optimization_barrier(jnp.mean(inputs * inputs, axis=1, keepdims=True)) + EPSILON)
    attn_in = low(inputs * first_scale * first_gain)
    projected_rows = low(low_back(product(attn_in, query_key_value_weight)))
    mixed = low(low_back(attend(projected_rows)))
    middle = inputs + low_back(product(mixed, output_weight))
    middle_low = low(middle)
    second_scale = lax.rsqrt(lax.optimization_barrier(jnp.mean(middle_low * middle_low, axis=1, keepdims=True)) + EPSILON)
    normed = low(middle_low * second_scale * second_gain)
    logits = low_back(product(normed, router_weight))
    chosen = jnp.take_along_axis(logits, experts_of, axis=1)
    gates = jax.nn.softmax(chosen, axis=1)
    return middle + experts(normed, experts_of, gates, gate_weight, up_weight, down_weight)

def reference(block_input, routes, first_gain, query_key_value_weight, output_weight, second_gain, router_weight, gate_weight, up_weight, down_weight, cotangent):
    seq_count = block_input.shape[0] // SEQUENCE_LENGTH
    route_blocks = routes.reshape(seq_count, SEQUENCE_LENGTH, TOPK).astype(jnp.int32)

    def forward(inputs, gain_one, weight_in, weight_out, gain_two, weight_router, weight_gate, weight_up, weight_down):

        def one_sequence(carry, item):
            result = layer(item[0], item[1], gain_one, weight_in, weight_out, gain_two, weight_router, weight_gate, weight_up, weight_down)
            return (carry, result)
        _, outputs = lax.scan(jax.checkpoint(one_sequence), jnp.zeros((), jnp.float32), (inputs.reshape(seq_count, SEQUENCE_LENGTH, MODEL_WIDTH), route_blocks))
        return outputs.reshape(seq_count * SEQUENCE_LENGTH, MODEL_WIDTH)
    output, pullback = jax.vjp(forward, block_input.astype(jnp.float32), first_gain.astype(jnp.float32), query_key_value_weight.astype(jnp.float32), output_weight.astype(jnp.float32), second_gain.astype(jnp.float32), router_weight.astype(jnp.float32), gate_weight.astype(jnp.float32), up_weight.astype(jnp.float32), down_weight.astype(jnp.float32))
    grads = pullback(cotangent.astype(jnp.float32))
    return (output.astype(jnp.bfloat16), grads[0], grads[1], grads[2], grads[3], grads[4], grads[5], grads[6], grads[7], grads[8])
```

```python
import functools

import jax
import jax.numpy as jnp
from jax import lax
from jax.experimental import pallas as pl
from jax.experimental.pallas import tpu as pltpu
from jax.sharding import PartitionSpec as P

QUERY_HEADS = 24
KEY_VALUE_HEADS = 8
HEAD_SIZE = 64
E = 16
TOPK = 2
SEQUENCE_LENGTH = 2048
BLOCK = 256
QB = 256
KB = 256
LANES = 128
PITCH = 16
UNROLL = 8
CHUNKS = (4, 4, 4, 4)
EPSILON = 1e-05
F32 = jnp.float32
BF16 = jnp.bfloat16

def stack_heads(ref, row, first, heads):
    return jnp.concatenate(
        [ref[row + h * HEAD_SIZE : row + (h + 1) * HEAD_SIZE, pl.ds(first, QB)] for h in range(heads)], axis=1
    )

def rows_of(block):
    return block.astype(jnp.float32).T.astype(jnp.bfloat16)

def forward_kernel(heads, qkv_ref, out_ref, total_ref, key_ref):
    index = pl.program_id(1)
    first = pl.multiple_of(index * QB, QB)
    key_row = heads * HEAD_SIZE
    value_row = key_row + HEAD_SIZE
    @pl.when(index == 0)
    def _():
        key_ref[...] = rows_of(qkv_ref[key_row:value_row, :])
    queries = stack_heads(qkv_ref, 0, first, heads) * jnp.bfloat16(0.125)
    lanes = heads * QB

    def step(block, carry, masked):
        highest, denominator, mixed = carry
        start = pl.multiple_of(block * KB, KB)
        scores = jnp.dot(key_ref[pl.ds(start, KB), :], queries, preferred_element_type=jnp.float32)
        if masked:
            key_at = lax.broadcasted_iota(jnp.int32, (KB, QB), 0)
            query_at = lax.broadcasted_iota(jnp.int32, (KB, QB), 1)
            seen = jnp.concatenate([key_at <= query_at] * heads, axis=1)
            scores = jnp.where(seen, scores, -1e30)
        raised_to = jnp.maximum(highest, jnp.max(scores, axis=0, keepdims=True))
        shrink = jnp.exp(highest - raised_to)
        raised = jnp.exp(scores - raised_to)
        denominator = denominator * shrink + jnp.sum(raised, axis=0, keepdims=True)
        mixed = mixed * shrink + jnp.dot(
            qkv_ref[value_row : value_row + HEAD_SIZE, pl.ds(start, KB)], raised.astype(jnp.bfloat16),
            preferred_element_type=jnp.float32)
        return raised_to, denominator, mixed

    carry = (jnp.full((1, lanes), -1e30, jnp.float32), jnp.zeros((1, lanes), jnp.float32), jnp.zeros((HEAD_SIZE, lanes), jnp.float32))
    carry = lax.fori_loop(0, index, lambda b, c: step(b, c, False), carry)
    highest, denominator, mixed = step(index, carry, True)
    mixed = (mixed / denominator).astype(jnp.bfloat16)
    for h in range(heads):
        out_ref[h * HEAD_SIZE : (h + 1) * HEAD_SIZE, :] = mixed[:, h * QB : (h + 1) * QB]
    total_ref[0, 0] = highest + jnp.log(denominator)

def attend_forward(qkv, groups, heads):
    tokens = qkv.shape[1]
    blocks = tokens // QB
    rows = (heads + 2) * HEAD_SIZE
    flops = groups * heads * tokens * tokens * HEAD_SIZE * 2
    return pl.pallas_call(
        functools.partial(forward_kernel, heads),
        grid=(groups, blocks),
        in_specs=[pl.BlockSpec((rows, tokens), lambda g, i: (g, 0))],
        out_specs=[pl.BlockSpec((heads * HEAD_SIZE, QB), lambda g, i: (g, i)),
                   pl.BlockSpec((1, 1, 1, heads * QB), lambda g, i: (g, i, 0, 0))],
        out_shape=[jax.ShapeDtypeStruct((groups * heads * HEAD_SIZE, tokens), jnp.bfloat16),
                   jax.ShapeDtypeStruct((groups, blocks, 1, heads * QB), jnp.float32)],
        scratch_shapes=[pltpu.VMEM((tokens, HEAD_SIZE), jnp.bfloat16)],
        cost_estimate=pl.CostEstimate(flops=flops * 4, bytes_accessed=qkv.size * 4, transcendentals=0),
        compiler_params=pltpu.CompilerParams(vmem_limit_bytes=32 << 20),
    )(qkv)

def backward_kernel(heads, qkv_ref, out_ref, total_ref, grad_ref, result_ref, key_ref, value_ref, grad_key_ref, grad_value_ref):
    index = pl.program_id(1)
    first = pl.multiple_of(index * QB, QB)
    key_row = heads * HEAD_SIZE
    value_row = key_row + HEAD_SIZE
    @pl.when(index == 0)
    def _():
        key_ref[...] = rows_of(qkv_ref[key_row:value_row, :])
        value_ref[...] = rows_of(qkv_ref[value_row : value_row + HEAD_SIZE, :])
        grad_key_ref[...] = jnp.zeros_like(grad_key_ref)
        grad_value_ref[...] = jnp.zeros_like(grad_value_ref)
    queries = stack_heads(qkv_ref, 0, first, heads) * jnp.bfloat16(0.125)
    grads = stack_heads(grad_ref, 0, 0, heads)
    outs = stack_heads(out_ref, 0, 0, heads)
    centre = jnp.sum(grads.astype(jnp.float32) * outs.astype(jnp.float32), axis=0, keepdims=True)
    totals = total_ref[0, 0]
    query_rows = rows_of(queries)
    grad_rows = rows_of(grads)

    def step(block, grad_query, masked):
        start = pl.multiple_of(block * KB, KB)
        keys = key_ref[pl.ds(start, KB), :]
        scores = jnp.dot(keys, queries, preferred_element_type=jnp.float32)
        probs = jnp.exp(scores - totals)
        if masked:
            key_at = lax.broadcasted_iota(jnp.int32, (KB, QB), 0)
            query_at = lax.broadcasted_iota(jnp.int32, (KB, QB), 1)
            seen = jnp.concatenate([key_at <= query_at] * heads, axis=1)
            probs = jnp.where(seen, probs, 0.0)
        grad_probs = jnp.dot(value_ref[pl.ds(start, KB), :], grads, preferred_element_type=jnp.float32)
        grad_scores = (probs * (grad_probs - centre)).astype(jnp.bfloat16)
        grad_value_ref[pl.ds(start, KB), :] += jnp.dot(probs.astype(jnp.bfloat16), grad_rows, preferred_element_type=jnp.float32)
        grad_key_ref[pl.ds(start, KB), :] += jnp.dot(grad_scores, query_rows, preferred_element_type=jnp.float32)
        return grad_query + jnp.dot(qkv_ref[key_row:value_row, pl.ds(start, KB)], grad_scores, preferred_element_type=jnp.float32)

    grad_query = lax.fori_loop(0, index, lambda b, c: step(b, c, False), jnp.zeros((HEAD_SIZE, heads * QB), jnp.float32))
    grad_query = (step(index, grad_query, True) * 0.125).astype(jnp.bfloat16)
    for h in range(heads):
        result_ref[h * HEAD_SIZE : (h + 1) * HEAD_SIZE, pl.ds(first, QB)] = grad_query[:, h * QB : (h + 1) * QB]
    @pl.when(index == pl.num_programs(1) - 1)
    def _():
        result_ref[key_row:value_row, :] = grad_key_ref[...].T.astype(jnp.bfloat16)
        result_ref[value_row : value_row + HEAD_SIZE, :] = grad_value_ref[...].T.astype(jnp.bfloat16)

def attend_backward(qkv, out, totals, grad, groups, heads):
    tokens = qkv.shape[1]
    blocks = tokens // QB
    rows = (heads + 2) * HEAD_SIZE
    flops = groups * heads * tokens * tokens * HEAD_SIZE * 5
    return pl.pallas_call(
        functools.partial(backward_kernel, heads),
        grid=(groups, blocks),
        in_specs=[pl.BlockSpec((rows, tokens), lambda g, i: (g, 0)),
                  pl.BlockSpec((heads * HEAD_SIZE, QB), lambda g, i: (g, i)),
                  pl.BlockSpec((1, 1, 1, heads * QB), lambda g, i: (g, i, 0, 0)),
                  pl.BlockSpec((heads * HEAD_SIZE, QB), lambda g, i: (g, i))],
        out_specs=pl.BlockSpec((rows, tokens), lambda g, i: (g, 0)),
        out_shape=jax.ShapeDtypeStruct((groups * rows, tokens), jnp.bfloat16),
        scratch_shapes=[pltpu.VMEM((tokens, HEAD_SIZE), jnp.bfloat16), pltpu.VMEM((tokens, HEAD_SIZE), jnp.bfloat16),
                        pltpu.VMEM((tokens, HEAD_SIZE), jnp.float32), pltpu.VMEM((tokens, HEAD_SIZE), jnp.float32)],
        cost_estimate=pl.CostEstimate(flops=flops * 4, bytes_accessed=qkv.size * 8, transcendentals=0),
        compiler_params=pltpu.CompilerParams(vmem_limit_bytes=40 << 20),
    )(qkv, out, totals, grad)


def arrange(experts_of):
    tokens = experts_of.shape[0]
    assigned = tokens * TOPK
    flat_ids = experts_of.reshape(assigned)
    one_hot = (flat_ids[:, None] == jnp.arange(E, dtype=jnp.int32)[None, :]).astype(jnp.int32)
    counts = jnp.sum(one_hot, axis=0, dtype=jnp.int32)
    blocks = jnp.maximum((counts + BLOCK - 1) // BLOCK, 1)
    block_ends = jnp.cumsum(blocks, dtype=jnp.int32)
    starts = (block_ends - blocks) * BLOCK
    before = jnp.cumsum(one_hot, axis=0, dtype=jnp.int32) - one_hot
    slot_of = jnp.sum((before + starts[None, :]) * one_hot, axis=1, dtype=jnp.int32)
    slots = assigned + E * BLOCK
    slot_token = (
        jnp.full((slots,), tokens, jnp.int32)
        .at[slot_of]
        .set(jnp.arange(assigned, dtype=jnp.int32) // TOPK)
    )
    firsts = jnp.arange(slots // BLOCK, dtype=jnp.int32)
    later = (firsts[:, None] >= block_ends[None, :]).astype(jnp.int32)
    block_expert = jnp.minimum(jnp.sum(later, axis=1, dtype=jnp.int32), E - 1)
    return slot_token, block_expert, block_ends


def row_at(index):
    return pl.ds(pl.multiple_of(index * PITCH, PITCH), PITCH)


def dispatch_kernel(gated, token_ref, expert_ref, live_ref, source_ref, *refs):
    if gated:
        weight_ref, out_ref, gate_ref, held, moved = refs
    else:
        out_ref, held, moved = refs
    step = pl.program_id(0)
    tokens, width = source_ref.shape
    parts = width // LANES

    @pl.when(step == 0)
    def _():
        held[tokens * PITCH : (tokens + 1) * PITCH, :] = jnp.zeros((PITCH, LANES), F32)
        for first in range(0, tokens, BLOCK):
            for part in range(parts):
                held[pl.ds(first * PITCH + part, BLOCK, stride=PITCH), :] = source_ref[
                    first : first + BLOCK, part * LANES : (part + 1) * LANES
                ].astype(F32)
            if gated:
                held[pl.ds(first * PITCH + parts, BLOCK, stride=PITCH), :] = weight_ref[
                    first : first + BLOCK, :
                ]

    @pl.when(step < live_ref[0])
    def _():
        def move(group, carry):
            base = group * UNROLL
            for j in range(UNROLL):
                moved[row_at(base + j), :] = held[row_at(token_ref[step * BLOCK + base + j]), :]
            return carry

        lax.fori_loop(0, BLOCK // UNROLL, move, 0)
        for part in range(parts):
            out_ref[:, part * LANES : (part + 1) * LANES] = moved[
                pl.ds(part, BLOCK, stride=PITCH), :
            ].astype(BF16)
        if gated:
            lanes = lax.broadcasted_iota(jnp.int32, (BLOCK, LANES), 1)
            spare = moved[pl.ds(parts, BLOCK, stride=PITCH), :]
            own = jnp.where(lanes == expert_ref[step], spare, 0.0)
            gate_ref[...] = jnp.sum(own, axis=1, keepdims=True)


def dispatch(source, weights, slot_token, block_expert, live):
    tokens, width = source.shape
    slots = slot_token.shape[0]
    gated = weights is not None
    at = lambda i, t, e, n: (jnp.minimum(i, n[0] - 1), 0)
    rows = pl.BlockSpec((BLOCK, width), at)
    column = pl.BlockSpec((BLOCK, 1), at)

    def whole(columns):
        return pl.BlockSpec((tokens, columns), lambda i, t, e, n: (0, 0), pipeline_mode=pl.Buffered(1))

    out = jax.ShapeDtypeStruct((slots, width), BF16)
    gate = jax.ShapeDtypeStruct((slots, 1), F32)
    return pl.pallas_call(
        functools.partial(dispatch_kernel, gated),
        grid_spec=pltpu.PrefetchScalarGridSpec(
            num_scalar_prefetch=3,
            grid=(slots // BLOCK,),
            in_specs=[whole(width), whole(LANES)] if gated else [whole(width)],
            out_specs=[rows, column] if gated else rows,
            scratch_shapes=[
                pltpu.VMEM(((tokens + 1) * PITCH, LANES), F32),
                pltpu.VMEM((BLOCK * PITCH, LANES), F32),
            ],
        ),
        out_shape=[out, gate] if gated else out,
        cost_estimate=pl.CostEstimate(
            flops=20 * 10**9, bytes_accessed=24 * BLOCK * width * 2, transcendentals=0
        ),
        compiler_params=pltpu.CompilerParams(vmem_limit_bytes=48 << 20),
    )(*((slot_token, block_expert, live, source) + ((weights,) if gated else ())))


def expert_kernel(
    span_ref,
    expert_ref,
    token_ref,
    row_ref,
    cot_ref,
    gate_ref,
    weight_ref,
    out_ref,
    back_ref,
    score_ref,
    grad_ref,
    gate_sum,
    up_sum,
    down_sum,
    out_sum,
    back_sum,
    moved,
    staging,
    sems,
):
    step = pl.program_id(0)
    total = span_ref[1]
    block = span_ref[0] + jnp.minimum(step, total - 1)
    expert = expert_ref[block]
    width = row_ref.shape[1]
    parts = width // LANES
    tokens = out_sum.shape[0] // PITCH - 1
    following = expert_ref[jnp.minimum(block + 1, expert_ref.shape[0] - 1)]
    closing = jnp.logical_or(step == total - 1, following != expert)

    @pl.when(step == 0)
    def _():
        for ref in (out_sum, back_sum, moved, gate_sum, up_sum, down_sum):
            ref[...] = jnp.zeros_like(ref)

    @pl.when(step < total)
    def _():
        rows = row_ref[...]
        cots = cot_ref[...]
        gates = gate_ref[...]
        gate_weight = weight_ref[0, 0]
        up_weight = weight_ref[1, 0]
        down_weight = weight_ref[2, 0]
        gate_val = jnp.dot(rows, gate_weight, preferred_element_type=F32)
        up_val = jnp.dot(rows, up_weight, preferred_element_type=F32)
        raw_grad = jnp.dot(cots, down_weight, preferred_element_type=F32)
        sigma = jax.nn.sigmoid(gate_val)
        silu_val = gate_val * sigma
        active = (silu_val * up_val).astype(BF16).astype(F32)
        scores = jnp.sum(active * raw_grad, axis=1, keepdims=True)
        act_grad = raw_grad * gates
        gate_d = (act_grad * up_val * sigma * (1.0 + gate_val * (1.0 - sigma))).astype(BF16)
        up_d = (act_grad * silu_val).astype(BF16)
        weighted = (active * gates).astype(BF16)
        over_rows = (((0,), (0,)), ((), ()))
        over_hidden = (((1,), (1,)), ((), ()))
        gate_sum[...] += lax.dot_general(gate_d, rows, over_rows, preferred_element_type=F32)
        up_sum[...] += lax.dot_general(up_d, rows, over_rows, preferred_element_type=F32)
        down_sum[...] += lax.dot_general(weighted, cots, over_rows, preferred_element_type=F32)

        def spread(value):
            for part in range(parts):
                moved[pl.ds(part, BLOCK, stride=PITCH), :] = value[:, part * LANES : (part + 1) * LANES]

        def combine(sum_ref):
            def add(group, carry):
                base = group * UNROLL
                at = [row_at(token_ref[block * BLOCK + base + j]) for j in range(UNROLL)]
                new = [sum_ref[at[j], :] + moved[row_at(base + j), :] for j in range(UNROLL)]
                for j in range(UNROLL):
                    sum_ref[at[j], :] = new[j]
                return carry

            lax.fori_loop(0, BLOCK // UNROLL, add, 0)

        spread(lax.dot_general(weighted, down_weight, over_hidden, preferred_element_type=F32))
        combine(out_sum)
        spread(
            lax.dot_general(gate_d, gate_weight, over_hidden, preferred_element_type=F32)
            + lax.dot_general(up_d, up_weight, over_hidden, preferred_element_type=F32)
        )
        lanes = lax.broadcasted_iota(jnp.int32, (BLOCK, LANES), 1)
        moved[pl.ds(parts, BLOCK, stride=PITCH), :] = jnp.where(lanes == expert, scores, 0.0)
        combine(back_sum)

        @pl.when(closing)
        def _():
            for index, ref in enumerate((gate_sum, up_sum, down_sum)):
                grad_ref[index, 0] = ref[...].T.astype(BF16)
                ref[...] = jnp.zeros_like(ref)

    @pl.when(step == total - 1)
    def _():
        for first in range(0, tokens, BLOCK):
            score_ref[first : first + BLOCK, :] = back_sum[
                pl.ds(first * PITCH + parts, BLOCK, stride=PITCH), :
            ]

        jobs = [
            (first, source, target)
            for first in range(0, tokens, BLOCK)
            for source, target in ((out_sum, out_ref), (back_sum, back_ref))
        ]

        def copy(number):
            first, _, target = jobs[number]
            slot = number % 2
            return pltpu.make_async_copy(
                staging.at[slot], target.at[pl.ds(first, BLOCK), :], sems.at[slot]
            )

        for number, (first, source, _) in enumerate(jobs):
            if number >= 2:
                copy(number - 2).wait()
            for part in range(parts):
                staging[number % 2, :, part * LANES : (part + 1) * LANES] = source[
                    pl.ds(first * PITCH + part, BLOCK, stride=PITCH), :
                ].astype(BF16)
            copy(number).start()
        copy(len(jobs) - 2).wait()
        copy(len(jobs) - 1).wait()


def run_experts(span, slot_token, block_expert, rows, cots, gates, weights, low, tokens):
    width = rows.shape[1]
    experts, hidden = weights.shape[1], weights.shape[3]
    index = lambda i, s: s[0] + jnp.minimum(i, s[1] - 1)
    at = lambda i, s, e, t: (index(i, s), 0)
    pick = pl.BlockSpec(
        (3, 1, width, hidden), lambda i, s, e, t: (0, e[index(i, s)] - low, 0, 0)
    )
    anywhere = pl.BlockSpec(memory_space=pl.ANY)
    block_count = experts * 3 // 2
    return pl.pallas_call(
        expert_kernel,
        grid_spec=pltpu.PrefetchScalarGridSpec(
            num_scalar_prefetch=3,
            grid=(tokens * TOPK // BLOCK + experts,),
            in_specs=[
                pl.BlockSpec((BLOCK, width), at),
                pl.BlockSpec((BLOCK, width), at),
                pl.BlockSpec((BLOCK, 1), at),
                pick,
            ],
            out_specs=[
                anywhere,
                anywhere,
                pl.BlockSpec((tokens, LANES), lambda i, s, e, t: (0, 0)),
                pick,
            ],
            scratch_shapes=[pltpu.VMEM((hidden, width), F32)] * 3
            + [pltpu.VMEM(((tokens + 1) * PITCH, LANES), F32)] * 2
            + [
                pltpu.VMEM((BLOCK * PITCH, LANES), F32),
                pltpu.VMEM((2, BLOCK, width), BF16),
                pltpu.SemaphoreType.DMA((2,)),
            ],
        ),
        out_shape=[
            jax.ShapeDtypeStruct((tokens, width), BF16),
            jax.ShapeDtypeStruct((tokens, width), BF16),
            jax.ShapeDtypeStruct((tokens, LANES), F32),
            jax.ShapeDtypeStruct(weights.shape, BF16),
        ],
        cost_estimate=pl.CostEstimate(
            flops=block_count * 2 * BLOCK * width * hidden * 9 * 3,
            bytes_accessed=weights.size * 4 + block_count * BLOCK * width * 4,
            transcendentals=0,
        ),
        compiler_params=pltpu.CompilerParams(vmem_limit_bytes=62 << 20),
    )(span, block_expert, slot_token, rows, cots, gates, weights)


def swap(value, bit):
    count = lax.axis_size("narrow")
    return lax.ppermute(value, "narrow", [(index, index ^ bit) for index in range(count)])


def gather_rows(value):
    count = lax.axis_size("narrow")
    if count != 4:
        return lax.all_gather(value, "narrow", axis=0, tiled=True)
    me = lax.axis_index("narrow")
    rows = value.shape[0]
    half = rows // 2
    one = swap(value, 1)
    two = swap(value, 2)
    far_low = swap(two[:half], 1)
    far_high = swap(one[half:], 2)
    full = jnp.zeros((count * rows,) + value.shape[1:], value.dtype)
    for piece, other, offset in (
        (value, 0, 0),
        (one, 1, 0),
        (two, 2, 0),
        (far_low, 3, 0),
        (far_high, 3, half),
    ):
        full = lax.dynamic_update_slice_in_dim(full, piece, (me ^ other) * rows + offset, 0)
    return full


def sum_rows(part):
    count = lax.axis_size("narrow")
    if count != 4:
        low = part.astype(BF16)
        return lax.psum_scatter(low, "narrow", scatter_dimension=0, tiled=True).astype(F32)
    me = lax.axis_index("narrow")
    rows = part.shape[0] // count
    half = rows // 2

    def block(other, offset):
        return lax.dynamic_slice_in_dim(part, (me ^ other) * rows + offset, half, 0)

    def send(pieces, bit):
        return swap(jnp.concatenate([piece.astype(BF16) for piece in pieces], axis=0), bit)

    low = send([block(1, 0), block(3, 0)], 1).astype(F32)
    high = send([block(2, half), block(3, half)], 2).astype(F32)
    low_far = send([block(2, 0).astype(F32) + low[half:]], 2).astype(F32)
    high_far = send([block(1, half).astype(F32) + high[half:]], 1).astype(F32)
    return jnp.concatenate(
        [
            block(0, 0).astype(F32) + low[:half] + low_far,
            block(0, half).astype(F32) + high[:half] + high_far,
        ],
        axis=0,
    )


def local(
    block_input,
    routes,
    first_gain,
    query_key_value_weight,
    output_weight,
    second_gain,
    router_weight,
    gate_weight,
    up_weight,
    down_weight,
    cotangent,
):
    row_part, width = block_input.shape
    me = lax.axis_index("narrow")
    row_offset = me * row_part
    gain_part = first_gain.shape[0]
    tokens = routes.shape[0]
    heads = QUERY_HEADS // KEY_VALUE_HEADS
    head_columns = query_key_value_weight.shape[1]
    groups = head_columns // ((heads + 2) * HEAD_SIZE)

    def own_rows(value):
        return lax.dynamic_slice_in_dim(value, row_offset, row_part, 0)

    inputs = gather_rows(block_input)
    gains = lax.all_gather(
        jnp.stack([first_gain, second_gain]), "narrow", axis=1, tiled=True
    ).astype(F32)
    gain_one, gain_two = gains[0], gains[1]
    router_padded = jnp.pad(router_weight, ((0, 0), (0, LANES - E)))
    input_router = lax.all_gather(
        jnp.concatenate([query_key_value_weight, router_padded], axis=1), "wide", axis=0, tiled=True
    )
    input_full = input_router[:, :head_columns]
    router_full = input_router[:, head_columns : head_columns + E]
    output_full = lax.all_gather(output_weight, "wide", axis=1, tiled=True)
    lows = [sum(CHUNKS[:index]) for index in range(len(CHUNKS))]
    chunk_weights = []
    for low, size in zip(lows, CHUNKS):
        packed = jnp.stack([w[low : low + size] for w in (gate_weight, up_weight, down_weight)])
        chunk_weights.append(lax.all_gather(packed, "wide", axis=2, tiled=True))
    slot_token, block_expert, block_ends = arrange(routes)

    x_full = inputs.astype(F32)
    scale_one = lax.rsqrt(jnp.mean(x_full * x_full, axis=1, keepdims=True) + EPSILON)
    normed_one = x_full * scale_one
    attn_in = (normed_one * gain_one).astype(BF16)
    late_cotangent, _ = lax.optimization_barrier((cotangent, inputs))
    cot_full = gather_rows(late_cotangent)
    projected = jnp.einsum(
        "td,dc->ct", attn_in, input_full, preferred_element_type=F32
    ).astype(BF16)
    mixed, log_totals = attend_forward(projected, groups, heads)
    branch_part = jnp.einsum("ct,cd->td", mixed, output_full, preferred_element_type=F32)
    middle_own = block_input.astype(F32) + sum_rows(branch_part)
    middle = gather_rows(middle_own.astype(BF16)).astype(F32)
    scale_two = lax.rsqrt(jnp.mean(middle * middle, axis=1, keepdims=True) + EPSILON)
    normed_two = middle * scale_two
    expert_in = (normed_two * gain_two).astype(BF16)
    logits = jnp.dot(expert_in, router_full, preferred_element_type=F32)
    picked = (routes[:, :, None] == jnp.arange(E, dtype=jnp.int32)[None, None, :]).astype(F32)
    chosen = jnp.sum(picked * logits[:, None, :], axis=2)
    gates = jax.nn.softmax(chosen, axis=1)
    gate_lanes = jnp.pad(jnp.sum(picked * gates[:, :, None], axis=1), ((0, 0), (0, LANES - E)))
    live = block_ends[E - 1 :]
    cot_rows = dispatch(cot_full, None, slot_token, block_expert, live)
    rows, slot_gates = dispatch(expert_in, gate_lanes, slot_token, block_expert, live)

    outs, backs, scores, grads = [], [], [], []
    for low, size, weights in zip(lows, CHUNKS, chunk_weights):
        first = block_ends[low - 1 : low] if low else jnp.zeros((1,), jnp.int32)
        count = block_ends[low + size - 1 : low + size] - first
        out, back, score, grad = run_experts(
            jnp.concatenate([first, count]), slot_token, block_expert, rows, cot_rows, slot_gates, weights, low, tokens
        )
        outs.append(out)
        backs.append(back)
        scores.append(score)
        grads.append(lax.psum_scatter(grad, "wide", scatter_dimension=2, tiled=True))

    def total(values):
        return sum(value.astype(F32) for value in values)

    expert_sum = sum_rows(total(backs))
    score_part = jnp.sum(picked * total(scores)[:, None, :E], axis=2)
    score_sum = lax.psum_scatter(score_part, "narrow", scatter_dimension=0, tiled=True)
    block_output = (middle_own + sum_rows(total(outs))).astype(BF16)

    gates_own = own_rows(gates)
    centre = jnp.sum(gates_own * score_sum, axis=1, keepdims=True)
    logit_part = gates_own * (score_sum - centre)
    logit_grad = jnp.sum(own_rows(picked) * logit_part[:, :, None], axis=1).astype(BF16)
    norm_grad = expert_sum + jnp.einsum(
        "te,de->td", logit_grad, router_full, preferred_element_type=F32
    )
    normed_two_own = own_rows(normed_two)
    row_dot = jnp.sum(norm_grad * normed_two_own * gain_two, axis=1, keepdims=True)
    gain_two_part = jnp.sum(norm_grad * normed_two_own, axis=0)
    mid_grad = cotangent.astype(F32) + own_rows(scale_two) * (
        gain_two * norm_grad - normed_two_own * row_dot / width
    )
    branch_grad = gather_rows(mid_grad.astype(BF16))
    logit_full = lax.all_gather(logit_grad, "narrow", axis=0, tiled=True)
    mixed_grad = jnp.einsum(
        "td,cd->ct", branch_grad, output_full, preferred_element_type=F32
    ).astype(BF16)
    projected_grad = attend_backward(projected, mixed, log_totals, mixed_grad, groups, heads)
    input_part = jnp.einsum("ct,dc->td", projected_grad, input_full, preferred_element_type=F32)
    grad_input_w = jnp.einsum(
        "td,ct->dc", attn_in, projected_grad, preferred_element_type=F32
    ).astype(BF16)
    grad_output_w = jnp.einsum(
        "ct,td->cd", mixed, branch_grad, preferred_element_type=F32
    ).astype(BF16)
    grad_router = jnp.einsum("td,te->de", expert_in, logit_full, preferred_element_type=F32)
    router_grad = lax.psum_scatter(grad_router, "wide", scatter_dimension=0, tiled=True)
    output_w_grad = lax.psum_scatter(grad_output_w, "wide", scatter_dimension=1, tiled=True)
    input_w_grad = lax.psum_scatter(grad_input_w, "wide", scatter_dimension=0, tiled=True)
    gain_one_part = jnp.sum(input_part * normed_one, axis=0)
    gain_pair = lax.psum(jnp.stack([gain_one_part, gain_two_part]), ("wide", "narrow"))
    gain_own = lax.dynamic_slice_in_dim(gain_pair, me * gain_part, gain_part, 1)
    input_sum = sum_rows(input_part)
    normed_one_own = own_rows(normed_one)
    input_dot = jnp.sum(input_sum * normed_one_own * gain_one, axis=1, keepdims=True)
    input_grad = mid_grad + own_rows(scale_one) * (
        gain_one * input_sum - normed_one_own * input_dot / width
    )
    gate_grad, up_grad, down_grad = (
        jnp.concatenate([grad[index] for grad in grads], axis=0).astype(F32) for index in range(3)
    )
    return (
        block_output,
        input_grad,
        gain_own[0],
        input_w_grad.astype(F32),
        output_w_grad.astype(F32),
        gain_own[1],
        router_grad,
        gate_grad,
        up_grad,
        down_grad,
    )


def solution(mesh):
    placed = (
        P(("wide", "narrow"), None),
        P("wide", None),
        P("narrow"),
        P("wide", "narrow"),
        P("narrow", "wide"),
        P("narrow"),
        P("wide", None),
        P(None, "wide", "narrow"),
        P(None, "wide", "narrow"),
        P(None, "wide", "narrow"),
        P(("wide", "narrow"), None),
    )
    return jax.shard_map(
        local,
        mesh=mesh,
        in_specs=placed,
        out_specs=(
            P(("wide", "narrow"), None),
            P(("wide", "narrow"), None),
            P("narrow"),
            P("wide", "narrow"),
            P("narrow", "wide"),
            P("narrow"),
            P("wide", None),
            P(None, "wide", "narrow"),
            P(None, "wide", "narrow"),
            P(None, "wide", "narrow"),
        ),
        check_vma=False,
    )
```

```python
import functools

import jax
import jax.numpy as jnp
from jax import lax
from jax.experimental import pallas as pl
from jax.experimental.pallas import tpu as pltpu
from jax.sharding import PartitionSpec as P

QUERY_HEADS = 24
KEY_VALUE_HEADS = 8
HEAD_SIZE = 64
E = 16
TOPK = 2
SEQUENCE_LENGTH = 2048
BLOCK = 256
QB = 256
KB = 256
LANES = 128
PITCH = 16
UNROLL = 8
CHUNKS = (4, 4, 4, 4)
EPSILON = 1e-05
F32 = jnp.float32
BF16 = jnp.bfloat16

def stack_heads(ref, row, first, heads):
    return jnp.concatenate(
        [ref[row + h * HEAD_SIZE : row + (h + 1) * HEAD_SIZE, pl.ds(first, QB)] for h in range(heads)], axis=1
    )

def rows_of(block):
    return block.astype(jnp.float32).T.astype(jnp.bfloat16)

def forward_kernel(heads, qkv_ref, out_ref, total_ref, key_ref):
    index = pl.program_id(1)
    first = pl.multiple_of(index * QB, QB)
    key_row = heads * HEAD_SIZE
    value_row = key_row + HEAD_SIZE
    @pl.when(index == 0)
    def _():
        key_ref[...] = rows_of(qkv_ref[key_row:value_row, :])
    queries = stack_heads(qkv_ref, 0, first, heads) * jnp.bfloat16(0.125)
    lanes = heads * QB

    def step(block, carry, masked):
        highest, denominator, mixed = carry
        start = pl.multiple_of(block * KB, KB)
        scores = jnp.dot(key_ref[pl.ds(start, KB), :], queries, preferred_element_type=jnp.float32)
        if masked:
            key_at = lax.broadcasted_iota(jnp.int32, (KB, QB), 0)
            query_at = lax.broadcasted_iota(jnp.int32, (KB, QB), 1)
            seen = jnp.concatenate([key_at <= query_at] * heads, axis=1)
            scores = jnp.where(seen, scores, -1e30)
        raised_to = jnp.maximum(highest, jnp.max(scores, axis=0, keepdims=True))
        shrink = jnp.exp(highest - raised_to)
        raised = jnp.exp(scores - raised_to)
        denominator = denominator * shrink + jnp.sum(raised, axis=0, keepdims=True)
        mixed = mixed * shrink + jnp.dot(
            qkv_ref[value_row : value_row + HEAD_SIZE, pl.ds(start, KB)], raised.astype(jnp.bfloat16),
            preferred_element_type=jnp.float32)
        return raised_to, denominator, mixed

    carry = (jnp.full((1, lanes), -1e30, jnp.float32), jnp.zeros((1, lanes), jnp.float32), jnp.zeros((HEAD_SIZE, lanes), jnp.float32))
    carry = lax.fori_loop(0, index, lambda b, c: step(b, c, False), carry)
    highest, denominator, mixed = step(index, carry, True)
    mixed = (mixed / denominator).astype(jnp.bfloat16)
    for h in range(heads):
        out_ref[h * HEAD_SIZE : (h + 1) * HEAD_SIZE, :] = mixed[:, h * QB : (h + 1) * QB]
    total_ref[0, 0] = highest + jnp.log(denominator)

def attend_forward(qkv, groups, heads):
    tokens = qkv.shape[1]
    blocks = tokens // QB
    rows = (heads + 2) * HEAD_SIZE
    flops = groups * heads * tokens * tokens * HEAD_SIZE * 2
    return pl.pallas_call(
        functools.partial(forward_kernel, heads),
        grid=(groups, blocks),
        in_specs=[pl.BlockSpec((rows, tokens), lambda g, i: (g, 0))],
        out_specs=[pl.BlockSpec((heads * HEAD_SIZE, QB), lambda g, i: (g, i)),
                   pl.BlockSpec((1, 1, 1, heads * QB), lambda g, i: (g, i, 0, 0))],
        out_shape=[jax.ShapeDtypeStruct((groups * heads * HEAD_SIZE, tokens), jnp.bfloat16),
                   jax.ShapeDtypeStruct((groups, blocks, 1, heads * QB), jnp.float32)],
        scratch_shapes=[pltpu.VMEM((tokens, HEAD_SIZE), jnp.bfloat16)],
        cost_estimate=pl.CostEstimate(flops=flops * 4, bytes_accessed=qkv.size * 4, transcendentals=0),
        compiler_params=pltpu.CompilerParams(vmem_limit_bytes=32 << 20),
    )(qkv)

def backward_kernel(heads, qkv_ref, out_ref, total_ref, grad_ref, result_ref, key_ref, value_ref, grad_key_ref, grad_value_ref):
    index = pl.program_id(1)
    first = pl.multiple_of(index * QB, QB)
    key_row = heads * HEAD_SIZE
    value_row = key_row + HEAD_SIZE
    @pl.when(index == 0)
    def _():
        key_ref[...] = rows_of(qkv_ref[key_row:value_row, :])
        value_ref[...] = rows_of(qkv_ref[value_row : value_row + HEAD_SIZE, :])
        grad_key_ref[...] = jnp.zeros_like(grad_key_ref)
        grad_value_ref[...] = jnp.zeros_like(grad_value_ref)
    queries = stack_heads(qkv_ref, 0, first, heads) * jnp.bfloat16(0.125)
    grads = stack_heads(grad_ref, 0, 0, heads)
    outs = stack_heads(out_ref, 0, 0, heads)
    centre = jnp.sum(grads.astype(jnp.float32) * outs.astype(jnp.float32), axis=0, keepdims=True)
    totals = total_ref[0, 0]
    query_rows = rows_of(queries)
    grad_rows = rows_of(grads)

    def step(block, grad_query, masked):
        start = pl.multiple_of(block * KB, KB)
        keys = key_ref[pl.ds(start, KB), :]
        scores = jnp.dot(keys, queries, preferred_element_type=jnp.float32)
        probs = jnp.exp(scores - totals)
        if masked:
            key_at = lax.broadcasted_iota(jnp.int32, (KB, QB), 0)
            query_at = lax.broadcasted_iota(jnp.int32, (KB, QB), 1)
            seen = jnp.concatenate([key_at <= query_at] * heads, axis=1)
            probs = jnp.where(seen, probs, 0.0)
        grad_probs = jnp.dot(value_ref[pl.ds(start, KB), :], grads, preferred_element_type=jnp.float32)
        grad_scores = (probs * (grad_probs - centre)).astype(jnp.bfloat16)
        grad_value_ref[pl.ds(start, KB), :] += jnp.dot(probs.astype(jnp.bfloat16), grad_rows, preferred_element_type=jnp.float32)
        grad_key_ref[pl.ds(start, KB), :] += jnp.dot(grad_scores, query_rows, preferred_element_type=jnp.float32)
        return grad_query + jnp.dot(qkv_ref[key_row:value_row, pl.ds(start, KB)], grad_scores, preferred_element_type=jnp.float32)

    grad_query = lax.fori_loop(0, index, lambda b, c: step(b, c, False), jnp.zeros((HEAD_SIZE, heads * QB), jnp.float32))
    grad_query = (step(index, grad_query, True) * 0.125).astype(jnp.bfloat16)
    for h in range(heads):
        result_ref[h * HEAD_SIZE : (h + 1) * HEAD_SIZE, pl.ds(first, QB)] = grad_query[:, h * QB : (h + 1) * QB]
    @pl.when(index == pl.num_programs(1) - 1)
    def _():
        result_ref[key_row:value_row, :] = grad_key_ref[...].T.astype(jnp.bfloat16)
        result_ref[value_row : value_row + HEAD_SIZE, :] = grad_value_ref[...].T.astype(jnp.bfloat16)

def attend_backward(qkv, out, totals, grad, groups, heads):
    tokens = qkv.shape[1]
    blocks = tokens // QB
    rows = (heads + 2) * HEAD_SIZE
    flops = groups * heads * tokens * tokens * HEAD_SIZE * 5
    return pl.pallas_call(
        functools.partial(backward_kernel, heads),
        grid=(groups, blocks),
        in_specs=[pl.BlockSpec((rows, tokens), lambda g, i: (g, 0)),
                  pl.BlockSpec((heads * HEAD_SIZE, QB), lambda g, i: (g, i)),
                  pl.BlockSpec((1, 1, 1, heads * QB), lambda g, i: (g, i, 0, 0)),
                  pl.BlockSpec((heads * HEAD_SIZE, QB), lambda g, i: (g, i))],
        out_specs=pl.BlockSpec((rows, tokens), lambda g, i: (g, 0)),
        out_shape=jax.ShapeDtypeStruct((groups * rows, tokens), jnp.bfloat16),
        scratch_shapes=[pltpu.VMEM((tokens, HEAD_SIZE), jnp.bfloat16), pltpu.VMEM((tokens, HEAD_SIZE), jnp.bfloat16),
                        pltpu.VMEM((tokens, HEAD_SIZE), jnp.float32), pltpu.VMEM((tokens, HEAD_SIZE), jnp.float32)],
        cost_estimate=pl.CostEstimate(flops=flops * 4, bytes_accessed=qkv.size * 8, transcendentals=0),
        compiler_params=pltpu.CompilerParams(vmem_limit_bytes=40 << 20),
    )(qkv, out, totals, grad)


def arrange(experts_of):
    tokens = experts_of.shape[0]
    assigned = tokens * TOPK
    flat_ids = experts_of.reshape(assigned)
    one_hot = (flat_ids[:, None] == jnp.arange(E, dtype=jnp.int32)[None, :]).astype(jnp.int32)
    counts = jnp.sum(one_hot, axis=0, dtype=jnp.int32)
    blocks = jnp.maximum((counts + BLOCK - 1) // BLOCK, 1)
    block_ends = jnp.cumsum(blocks, dtype=jnp.int32)
    starts = (block_ends - blocks) * BLOCK
    before = jnp.cumsum(one_hot, axis=0, dtype=jnp.int32) - one_hot
    slot_of = jnp.sum((before + starts[None, :]) * one_hot, axis=1, dtype=jnp.int32)
    slots = assigned + E * BLOCK
    slot_token = (
        jnp.full((slots,), tokens, jnp.int32)
        .at[slot_of]
        .set(jnp.arange(assigned, dtype=jnp.int32) // TOPK)
    )
    firsts = jnp.arange(slots // BLOCK, dtype=jnp.int32)
    later = (firsts[:, None] >= block_ends[None, :]).astype(jnp.int32)
    block_expert = jnp.minimum(jnp.sum(later, axis=1, dtype=jnp.int32), E - 1)
    return slot_token, block_expert, block_ends


def row_at(index):
    return pl.ds(pl.multiple_of(index * PITCH, PITCH), PITCH)


def dispatch_kernel(gated, token_ref, expert_ref, live_ref, source_ref, *refs):
    if gated:
        weight_ref, out_ref, gate_ref, held, moved = refs
    else:
        out_ref, held, moved = refs
    step = pl.program_id(0)
    tokens, width = source_ref.shape
    parts = width // LANES

    @pl.when(step == 0)
    def _():
        held[tokens * PITCH : (tokens + 1) * PITCH, :] = jnp.zeros((PITCH, LANES), F32)
        for first in range(0, tokens, BLOCK):
            for part in range(parts):
                held[pl.ds(first * PITCH + part, BLOCK, stride=PITCH), :] = source_ref[
                    first : first + BLOCK, part * LANES : (part + 1) * LANES
                ].astype(F32)
            if gated:
                held[pl.ds(first * PITCH + parts, BLOCK, stride=PITCH), :] = weight_ref[
                    first : first + BLOCK, :
                ]

    @pl.when(step < live_ref[0])
    def _():
        def move(group, carry):
            base = group * UNROLL
            for j in range(UNROLL):
                moved[row_at(base + j), :] = held[row_at(token_ref[step * BLOCK + base + j]), :]
            return carry

        lax.fori_loop(0, BLOCK // UNROLL, move, 0)
        for part in range(parts):
            out_ref[:, part * LANES : (part + 1) * LANES] = moved[
                pl.ds(part, BLOCK, stride=PITCH), :
            ].astype(BF16)
        if gated:
            lanes = lax.broadcasted_iota(jnp.int32, (BLOCK, LANES), 1)
            spare = moved[pl.ds(parts, BLOCK, stride=PITCH), :]
            own = jnp.where(lanes == expert_ref[step], spare, 0.0)
            gate_ref[...] = jnp.sum(own, axis=1, keepdims=True)


def dispatch(source, weights, slot_token, block_expert, live):
    tokens, width = source.shape
    slots = slot_token.shape[0]
    gated = weights is not None
    at = lambda i, t, e, n: (jnp.minimum(i, n[0] - 1), 0)
    rows = pl.BlockSpec((BLOCK, width), at)
    column = pl.BlockSpec((BLOCK, 1), at)

    def whole(columns):
        return pl.BlockSpec((tokens, columns), lambda i, t, e, n: (0, 0), pipeline_mode=pl.Buffered(1))

    out = jax.ShapeDtypeStruct((slots, width), BF16)
    gate = jax.ShapeDtypeStruct((slots, 1), F32)
    return pl.pallas_call(
        functools.partial(dispatch_kernel, gated),
        grid_spec=pltpu.PrefetchScalarGridSpec(
            num_scalar_prefetch=3,
            grid=(slots // BLOCK,),
            in_specs=[whole(width), whole(LANES)] if gated else [whole(width)],
            out_specs=[rows, column] if gated else rows,
            scratch_shapes=[
                pltpu.VMEM(((tokens + 1) * PITCH, LANES), F32),
                pltpu.VMEM((BLOCK * PITCH, LANES), F32),
            ],
        ),
        out_shape=[out, gate] if gated else out,
        cost_estimate=pl.CostEstimate(
            flops=20 * 10**9, bytes_accessed=24 * BLOCK * width * 2, transcendentals=0
        ),
        compiler_params=pltpu.CompilerParams(vmem_limit_bytes=48 << 20),
    )(*((slot_token, block_expert, live, source) + ((weights,) if gated else ())))


def expert_kernel(
    span_ref,
    expert_ref,
    token_ref,
    row_ref,
    cot_ref,
    gate_ref,
    weight_ref,
    out_ref,
    back_ref,
    score_ref,
    grad_ref,
    gate_sum,
    up_sum,
    down_sum,
    out_sum,
    back_sum,
    moved,
    staging,
    sems,
):
    step = pl.program_id(0)
    total = span_ref[1]
    block = span_ref[0] + jnp.minimum(step, total - 1)
    expert = expert_ref[block]
    width = row_ref.shape[1]
    parts = width // LANES
    tokens = out_sum.shape[0] // PITCH - 1
    following = expert_ref[jnp.minimum(block + 1, expert_ref.shape[0] - 1)]
    closing = jnp.logical_or(step == total - 1, following != expert)

    @pl.when(step == 0)
    def _():
        for ref in (out_sum, back_sum, moved, gate_sum, up_sum, down_sum):
            ref[...] = jnp.zeros_like(ref)

    @pl.when(step < total)
    def _():
        rows = row_ref[...]
        cots = cot_ref[...]
        gates = gate_ref[...]
        gate_weight = weight_ref[0, 0]
        up_weight = weight_ref[1, 0]
        down_weight = weight_ref[2, 0]
        gate_val = jnp.dot(rows, gate_weight, preferred_element_type=F32)
        up_val = jnp.dot(rows, up_weight, preferred_element_type=F32)
        raw_grad = jnp.dot(cots, down_weight, preferred_element_type=F32)
        sigma = jax.nn.sigmoid(gate_val)
        silu_val = gate_val * sigma
        active = (silu_val * up_val).astype(BF16).astype(F32)
        scores = jnp.sum(active * raw_grad, axis=1, keepdims=True)
        act_grad = raw_grad * gates
        gate_d = (act_grad * up_val * sigma * (1.0 + gate_val * (1.0 - sigma))).astype(BF16)
        up_d = (act_grad * silu_val).astype(BF16)
        weighted = (active * gates).astype(BF16)
        over_rows = (((0,), (0,)), ((), ()))
        over_hidden = (((1,), (1,)), ((), ()))
        gate_sum[...] += lax.dot_general(gate_d, rows, over_rows, preferred_element_type=F32)
        up_sum[...] += lax.dot_general(up_d, rows, over_rows, preferred_element_type=F32)
        down_sum[...] += lax.dot_general(weighted, cots, over_rows, preferred_element_type=F32)

        def spread(value):
            for part in range(parts):
                moved[pl.ds(part, BLOCK, stride=PITCH), :] = value[:, part * LANES : (part + 1) * LANES]

        def combine(sum_ref):
            def add(group, carry):
                base = group * UNROLL
                at = [row_at(token_ref[block * BLOCK + base + j]) for j in range(UNROLL)]
                new = [sum_ref[at[j], :] + moved[row_at(base + j), :] for j in range(UNROLL)]
                for j in range(UNROLL):
                    sum_ref[at[j], :] = new[j]
                return carry

            lax.fori_loop(0, BLOCK // UNROLL, add, 0)

        spread(lax.dot_general(weighted, down_weight, over_hidden, preferred_element_type=F32))
        combine(out_sum)
        spread(
            lax.dot_general(gate_d, gate_weight, over_hidden, preferred_element_type=F32)
            + lax.dot_general(up_d, up_weight, over_hidden, preferred_element_type=F32)
        )
        lanes = lax.broadcasted_iota(jnp.int32, (BLOCK, LANES), 1)
        moved[pl.ds(parts, BLOCK, stride=PITCH), :] = jnp.where(lanes == expert, scores, 0.0)
        combine(back_sum)

        @pl.when(closing)
        def _():
            for index, ref in enumerate((gate_sum, up_sum, down_sum)):
                grad_ref[index, 0] = ref[...].T.astype(BF16)
                ref[...] = jnp.zeros_like(ref)

    @pl.when(step == total - 1)
    def _():
        for first in range(0, tokens, BLOCK):
            score_ref[first : first + BLOCK, :] = back_sum[
                pl.ds(first * PITCH + parts, BLOCK, stride=PITCH), :
            ]

        jobs = [
            (first, source, target)
            for first in range(0, tokens, BLOCK)
            for source, target in ((out_sum, out_ref), (back_sum, back_ref))
        ]

        def copy(number):
            first, _, target = jobs[number]
            slot = number % 2
            return pltpu.make_async_copy(
                staging.at[slot], target.at[pl.ds(first, BLOCK), :], sems.at[slot]
            )

        for number, (first, source, _) in enumerate(jobs):
            if number >= 2:
                copy(number - 2).wait()
            for part in range(parts):
                staging[number % 2, :, part * LANES : (part + 1) * LANES] = source[
                    pl.ds(first * PITCH + part, BLOCK, stride=PITCH), :
                ].astype(BF16)
            copy(number).start()
        copy(len(jobs) - 2).wait()
        copy(len(jobs) - 1).wait()


def run_experts(span, slot_token, block_expert, rows, cots, gates, weights, tokens):
    width = rows.shape[1]
    experts, hidden = weights.shape[1], weights.shape[3]
    index = lambda i, s: s[0] + jnp.minimum(i, s[1] - 1)
    at = lambda i, s, e, t: (index(i, s), 0)
    pick = pl.BlockSpec(
        (3, 1, width, hidden), lambda i, s, e, t: (0, e[index(i, s)] - s[2], 0, 0)
    )
    anywhere = pl.BlockSpec(memory_space=pl.ANY)
    block_count = experts * 3 // 2
    return pl.pallas_call(
        expert_kernel,
        grid_spec=pltpu.PrefetchScalarGridSpec(
            num_scalar_prefetch=3,
            grid=(tokens * TOPK // BLOCK + experts,),
            in_specs=[
                pl.BlockSpec((BLOCK, width), at),
                pl.BlockSpec((BLOCK, width), at),
                pl.BlockSpec((BLOCK, 1), at),
                pick,
            ],
            out_specs=[
                anywhere,
                anywhere,
                pl.BlockSpec((tokens, LANES), lambda i, s, e, t: (0, 0)),
                pick,
            ],
            scratch_shapes=[pltpu.VMEM((hidden, width), F32)] * 3
            + [pltpu.VMEM(((tokens + 1) * PITCH, LANES), F32)] * 2
            + [
                pltpu.VMEM((BLOCK * PITCH, LANES), F32),
                pltpu.VMEM((2, BLOCK, width), BF16),
                pltpu.SemaphoreType.DMA((2,)),
            ],
        ),
        out_shape=[
            jax.ShapeDtypeStruct((tokens, width), BF16),
            jax.ShapeDtypeStruct((tokens, width), BF16),
            jax.ShapeDtypeStruct((tokens, LANES), F32),
            jax.ShapeDtypeStruct(weights.shape, BF16),
        ],
        cost_estimate=pl.CostEstimate(
            flops=block_count * 2 * BLOCK * width * hidden * 9 * 3,
            bytes_accessed=weights.size * 4 + block_count * BLOCK * width * 4,
            transcendentals=0,
        ),
        compiler_params=pltpu.CompilerParams(vmem_limit_bytes=62 << 20),
    )(span, block_expert, slot_token, rows, cots, gates, weights)


def swap(value, bit):
    count = lax.axis_size("narrow")
    return lax.ppermute(value, "narrow", [(index, index ^ bit) for index in range(count)])


def gather_rows(value):
    count = lax.axis_size("narrow")
    if count != 4:
        return lax.all_gather(value, "narrow", axis=0, tiled=True)
    me = lax.axis_index("narrow")
    rows = value.shape[0]
    half = rows // 2
    one = swap(value, 1)
    two = swap(value, 2)
    far_low = swap(two[:half], 1)
    far_high = swap(one[half:], 2)
    full = jnp.zeros((count * rows,) + value.shape[1:], value.dtype)
    for piece, other, offset in (
        (value, 0, 0),
        (one, 1, 0),
        (two, 2, 0),
        (far_low, 3, 0),
        (far_high, 3, half),
    ):
        full = lax.dynamic_update_slice_in_dim(full, piece, (me ^ other) * rows + offset, 0)
    return full


def sum_rows(part):
    count = lax.axis_size("narrow")
    if count != 4:
        low = part.astype(BF16)
        return lax.psum_scatter(low, "narrow", scatter_dimension=0, tiled=True).astype(F32)
    me = lax.axis_index("narrow")
    rows = part.shape[0] // count
    half = rows // 2

    def block(other, offset):
        return lax.dynamic_slice_in_dim(part, (me ^ other) * rows + offset, half, 0)

    def send(pieces, bit):
        return swap(jnp.concatenate([piece.astype(BF16) for piece in pieces], axis=0), bit)

    low = send([block(1, 0), block(3, 0)], 1).astype(F32)
    high = send([block(2, half), block(3, half)], 2).astype(F32)
    low_far = send([block(2, 0).astype(F32) + low[half:]], 2).astype(F32)
    high_far = send([block(1, half).astype(F32) + high[half:]], 1).astype(F32)
    return jnp.concatenate(
        [
            block(0, 0).astype(F32) + low[:half] + low_far,
            block(0, half).astype(F32) + high[:half] + high_far,
        ],
        axis=0,
    )


def place(target, piece, start, axis):
    return lax.dynamic_update_slice_in_dim(target, piece, start, axis)


def gather_shared(value):
    count = lax.axis_size("narrow")
    if count != 4:
        return lax.all_gather(value, "narrow", axis=0, tiled=True)
    me = lax.axis_index("narrow")
    core = lax.rem(lax.axis_index("wide"), 2)
    rows = value.shape[0]
    half = rows // 2
    quarter = half // 2
    mine = lax.dynamic_slice_in_dim(value, core * half, half, 0)
    one = swap(mine, 1)
    two = swap(mine, 2)
    far = jnp.concatenate([swap(two[:quarter], 1), swap(one[quarter:], 2)], axis=0)
    fetched = jnp.concatenate([one, two, far], axis=0)
    pairs = [(index, index ^ 1) for index in range(lax.axis_size("wide"))]
    other = lax.ppermute(fetched, "wide", pairs)
    full = jnp.zeros((count * rows,) + value.shape[1:], value.dtype)
    full = place(full, value, me * rows, 0)
    for step in range(1, count):
        piece = slice((step - 1) * half, step * half)
        full = place(full, fetched[piece], (me ^ step) * rows + core * half, 0)
        full = place(full, other[piece], (me ^ step) * rows + (1 - core) * half, 0)
    return full


def exchange(value, split_axis, concat_axis):
    count = lax.axis_size("narrow")
    if count != 4:
        return lax.all_to_all(
            value, "narrow", split_axis=split_axis, concat_axis=concat_axis, tiled=True
        )
    me = lax.axis_index("narrow")
    size = value.shape[split_axis] // count
    pitch = value.shape[concat_axis]
    shape = list(value.shape)
    shape[split_axis] = size
    shape[concat_axis] = pitch * count
    result = jnp.zeros(shape, value.dtype)
    for step in range(count):
        piece = lax.dynamic_slice_in_dim(value, (me ^ step) * size, size, split_axis)
        if step:
            piece = swap(piece, step)
        result = place(result, piece, (me ^ step) * pitch, concat_axis)
    return result


def gather_columns(value):
    count = lax.axis_size("narrow")
    me = lax.axis_index("narrow")
    columns = value.shape[1]
    full = place(jnp.zeros((value.shape[0], count * columns), value.dtype), value, me * columns, 1)
    for step in range(1, count):
        full = place(full, swap(value, step), (me ^ step) * columns, 1)
    return full


def sum_columns(part):
    count = lax.axis_size("narrow")
    me = lax.axis_index("narrow")
    columns = part.shape[1] // count
    result = lax.dynamic_slice_in_dim(part, me * columns, columns, 1)
    for step in range(1, count):
        piece = lax.dynamic_slice_in_dim(part, (me ^ step) * columns, columns, 1)
        result = result + swap(piece, step)
    return result


def sum_all(value):
    for axis in ("wide", "narrow"):
        count = lax.axis_size(axis)
        bit = 1
        while bit < count:
            value = value + lax.ppermute(value, axis, [(index, index ^ bit) for index in range(count)])
            bit *= 2
    return value


def after(value, *others):
    return lax.optimization_barrier((value,) + others)[0]


def local(
    block_input,
    routes,
    first_gain,
    query_key_value_weight,
    output_weight,
    second_gain,
    router_weight,
    gate_weight,
    up_weight,
    down_weight,
    cotangent,
):
    row_part, width = block_input.shape
    me = lax.axis_index("narrow")
    row_offset = me * row_part
    gain_part = first_gain.shape[0]
    tokens = routes.shape[0]
    heads = QUERY_HEADS // KEY_VALUE_HEADS
    head_columns = query_key_value_weight.shape[1]
    groups = head_columns // ((heads + 2) * HEAD_SIZE)

    def own_rows(value):
        return lax.dynamic_slice_in_dim(value, row_offset, row_part, 0)

    inputs = gather_rows(block_input)
    gains = gather_columns(jnp.stack([first_gain, second_gain])).astype(F32)
    gain_one, gain_two = gains[0], gains[1]
    router_padded = jnp.pad(router_weight, ((0, 0), (0, LANES - E)))
    input_router = lax.all_gather(
        jnp.concatenate([query_key_value_weight, router_padded], axis=1), "wide", axis=0, tiled=True
    )
    input_full = input_router[:, :head_columns]
    router_full = input_router[:, head_columns : head_columns + E]
    output_part = lax.all_gather(output_weight, "wide", axis=1, tiled=True)
    output_full = gather_shared(after(output_part, inputs))
    lows = [sum(CHUNKS[:index]) for index in range(len(CHUNKS))]
    chunk_weights = []
    for low, size in zip(lows, CHUNKS):
        packed = jnp.stack([w[low : low + size] for w in (gate_weight, up_weight, down_weight)])
        chunk_weights.append(lax.all_gather(packed, "wide", axis=2, tiled=True))
    slot_token, block_expert, block_ends = arrange(routes)

    x_full = inputs.astype(F32)
    scale_one = lax.rsqrt(jnp.mean(x_full * x_full, axis=1, keepdims=True) + EPSILON)
    normed_one = x_full * scale_one
    attn_in = (normed_one * gain_one).astype(BF16)
    cot_full = gather_rows(after(cotangent, output_full))
    projected = jnp.einsum(
        "td,dc->ct", attn_in, input_full, preferred_element_type=F32
    ).astype(BF16)
    mixed, log_totals = attend_forward(projected, groups, heads)
    mixed_own = exchange(mixed, 1, 0)
    middle_own = block_input.astype(F32) + jnp.einsum(
        "ct,cd->td", mixed_own, output_full, preferred_element_type=F32
    )
    middle = gather_rows(middle_own.astype(BF16)).astype(F32)
    scale_two = lax.rsqrt(jnp.mean(middle * middle, axis=1, keepdims=True) + EPSILON)
    normed_two = middle * scale_two
    expert_in = (normed_two * gain_two).astype(BF16)
    logits = jnp.dot(expert_in, router_full, preferred_element_type=F32)
    picked = (routes[:, :, None] == jnp.arange(E, dtype=jnp.int32)[None, None, :]).astype(F32)
    chosen = jnp.sum(picked * logits[:, None, :], axis=2)
    gates = jax.nn.softmax(chosen, axis=1)
    gate_lanes = jnp.pad(jnp.sum(picked * gates[:, :, None], axis=1), ((0, 0), (0, LANES - E)))
    live = block_ends[E - 1 :]
    cot_rows = dispatch(cot_full, None, slot_token, block_expert, live)
    input_back = gather_shared(after(input_full.T, cot_rows))
    rows, slot_gates = dispatch(expert_in, gate_lanes, slot_token, block_expert, live)

    outs, backs, scores, grads = [], [], [], []
    for low, size, weights in zip(lows, CHUNKS, chunk_weights):
        if len(outs) == 1:
            weights, input_back = lax.optimization_barrier((weights, input_back))
        first = block_ends[low - 1 : low] if low else jnp.zeros((1,), jnp.int32)
        count = block_ends[low + size - 1 : low + size] - first
        out, back, score, grad = run_experts(
            jnp.concatenate([first, count, jnp.full((1,), low, jnp.int32)]),
            slot_token, block_expert, rows, cot_rows, slot_gates, weights, tokens
        )
        outs.append(out)
        backs.append(back)
        scores.append(score)
        grads.append(lax.psum_scatter(grad, "wide", scatter_dimension=2, tiled=True))

    def total(values):
        return sum(value.astype(F32) for value in values)

    expert_sum = sum_rows(total(backs))
    score_part = jnp.sum(picked * total(scores)[:, None, :E], axis=2)
    score_sum = sum_columns(score_part.T).T

    gates_own = own_rows(gates)
    centre = jnp.sum(gates_own * score_sum, axis=1, keepdims=True)
    logit_part = gates_own * (score_sum - centre)
    logit_grad = jnp.sum(own_rows(picked) * logit_part[:, :, None], axis=1).astype(BF16)
    norm_grad = expert_sum + jnp.einsum(
        "te,de->td", logit_grad, router_full, preferred_element_type=F32
    )
    normed_two_own = own_rows(normed_two)
    row_dot = jnp.sum(norm_grad * normed_two_own * gain_two, axis=1, keepdims=True)
    gain_two_part = jnp.sum(norm_grad * normed_two_own, axis=0)
    mid_grad = cotangent.astype(F32) + own_rows(scale_two) * (
        gain_two * norm_grad - normed_two_own * row_dot / width
    )
    branch_grad = mid_grad.astype(BF16)
    mixed_grad_own = jnp.einsum(
        "td,cd->ct", branch_grad, output_full, preferred_element_type=F32
    ).astype(BF16)
    mixed_grad = exchange(after(mixed_grad_own, grads[0]), 0, 1)
    block_output = (middle_own + sum_rows(after(total(outs), mixed_grad))).astype(BF16)
    projected_grad = attend_backward(projected, mixed, log_totals, mixed_grad, groups, heads)
    grad_input_w = jnp.einsum(
        "td,ct->dc", attn_in, projected_grad, preferred_element_type=F32
    ).astype(BF16)
    projected_own = exchange(after(projected_grad, grads[1]), 1, 0)
    input_sum = jnp.einsum("ct,cd->td", after(projected_own, grads[2]), input_back, preferred_element_type=F32)
    grad_output_w = sum_rows(
        after(
            jnp.einsum("ct,td->cd", mixed_own, branch_grad, preferred_element_type=F32),
            projected_own,
        )
    ).astype(BF16)
    grad_router = jnp.einsum(
        "te,td->ed", logit_grad, own_rows(expert_in), preferred_element_type=F32
    )
    early_sum = sum_all(jnp.concatenate([grad_router, gain_two_part[None]], axis=0))
    input_w_grad = lax.psum_scatter(
        grad_input_w, "wide", scatter_dimension=0, tiled=True
    )
    output_w_grad = lax.psum_scatter(
        grad_output_w, "wide", scatter_dimension=1, tiled=True
    )
    router_part = router_weight.shape[0]
    router_grad = lax.dynamic_slice_in_dim(
        early_sum[:E], lax.axis_index("wide") * router_part, router_part, 1
    ).T
    normed_one_own = own_rows(normed_one)
    gain_one_sum = sum_all(jnp.sum(input_sum * normed_one_own, axis=0)[None])
    gain_own = lax.dynamic_slice_in_dim(
        jnp.concatenate([gain_one_sum, early_sum[E:]], axis=0), me * gain_part, gain_part, 1
    )
    input_dot = jnp.sum(input_sum * normed_one_own * gain_one, axis=1, keepdims=True)
    input_grad = mid_grad + own_rows(scale_one) * (
        gain_one * input_sum - normed_one_own * input_dot / width
    )
    grads, _ = lax.optimization_barrier((grads, input_sum))
    gate_grad, up_grad, down_grad = (
        jnp.concatenate([grad[index] for grad in grads], axis=0).astype(F32) for index in range(3)
    )
    return (
        block_output,
        input_grad,
        gain_own[0],
        input_w_grad.astype(F32),
        output_w_grad.astype(F32),
        gain_own[1],
        router_grad,
        gate_grad,
        up_grad,
        down_grad,
    )


def solution(mesh):
    placed = (
        P(("wide", "narrow"), None),
        P("wide", None),
        P("narrow"),
        P("wide", "narrow"),
        P("narrow", "wide"),
        P("narrow"),
        P("wide", None),
        P(None, "wide", "narrow"),
        P(None, "wide", "narrow"),
        P(None, "wide", "narrow"),
        P(("wide", "narrow"), None),
    )
    return jax.shard_map(
        local,
        mesh=mesh,
        in_specs=placed,
        out_specs=(
            P(("wide", "narrow"), None),
            P(("wide", "narrow"), None),
            P("narrow"),
            P("wide", "narrow"),
            P("narrow", "wide"),
            P("narrow"),
            P("wide", None),
            P(None, "wide", "narrow"),
            P(None, "wide", "narrow"),
            P(None, "wide", "narrow"),
        ),
        check_vma=False,
    )
```

```python
import functools

import jax
import jax.numpy as jnp
from jax import lax
from jax.experimental import pallas as pl
from jax.experimental.pallas import tpu as pltpu
from jax.sharding import PartitionSpec as P

QUERY_HEADS = 24
KEY_VALUE_HEADS = 8
HEAD_SIZE = 64
E = 16
TOPK = 2
SEQUENCE_LENGTH = 2048
BLOCK = 256
QB = 256
KB = 256
LANES = 128
PITCH = 13
UNROLL = 8
CHUNKS = (6, 6, 4)
EPSILON = 1e-05
F32 = jnp.float32
BF16 = jnp.bfloat16

def stack_heads(ref, row, first, heads):
    return jnp.concatenate(
        [ref[row + h * HEAD_SIZE : row + (h + 1) * HEAD_SIZE, pl.ds(first, QB)] for h in range(heads)], axis=1
    )

def rows_of(block):
    return block.astype(jnp.float32).T.astype(jnp.bfloat16)

def forward_kernel(heads, qkv_ref, out_ref, total_ref, key_ref):
    index = pl.program_id(1)
    first = pl.multiple_of(index * QB, QB)
    key_row = heads * HEAD_SIZE
    value_row = key_row + HEAD_SIZE
    @pl.when(index == 0)
    def _():
        key_ref[...] = rows_of(qkv_ref[key_row:value_row, :])
    queries = stack_heads(qkv_ref, 0, first, heads) * jnp.bfloat16(0.125)
    lanes = heads * QB

    def step(block, carry, masked):
        highest, denominator, mixed = carry
        start = pl.multiple_of(block * KB, KB)
        scores = jnp.dot(key_ref[pl.ds(start, KB), :], queries, preferred_element_type=jnp.float32)
        if masked:
            key_at = lax.broadcasted_iota(jnp.int32, (KB, QB), 0)
            query_at = lax.broadcasted_iota(jnp.int32, (KB, QB), 1)
            seen = jnp.concatenate([key_at <= query_at] * heads, axis=1)
            scores = jnp.where(seen, scores, -1e30)
        raised_to = jnp.maximum(highest, jnp.max(scores, axis=0, keepdims=True))
        shrink = jnp.exp(highest - raised_to)
        raised = jnp.exp(scores - raised_to)
        denominator = denominator * shrink + jnp.sum(raised, axis=0, keepdims=True)
        mixed = mixed * shrink + jnp.dot(
            qkv_ref[value_row : value_row + HEAD_SIZE, pl.ds(start, KB)], raised.astype(jnp.bfloat16),
            preferred_element_type=jnp.float32)
        return raised_to, denominator, mixed

    carry = (jnp.full((1, lanes), -1e30, jnp.float32), jnp.zeros((1, lanes), jnp.float32), jnp.zeros((HEAD_SIZE, lanes), jnp.float32))
    carry = lax.fori_loop(0, index, lambda b, c: step(b, c, False), carry)
    highest, denominator, mixed = step(index, carry, True)
    mixed = (mixed / denominator).astype(jnp.bfloat16)
    for h in range(heads):
        out_ref[h * HEAD_SIZE : (h + 1) * HEAD_SIZE, :] = mixed[:, h * QB : (h + 1) * QB]
    total_ref[0, 0] = highest + jnp.log(denominator)

def attend_forward(qkv, groups, heads):
    tokens = qkv.shape[1]
    blocks = tokens // QB
    rows = (heads + 2) * HEAD_SIZE
    flops = groups * heads * tokens * tokens * HEAD_SIZE * 2
    return pl.pallas_call(
        functools.partial(forward_kernel, heads),
        grid=(groups, blocks),
        in_specs=[pl.BlockSpec((rows, tokens), lambda g, i: (g, 0))],
        out_specs=[pl.BlockSpec((heads * HEAD_SIZE, QB), lambda g, i: (g, i)),
                   pl.BlockSpec((1, 1, 1, heads * QB), lambda g, i: (g, i, 0, 0))],
        out_shape=[jax.ShapeDtypeStruct((groups * heads * HEAD_SIZE, tokens), jnp.bfloat16),
                   jax.ShapeDtypeStruct((groups, blocks, 1, heads * QB), jnp.float32)],
        scratch_shapes=[pltpu.VMEM((tokens, HEAD_SIZE), jnp.bfloat16)],
        cost_estimate=pl.CostEstimate(flops=flops * 14, bytes_accessed=qkv.size * 4, transcendentals=0),
        compiler_params=pltpu.CompilerParams(vmem_limit_bytes=32 << 20),
    )(qkv)

def backward_kernel(heads, qkv_ref, out_ref, total_ref, grad_ref, result_ref, key_ref, value_ref, grad_key_ref, grad_value_ref):
    index = pl.program_id(1)
    first = pl.multiple_of(index * QB, QB)
    key_row = heads * HEAD_SIZE
    value_row = key_row + HEAD_SIZE
    @pl.when(index == 0)
    def _():
        key_ref[...] = rows_of(qkv_ref[key_row:value_row, :])
        value_ref[...] = rows_of(qkv_ref[value_row : value_row + HEAD_SIZE, :])
        grad_key_ref[...] = jnp.zeros_like(grad_key_ref)
        grad_value_ref[...] = jnp.zeros_like(grad_value_ref)
    queries = stack_heads(qkv_ref, 0, first, heads) * jnp.bfloat16(0.125)
    grads = stack_heads(grad_ref, 0, 0, heads)
    outs = stack_heads(out_ref, 0, 0, heads)
    centre = jnp.sum(grads.astype(jnp.float32) * outs.astype(jnp.float32), axis=0, keepdims=True)
    totals = total_ref[0, 0]
    query_rows = rows_of(queries)
    grad_rows = rows_of(grads)

    def step(block, grad_query, masked):
        start = pl.multiple_of(block * KB, KB)
        keys = key_ref[pl.ds(start, KB), :]
        scores = jnp.dot(keys, queries, preferred_element_type=jnp.float32)
        probs = jnp.exp(scores - totals)
        if masked:
            key_at = lax.broadcasted_iota(jnp.int32, (KB, QB), 0)
            query_at = lax.broadcasted_iota(jnp.int32, (KB, QB), 1)
            seen = jnp.concatenate([key_at <= query_at] * heads, axis=1)
            probs = jnp.where(seen, probs, 0.0)
        grad_probs = jnp.dot(value_ref[pl.ds(start, KB), :], grads, preferred_element_type=jnp.float32)
        grad_scores = (probs * (grad_probs - centre)).astype(jnp.bfloat16)
        grad_value_ref[pl.ds(start, KB), :] += jnp.dot(probs.astype(jnp.bfloat16), grad_rows, preferred_element_type=jnp.float32)
        grad_key_ref[pl.ds(start, KB), :] += jnp.dot(grad_scores, query_rows, preferred_element_type=jnp.float32)
        return grad_query + jnp.dot(qkv_ref[key_row:value_row, pl.ds(start, KB)], grad_scores, preferred_element_type=jnp.float32)

    grad_query = lax.fori_loop(0, index, lambda b, c: step(b, c, False), jnp.zeros((HEAD_SIZE, heads * QB), jnp.float32))
    grad_query = (step(index, grad_query, True) * 0.125).astype(jnp.bfloat16)
    for h in range(heads):
        result_ref[h * HEAD_SIZE : (h + 1) * HEAD_SIZE, pl.ds(first, QB)] = grad_query[:, h * QB : (h + 1) * QB]
    @pl.when(index == pl.num_programs(1) - 1)
    def _():
        result_ref[key_row:value_row, :] = grad_key_ref[...].T.astype(jnp.bfloat16)
        result_ref[value_row : value_row + HEAD_SIZE, :] = grad_value_ref[...].T.astype(jnp.bfloat16)

def attend_backward(qkv, out, totals, grad, groups, heads):
    tokens = qkv.shape[1]
    blocks = tokens // QB
    rows = (heads + 2) * HEAD_SIZE
    flops = groups * heads * tokens * tokens * HEAD_SIZE * 5
    return pl.pallas_call(
        functools.partial(backward_kernel, heads),
        grid=(groups, blocks),
        in_specs=[pl.BlockSpec((rows, tokens), lambda g, i: (g, 0)),
                  pl.BlockSpec((heads * HEAD_SIZE, QB), lambda g, i: (g, i)),
                  pl.BlockSpec((1, 1, 1, heads * QB), lambda g, i: (g, i, 0, 0)),
                  pl.BlockSpec((heads * HEAD_SIZE, QB), lambda g, i: (g, i))],
        out_specs=pl.BlockSpec((rows, tokens), lambda g, i: (g, 0)),
        out_shape=jax.ShapeDtypeStruct((groups * rows, tokens), jnp.bfloat16),
        scratch_shapes=[pltpu.VMEM((tokens, HEAD_SIZE), jnp.bfloat16), pltpu.VMEM((tokens, HEAD_SIZE), jnp.bfloat16),
                        pltpu.VMEM((tokens, HEAD_SIZE), jnp.float32), pltpu.VMEM((tokens, HEAD_SIZE), jnp.float32)],
        cost_estimate=pl.CostEstimate(flops=flops * 7, bytes_accessed=qkv.size * 8, transcendentals=0),
        compiler_params=pltpu.CompilerParams(vmem_limit_bytes=40 << 20),
    )(qkv, out, totals, grad)


def arrange(experts_of):
    tokens = experts_of.shape[0]
    assigned = tokens * TOPK
    flat_ids = experts_of.reshape(assigned)
    one_hot = (flat_ids[:, None] == jnp.arange(E, dtype=jnp.int32)[None, :]).astype(jnp.int32)
    counts = jnp.sum(one_hot, axis=0, dtype=jnp.int32)
    blocks = jnp.maximum((counts + BLOCK - 1) // BLOCK, 1)
    block_ends = jnp.cumsum(blocks, dtype=jnp.int32)
    starts = (block_ends - blocks) * BLOCK
    before = jnp.cumsum(one_hot, axis=0, dtype=jnp.int32) - one_hot
    slot_of = jnp.sum((before + starts[None, :]) * one_hot, axis=1, dtype=jnp.int32)
    slots = assigned + E * BLOCK
    slot_token = (
        jnp.full((slots,), tokens, jnp.int32)
        .at[slot_of]
        .set(jnp.arange(assigned, dtype=jnp.int32) // TOPK)
    )
    firsts = jnp.arange(slots // BLOCK, dtype=jnp.int32)
    later = (firsts[:, None] >= block_ends[None, :]).astype(jnp.int32)
    block_expert = jnp.minimum(jnp.sum(later, axis=1, dtype=jnp.int32), E - 1)
    return slot_token, block_expert, block_ends


def row_at(index):
    return pl.ds(index * PITCH, PITCH)


def dispatch_kernel(blocks, gated, token_ref, expert_ref, live_ref, me_ref, *refs):
    sources, refs = refs[:blocks], refs[blocks:]
    if gated:
        gain_ref, router_ref, route_ref, out_ref, gate_ref, held, moved = refs
    else:
        out_ref, held, moved = refs
    step = pl.program_id(0)
    rows, width = sources[0].shape
    tokens = rows * blocks
    parts = width // LANES
    lanes = lax.broadcasted_iota(jnp.int32, (BLOCK, LANES), 1)

    def hold(number, source_ref):
        def part_of(piece, carry):
            start = pl.multiple_of(piece * BLOCK, BLOCK)
            first = pl.multiple_of((me_ref[0] ^ number) * rows + start, BLOCK)
            value = source_ref[pl.ds(start, BLOCK), :].astype(F32)
            if gated:
                scale = lax.rsqrt(jnp.mean(value * value, axis=1, keepdims=True) + EPSILON)
                low = (value * scale * gain_ref[...]).astype(BF16)
                logits = jnp.dot(low, router_ref[...], preferred_element_type=F32)
                routes = route_ref[pl.ds(first, BLOCK), :]
                picks = [lanes == routes[:, slot : slot + 1] for slot in range(TOPK)]
                chosen = [
                    jnp.sum(jnp.where(pick, logits, 0.0), axis=1, keepdims=True) for pick in picks
                ]
                highest = jnp.maximum(chosen[0], chosen[1])
                raised = [jnp.exp(value - highest) for value in chosen]
                total = raised[0] + raised[1]
                held[pl.ds(first * PITCH + parts, BLOCK, stride=PITCH), :] = jnp.where(
                    picks[0],
                    raised[0] / total,
                    jnp.where(picks[1], raised[1] / total, 0.0),
                )
                value = low.astype(F32)
            for part in range(parts):
                held[pl.ds(first * PITCH + part, BLOCK, stride=PITCH), :] = value[
                    :, part * LANES : (part + 1) * LANES
                ]
            return carry

        lax.fori_loop(0, rows // BLOCK, part_of, 0)

    @pl.when(step == 0)
    def _():
        held[tokens * PITCH : (tokens + 1) * PITCH, :] = jnp.zeros((PITCH, LANES), F32)
        for number, source_ref in enumerate(sources):
            hold(number, source_ref)

    @pl.when(step < live_ref[0])
    def _():
        def move(group, carry):
            base = group * UNROLL
            for j in range(UNROLL):
                moved[row_at(base + j), :] = held[row_at(token_ref[step * BLOCK + base + j]), :]
            return carry

        lax.fori_loop(0, BLOCK // UNROLL, move, 0)
        for part in range(parts):
            out_ref[:, part * LANES : (part + 1) * LANES] = moved[
                pl.ds(part, BLOCK, stride=PITCH), :
            ].astype(BF16)
        if gated:
            spare = moved[pl.ds(parts, BLOCK, stride=PITCH), :]
            own = jnp.where(lanes == expert_ref[step], spare, 0.0)
            gate_ref[...] = jnp.sum(own, axis=1, keepdims=True)


def dispatch(sources, extras, slot_token, block_expert, live):
    rows, width = sources[0].shape
    tokens = rows * len(sources)
    slots = slot_token.shape[0]
    gated = bool(extras)
    at = lambda i, t, e, n, m: (jnp.minimum(i, n[0] - 1), 0)

    def whole(value):
        return pl.BlockSpec(
            value.shape, lambda i, t, e, n, m: (0, 0), pipeline_mode=pl.Buffered(1)
        )

    out_specs = [pl.BlockSpec((BLOCK, width), at), pl.BlockSpec((BLOCK, 1), at)]
    out_shape = [
        jax.ShapeDtypeStruct((slots, width), BF16),
        jax.ShapeDtypeStruct((slots, 1), F32),
    ]
    me = lax.axis_index("narrow").astype(jnp.int32)[None]
    if len(sources) == 1:
        me = jnp.zeros((1,), jnp.int32)
    return pl.pallas_call(
        functools.partial(dispatch_kernel, len(sources), gated),
        grid_spec=pltpu.PrefetchScalarGridSpec(
            num_scalar_prefetch=4,
            grid=(slots // BLOCK,),
            in_specs=[whole(value) for value in (*sources, *extras)],
            out_specs=out_specs if gated else out_specs[:1],
            scratch_shapes=[
                pltpu.VMEM(((tokens + 1) * PITCH, LANES), F32),
                pltpu.VMEM((BLOCK * PITCH, LANES), F32),
            ],
        ),
        out_shape=out_shape if gated else out_shape[:1],
        cost_estimate=pl.CostEstimate(
            flops=42 * 10**9, bytes_accessed=24 * BLOCK * width * 2, transcendentals=0
        ),
        compiler_params=pltpu.CompilerParams(vmem_limit_bytes=48 << 20),
    )(slot_token, block_expert, live, me, *sources, *extras)


def expert_kernel(
    span_ref,
    expert_ref,
    token_ref,
    row_ref,
    cot_ref,
    gate_ref,
    weight_ref,
    out_ref,
    back_ref,
    score_ref,
    grad_ref,
    gate_sum,
    up_sum,
    down_sum,
    out_sum,
    back_sum,
    moved,
    staging,
    sems,
):
    step = pl.program_id(0)
    total = span_ref[1]
    block = span_ref[0] + jnp.minimum(step, total - 1)
    expert = expert_ref[block]
    width = row_ref.shape[1]
    parts = width // LANES
    tokens = out_sum.shape[0] // PITCH - 1
    following = expert_ref[jnp.minimum(block + 1, expert_ref.shape[0] - 1)]
    closing = jnp.logical_or(step == total - 1, following != expert)

    @pl.when(step == 0)
    def _():
        for ref in (out_sum, back_sum, moved, gate_sum, up_sum, down_sum):
            ref[...] = jnp.zeros_like(ref)

    @pl.when(step < total)
    def _():
        rows = row_ref[...]
        cots = cot_ref[...]
        gates = gate_ref[...]
        gate_weight = weight_ref[0, 0]
        up_weight = weight_ref[1, 0]
        down_weight = weight_ref[2, 0]
        gate_val = jnp.dot(rows, gate_weight, preferred_element_type=F32)
        up_val = jnp.dot(rows, up_weight, preferred_element_type=F32)
        raw_grad = jnp.dot(cots, down_weight, preferred_element_type=F32)
        sigma = jax.nn.sigmoid(gate_val)
        silu_val = gate_val * sigma
        active = (silu_val * up_val).astype(BF16).astype(F32)
        scores = jnp.sum(active * raw_grad, axis=1, keepdims=True)
        act_grad = raw_grad * gates
        gate_d = (act_grad * up_val * sigma * (1.0 + gate_val * (1.0 - sigma))).astype(BF16)
        up_d = (act_grad * silu_val).astype(BF16)
        weighted = (active * gates).astype(BF16)
        over_rows = (((0,), (0,)), ((), ()))
        over_hidden = (((1,), (1,)), ((), ()))
        gate_sum[...] += lax.dot_general(gate_d, rows, over_rows, preferred_element_type=F32)
        up_sum[...] += lax.dot_general(up_d, rows, over_rows, preferred_element_type=F32)
        down_sum[...] += lax.dot_general(weighted, cots, over_rows, preferred_element_type=F32)

        def spread(value):
            for part in range(parts):
                moved[pl.ds(part, BLOCK, stride=PITCH), :] = value[:, part * LANES : (part + 1) * LANES]

        def combine(sum_ref):
            def add(group, carry):
                base = group * UNROLL
                at = [row_at(token_ref[block * BLOCK + base + j]) for j in range(UNROLL)]
                new = [sum_ref[at[j], :] + moved[row_at(base + j), :] for j in range(UNROLL)]
                for j in range(UNROLL):
                    sum_ref[at[j], :] = new[j]
                return carry

            lax.fori_loop(0, BLOCK // UNROLL, add, 0)

        spread(lax.dot_general(weighted, down_weight, over_hidden, preferred_element_type=F32))
        combine(out_sum)
        spread(
            lax.dot_general(gate_d, gate_weight, over_hidden, preferred_element_type=F32)
            + lax.dot_general(up_d, up_weight, over_hidden, preferred_element_type=F32)
        )
        lanes = lax.broadcasted_iota(jnp.int32, (BLOCK, LANES), 1)
        moved[pl.ds(parts, BLOCK, stride=PITCH), :] = jnp.where(lanes == expert, scores, 0.0)
        combine(back_sum)

        @pl.when(closing)
        def _():
            for index, ref in enumerate((gate_sum, up_sum, down_sum)):
                grad_ref[index, 0] = ref[...].T.astype(BF16)
                ref[...] = jnp.zeros_like(ref)

    @pl.when(step == total - 1)
    def _():
        for first in range(0, tokens, BLOCK):
            score_ref[first : first + BLOCK, :] = back_sum[
                pl.ds(first * PITCH + parts, BLOCK, stride=PITCH), :
            ]

        jobs = [
            (first, source, target)
            for first in range(0, tokens, BLOCK)
            for source, target in ((out_sum, out_ref), (back_sum, back_ref))
        ]

        def copy(number):
            first, _, target = jobs[number]
            slot = number % 2
            return pltpu.make_async_copy(
                staging.at[slot], target.at[pl.ds(first, BLOCK), :], sems.at[slot]
            )

        for number, (first, source, _) in enumerate(jobs):
            if number >= 2:
                copy(number - 2).wait()
            for part in range(parts):
                staging[number % 2, :, part * LANES : (part + 1) * LANES] = source[
                    pl.ds(first * PITCH + part, BLOCK, stride=PITCH), :
                ].astype(BF16)
            copy(number).start()
        copy(len(jobs) - 2).wait()
        copy(len(jobs) - 1).wait()


def run_experts(span, slot_token, block_expert, rows, cots, gates, weights, tokens):
    width = rows.shape[1]
    experts, hidden = weights.shape[1], weights.shape[3]
    index = lambda i, s: s[0] + jnp.minimum(i, s[1] - 1)
    at = lambda i, s, e, t: (index(i, s), 0)
    pick = pl.BlockSpec(
        (3, 1, width, hidden), lambda i, s, e, t: (0, e[index(i, s)] - s[2], 0, 0)
    )
    anywhere = pl.BlockSpec(memory_space=pl.ANY)
    block_count = experts * 3 // 2
    return pl.pallas_call(
        expert_kernel,
        grid_spec=pltpu.PrefetchScalarGridSpec(
            num_scalar_prefetch=3,
            grid=(tokens * TOPK // BLOCK + experts,),
            in_specs=[
                pl.BlockSpec((BLOCK, width), at),
                pl.BlockSpec((BLOCK, width), at),
                pl.BlockSpec((BLOCK, 1), at),
                pick,
            ],
            out_specs=[
                anywhere,
                anywhere,
                pl.BlockSpec((tokens, LANES), lambda i, s, e, t: (0, 0)),
                pick,
            ],
            scratch_shapes=[pltpu.VMEM((hidden, width), F32)] * 3
            + [pltpu.VMEM(((tokens + 1) * PITCH, LANES), F32)] * 2
            + [
                pltpu.VMEM((BLOCK * PITCH, LANES), F32),
                pltpu.VMEM((2, BLOCK, width), BF16),
                pltpu.SemaphoreType.DMA((2,)),
            ],
        ),
        out_shape=[
            jax.ShapeDtypeStruct((tokens, width), BF16),
            jax.ShapeDtypeStruct((tokens, width), BF16),
            jax.ShapeDtypeStruct((tokens, LANES), F32),
            jax.ShapeDtypeStruct(weights.shape, BF16),
        ],
        cost_estimate=pl.CostEstimate(
            flops=block_count * 2 * BLOCK * width * hidden * 9 * 6,
            bytes_accessed=weights.size * 4 + block_count * BLOCK * width * 4,
            transcendentals=0,
        ),
        compiler_params=pltpu.CompilerParams(vmem_limit_bytes=62 << 20),
    )(span, block_expert, slot_token, rows, cots, gates, weights)


def swap(value, bit):
    count = lax.axis_size("narrow")
    return lax.ppermute(value, "narrow", [(index, index ^ bit) for index in range(count)])


def ordered(pieces, axis):
    me = lax.axis_index("narrow")
    count = len(pieces)
    return jnp.concatenate(
        [lax.select_n(me ^ index, *pieces) for index in range(count)], axis=axis
    )


def gather_blocks(value):
    half = value.shape[0] // 2
    one = swap(value, 1)
    two = swap(value, 2)
    before = yield
    low, high = (two[:half], one[half:]) if before is None else after((two[:half], one[half:]), before)
    far = jnp.concatenate([swap(low, 1), swap(high, 2)], axis=0)
    yield [value, one, two, far]


def gather_start(value):
    if lax.axis_size("narrow") != 4:
        return [lax.all_gather(value, "narrow", axis=0, tiled=True)]
    rounds = gather_blocks(value)
    next(rounds)
    return rounds


def gather_end(rounds, before=None):
    return rounds if isinstance(rounds, list) else rounds.send(before)


def gather_rows_end(rounds, before=None):
    blocks = gather_end(rounds, before)
    return ordered(blocks, 0) if len(blocks) > 1 else blocks[0]


def gather_rows(value):
    return gather_rows_end(gather_start(value))


def sum_rows(parts, turned):
    count = lax.axis_size("narrow")
    if count != 4:
        low = sum(part.astype(F32) for part in parts).astype(BF16)
        return lax.psum_scatter(low, "narrow", scatter_dimension=0, tiled=True).astype(F32)
    me = lax.axis_index("narrow")
    rows = parts[0].shape[0] // count
    half = rows // 2

    def block(other, offset):
        if turned:
            first = other * rows + offset
            pieces = [lax.slice_in_dim(part, first, first + half) for part in parts]
        else:
            first = (me ^ other) * rows + offset
            pieces = [lax.dynamic_slice_in_dim(part, first, half, 0) for part in parts]
        return sum(piece.astype(F32) for piece in pieces)

    def send(low_blocks, low_bit, high_blocks, high_bit):
        both = [
            jnp.concatenate([piece.astype(BF16) for piece in blocks], axis=0)
            for blocks in (low_blocks, high_blocks)
        ]
        low_send, high_send = lax.optimization_barrier(both)
        return swap(low_send, low_bit).astype(F32), swap(high_send, high_bit).astype(F32)

    low, high = send([block(1, 0), block(3, 0)], 1, [block(2, half), block(3, half)], 2)
    low_far, high_far = send(
        [block(2, 0) + low[half:]], 2, [block(1, half) + high[half:]], 1
    )
    return jnp.concatenate(
        [block(0, 0) + low[:half] + low_far, block(0, half) + high[:half] + high_far], axis=0
    )


def to_rows(value):
    count = lax.axis_size("narrow")
    if count != 4:
        return [lax.all_to_all(value, "narrow", split_axis=1, concat_axis=0, tiled=True)]
    me = lax.axis_index("narrow")
    size = value.shape[1] // count
    pieces = [
        lax.dynamic_slice_in_dim(value, (me ^ step) * size, size, 1) for step in range(count)
    ]
    return [swap(piece, step) if step else piece for step, piece in enumerate(pieces)]


def product_sum(equation, lefts, rights):
    return sum(
        jnp.einsum(equation, left, right, preferred_element_type=F32)
        for left, right in zip(lefts, rights)
    )


def to_heads(value):
    if len(value) == 1:
        return lax.all_to_all(value[0], "narrow", split_axis=0, concat_axis=1, tiled=True)
    pieces = value
    return ordered([swap(piece, step) if step else piece for step, piece in enumerate(pieces)], 1)


def gather_columns(value):
    count = lax.axis_size("narrow")
    return ordered([value] + [swap(value, step) for step in range(1, count)], 1)


def sum_columns(part):
    count = lax.axis_size("narrow")
    me = lax.axis_index("narrow")
    columns = part.shape[1] // count
    result = lax.dynamic_slice_in_dim(part, me * columns, columns, 1)
    for step in range(1, count):
        piece = lax.dynamic_slice_in_dim(part, (me ^ step) * columns, columns, 1)
        result = result + swap(piece, step)
    return result


def sum_all(value):
    for axis in ("wide", "narrow"):
        count = lax.axis_size(axis)
        bit = 1
        while bit < count:
            value = value + lax.ppermute(value, axis, [(index, index ^ bit) for index in range(count)])
            bit *= 2
    return value


def after(value, *others):
    return lax.optimization_barrier((value,) + others)[0]


def local(
    block_input,
    routes,
    first_gain,
    query_key_value_weight,
    output_weight,
    second_gain,
    router_weight,
    gate_weight,
    up_weight,
    down_weight,
    cotangent,
):
    row_part, width = block_input.shape
    me = lax.axis_index("narrow")
    row_offset = me * row_part
    gain_part = first_gain.shape[0]
    tokens = routes.shape[0]
    heads = QUERY_HEADS // KEY_VALUE_HEADS
    head_columns = query_key_value_weight.shape[1]
    groups = head_columns // ((heads + 2) * HEAD_SIZE)

    def own_rows(value):
        return lax.dynamic_slice_in_dim(value, row_offset, row_part, 0)

    inputs = gather_rows(block_input)
    gains = gather_columns(jnp.stack([first_gain, second_gain])).astype(F32)
    gain_one, gain_two = gains[0], gains[1]
    input_router = lax.all_gather(
        jnp.concatenate(
            [query_key_value_weight, jnp.pad(router_weight, ((0, 0), (0, LANES - E)))], axis=1
        ),
        "wide",
        axis=0,
        tiled=True,
    )
    input_full = input_router[:, :head_columns]
    router_padded = input_router[:, head_columns:]
    router_full = router_padded[:, :E]
    output_part = lax.all_gather(output_weight, "wide", axis=1, tiled=True)
    lows = [sum(CHUNKS[:index]) for index in range(len(CHUNKS))]
    chunk_weights = []
    for low, size in zip(lows, CHUNKS):
        packed = jnp.stack([w[low : low + size] for w in (gate_weight, up_weight, down_weight)])
        chunk_weights.append(lax.all_gather(packed, "wide", axis=2, tiled=True))
    slot_token, block_expert, block_ends = arrange(routes)

    x_full = inputs.astype(F32)
    scale_one = lax.rsqrt(jnp.mean(x_full * x_full, axis=1, keepdims=True) + EPSILON)
    attn_in = (x_full * scale_one * gain_one).astype(BF16)
    projected = jnp.einsum(
        "td,dc->ct", attn_in, input_full, preferred_element_type=F32
    ).astype(BF16)
    output_rounds = gather_start(after(output_part, projected))
    cot_rounds = gather_start(after(cotangent, projected))
    mixed, log_totals = attend_forward(projected, groups, heads)
    mixed_own = to_rows(mixed)
    output_blocks = gather_end(output_rounds, mixed)
    middle_own = block_input.astype(F32) + product_sum("ct,cd->td", mixed_own, output_blocks)
    middle_low = middle_own.astype(BF16)
    cot_blocks = gather_end(cot_rounds, middle_low)
    live = block_ends[E - 1 :]
    (cot_rows,) = dispatch(cot_blocks, (), slot_token, block_expert, live)
    middle_blocks = gather_end(gather_start(middle_low))
    rows, slot_gates = dispatch(
        middle_blocks, (gain_two[None], router_padded, routes), slot_token, block_expert, live
    )

    outs, backs, scores, grads = [], [], [], []
    for low, size, weights in zip(lows, CHUNKS, chunk_weights):
        first = block_ends[low - 1 : low] if low else jnp.zeros((1,), jnp.int32)
        count = block_ends[low + size - 1 : low + size] - first
        out, back, score, grad = run_experts(
            jnp.concatenate([first, count, jnp.full((1,), low, jnp.int32)]),
            slot_token, block_expert, rows, cot_rows, slot_gates, weights, tokens
        )
        outs.append(out)
        backs.append(back)
        scores.append(score)
        grads.append(lax.psum_scatter(grad, "wide", scatter_dimension=2, tiled=True))

    def total(values):
        return sum(value.astype(F32) for value in values)

    expert_sum = sum_rows(backs, False)
    picked = (routes[:, :, None] == jnp.arange(E, dtype=jnp.int32)[None, None, :]).astype(F32)
    score_part = jnp.sum(picked * total(scores)[:, None, :E], axis=2)
    score_sum = sum_columns(score_part.T).T

    middle_back = after(middle_low, rows).astype(F32)
    scale_two_own = lax.rsqrt(jnp.mean(middle_back * middle_back, axis=1, keepdims=True) + EPSILON)
    normed_two_own = middle_back * scale_two_own
    expert_in_own = (normed_two_own * gain_two).astype(BF16)
    picked_own = own_rows(picked)
    logits_own = jnp.dot(expert_in_own, router_full, preferred_element_type=F32)
    gates_own = jax.nn.softmax(jnp.sum(picked_own * logits_own[:, None, :], axis=2), axis=1)
    centre = jnp.sum(gates_own * score_sum, axis=1, keepdims=True)
    logit_part = gates_own * (score_sum - centre)
    logit_grad = jnp.sum(picked_own * logit_part[:, :, None], axis=1).astype(BF16)
    norm_grad = expert_sum + jnp.einsum(
        "te,de->td", logit_grad, router_full, preferred_element_type=F32
    )
    row_dot = jnp.sum(norm_grad * normed_two_own * gain_two, axis=1, keepdims=True)
    gain_two_part = jnp.sum(norm_grad * normed_two_own, axis=0)
    mid_grad = cotangent.astype(F32) + scale_two_own * (
        gain_two * norm_grad - normed_two_own * row_dot / width
    )
    branch_grad = mid_grad.astype(BF16)
    mixed_grad_own = [
        jnp.einsum("td,cd->ct", branch_grad, block, preferred_element_type=F32).astype(BF16)
        for block in output_blocks
    ]
    mixed_grad = to_heads(mixed_grad_own)
    projected_grad = attend_backward(projected, mixed, log_totals, mixed_grad, groups, heads)
    grad_input_w = jnp.einsum(
        "td,ct->dc", attn_in, projected_grad, preferred_element_type=F32
    ).astype(BF16)
    input_part = jnp.einsum(
        "ct,dc->td", after(projected_grad, grads[0]), input_full, preferred_element_type=F32
    ).astype(BF16)
    input_sum = sum_rows([input_part], False)
    grad_output_w = sum_rows(
        [
            jnp.concatenate(
                [
                    jnp.einsum("ct,td->cd", block, branch_grad, preferred_element_type=F32).astype(
                        BF16
                    )
                    for block in after(mixed_own, input_sum)
                ],
                axis=0,
            )
        ],
        True,
    ).astype(BF16)
    block_output = (
        middle_own + sum_rows(after(outs, input_sum), False)
    ).astype(BF16)
    grad_router = jnp.einsum(
        "te,td->ed", logit_grad, expert_in_own, preferred_element_type=F32
    )
    x_own = after(block_input, projected_grad).astype(F32)
    scale_one_own = lax.rsqrt(jnp.mean(x_own * x_own, axis=1, keepdims=True) + EPSILON)
    normed_one_own = x_own * scale_one_own
    gain_one_part = jnp.sum(input_sum * normed_one_own, axis=0)
    small_sum = sum_all(
        jnp.concatenate([grad_router, gain_one_part[None], gain_two_part[None]], axis=0)
    )
    gain_own = lax.dynamic_slice_in_dim(small_sum[E:], me * gain_part, gain_part, 1)
    router_part = router_weight.shape[0]
    router_grad = lax.dynamic_slice_in_dim(
        small_sum[:E], lax.axis_index("wide") * router_part, router_part, 1
    ).T
    input_dot = jnp.sum(input_sum * normed_one_own * gain_one, axis=1, keepdims=True)
    input_grad = mid_grad + scale_one_own * (
        gain_one * input_sum - normed_one_own * input_dot / width
    )
    input_w_grad = lax.psum_scatter(
        after(grad_input_w, grads[1], input_grad), "wide", scatter_dimension=0, tiled=True
    )
    output_w_grad = lax.psum_scatter(
        after(grad_output_w, grads[1]), "wide", scatter_dimension=1, tiled=True
    )
    grads = after(grads, block_output, small_sum, grad_output_w, input_grad)
    gate_grad, up_grad, down_grad = (
        jnp.concatenate([grad[index] for grad in grads], axis=0).astype(F32) for index in range(3)
    )
    return (
        block_output,
        input_grad,
        gain_own[0],
        input_w_grad.astype(F32),
        output_w_grad.astype(F32),
        gain_own[1],
        router_grad,
        gate_grad,
        up_grad,
        down_grad,
    )


def solution(mesh):
    placed = (
        P(("wide", "narrow"), None),
        P("wide", None),
        P("narrow"),
        P("wide", "narrow"),
        P("narrow", "wide"),
        P("narrow"),
        P("wide", None),
        P(None, "wide", "narrow"),
        P(None, "wide", "narrow"),
        P(None, "wide", "narrow"),
        P(("wide", "narrow"), None),
    )
    return jax.shard_map(
        local,
        mesh=mesh,
        in_specs=placed,
        out_specs=(
            P(("wide", "narrow"), None),
            P(("wide", "narrow"), None),
            P("narrow"),
            P("wide", "narrow"),
            P("narrow", "wide"),
            P("narrow"),
            P("wide", None),
            P(None, "wide", "narrow"),
            P(None, "wide", "narrow"),
            P(None, "wide", "narrow"),
        ),
        check_vma=False,
    )
```

```python
import functools

import jax
import jax.numpy as jnp
from jax import lax
from jax.experimental import pallas as pl
from jax.experimental.pallas import tpu as pltpu
from jax.sharding import PartitionSpec as P

QUERY_HEADS = 24
KEY_VALUE_HEADS = 8
HEAD_SIZE = 64
E = 16
TOPK = 2
SEQUENCE_LENGTH = 2048
BLOCK = 256
QB = 256
KB = 256
LANES = 128
PITCH = 13
UNROLL = 8
CHUNKS = (4, 6, 6)
EPSILON = 1e-05
F32 = jnp.float32
BF16 = jnp.bfloat16

def stack_heads(ref, row, first, heads):
    return jnp.concatenate(
        [ref[row + h * HEAD_SIZE : row + (h + 1) * HEAD_SIZE, pl.ds(first, QB)] for h in range(heads)], axis=1
    )

def rows_of(block):
    return block.astype(jnp.float32).T.astype(jnp.bfloat16)

def forward_kernel(heads, qkv_ref, out_ref, total_ref, key_ref):
    index = pl.program_id(1)
    first = pl.multiple_of(index * QB, QB)
    key_row = heads * HEAD_SIZE
    value_row = key_row + HEAD_SIZE
    @pl.when(index == 0)
    def _():
        key_ref[...] = rows_of(qkv_ref[key_row:value_row, :])
    queries = stack_heads(qkv_ref, 0, first, heads) * jnp.bfloat16(0.125)
    lanes = heads * QB

    def step(block, carry, masked):
        highest, denominator, mixed = carry
        start = pl.multiple_of(block * KB, KB)
        scores = jnp.dot(key_ref[pl.ds(start, KB), :], queries, preferred_element_type=jnp.float32)
        if masked:
            key_at = lax.broadcasted_iota(jnp.int32, (KB, QB), 0)
            query_at = lax.broadcasted_iota(jnp.int32, (KB, QB), 1)
            seen = jnp.concatenate([key_at <= query_at] * heads, axis=1)
            scores = jnp.where(seen, scores, -1e30)
        raised_to = jnp.maximum(highest, jnp.max(scores, axis=0, keepdims=True))
        shrink = jnp.exp(highest - raised_to)
        raised = jnp.exp(scores - raised_to)
        denominator = denominator * shrink + jnp.sum(raised, axis=0, keepdims=True)
        mixed = mixed * shrink + jnp.dot(
            qkv_ref[value_row : value_row + HEAD_SIZE, pl.ds(start, KB)], raised.astype(jnp.bfloat16),
            preferred_element_type=jnp.float32)
        return raised_to, denominator, mixed

    carry = (jnp.full((1, lanes), -1e30, jnp.float32), jnp.zeros((1, lanes), jnp.float32), jnp.zeros((HEAD_SIZE, lanes), jnp.float32))
    carry = lax.fori_loop(0, index, lambda b, c: step(b, c, False), carry)
    highest, denominator, mixed = step(index, carry, True)
    mixed = (mixed / denominator).astype(jnp.bfloat16)
    for h in range(heads):
        out_ref[h * HEAD_SIZE : (h + 1) * HEAD_SIZE, :] = mixed[:, h * QB : (h + 1) * QB]
    total_ref[0, 0] = highest + jnp.log(denominator)

def attend_forward(qkv, groups, heads):
    tokens = qkv.shape[1]
    blocks = tokens // QB
    rows = (heads + 2) * HEAD_SIZE
    flops = groups * heads * tokens * tokens * HEAD_SIZE * 2
    return pl.pallas_call(
        functools.partial(forward_kernel, heads),
        grid=(groups, blocks),
        in_specs=[pl.BlockSpec((rows, tokens), lambda g, i: (g, 0))],
        out_specs=[pl.BlockSpec((heads * HEAD_SIZE, QB), lambda g, i: (g, i)),
                   pl.BlockSpec((1, 1, 1, heads * QB), lambda g, i: (g, i, 0, 0))],
        out_shape=[jax.ShapeDtypeStruct((groups * heads * HEAD_SIZE, tokens), jnp.bfloat16),
                   jax.ShapeDtypeStruct((groups, blocks, 1, heads * QB), jnp.float32)],
        scratch_shapes=[pltpu.VMEM((tokens, HEAD_SIZE), jnp.bfloat16)],
        cost_estimate=pl.CostEstimate(flops=flops * 14, bytes_accessed=qkv.size * 4, transcendentals=0),
        compiler_params=pltpu.CompilerParams(vmem_limit_bytes=32 << 20),
    )(qkv)

def backward_kernel(heads, qkv_ref, out_ref, total_ref, grad_ref, result_ref, key_ref, value_ref, grad_key_ref, grad_value_ref):
    index = pl.program_id(1)
    first = pl.multiple_of(index * QB, QB)
    key_row = heads * HEAD_SIZE
    value_row = key_row + HEAD_SIZE
    @pl.when(index == 0)
    def _():
        key_ref[...] = rows_of(qkv_ref[key_row:value_row, :])
        value_ref[...] = rows_of(qkv_ref[value_row : value_row + HEAD_SIZE, :])
        grad_key_ref[...] = jnp.zeros_like(grad_key_ref)
        grad_value_ref[...] = jnp.zeros_like(grad_value_ref)
    queries = stack_heads(qkv_ref, 0, first, heads) * jnp.bfloat16(0.125)
    grads = stack_heads(grad_ref, 0, 0, heads)
    outs = stack_heads(out_ref, 0, 0, heads)
    centre = jnp.sum(grads.astype(jnp.float32) * outs.astype(jnp.float32), axis=0, keepdims=True)
    totals = total_ref[0, 0]
    query_rows = rows_of(queries)
    grad_rows = rows_of(grads)

    def step(block, grad_query, masked):
        start = pl.multiple_of(block * KB, KB)
        keys = key_ref[pl.ds(start, KB), :]
        scores = jnp.dot(keys, queries, preferred_element_type=jnp.float32)
        probs = jnp.exp(scores - totals)
        if masked:
            key_at = lax.broadcasted_iota(jnp.int32, (KB, QB), 0)
            query_at = lax.broadcasted_iota(jnp.int32, (KB, QB), 1)
            seen = jnp.concatenate([key_at <= query_at] * heads, axis=1)
            probs = jnp.where(seen, probs, 0.0)
        grad_probs = jnp.dot(value_ref[pl.ds(start, KB), :], grads, preferred_element_type=jnp.float32)
        grad_scores = (probs * (grad_probs - centre)).astype(jnp.bfloat16)
        grad_value_ref[pl.ds(start, KB), :] += jnp.dot(probs.astype(jnp.bfloat16), grad_rows, preferred_element_type=jnp.float32)
        grad_key_ref[pl.ds(start, KB), :] += jnp.dot(grad_scores, query_rows, preferred_element_type=jnp.float32)
        return grad_query + jnp.dot(qkv_ref[key_row:value_row, pl.ds(start, KB)], grad_scores, preferred_element_type=jnp.float32)

    grad_query = lax.fori_loop(0, index, lambda b, c: step(b, c, False), jnp.zeros((HEAD_SIZE, heads * QB), jnp.float32))
    grad_query = (step(index, grad_query, True) * 0.125).astype(jnp.bfloat16)
    for h in range(heads):
        result_ref[h * HEAD_SIZE : (h + 1) * HEAD_SIZE, pl.ds(first, QB)] = grad_query[:, h * QB : (h + 1) * QB]
    @pl.when(index == pl.num_programs(1) - 1)
    def _():
        result_ref[key_row:value_row, :] = grad_key_ref[...].T.astype(jnp.bfloat16)
        result_ref[value_row : value_row + HEAD_SIZE, :] = grad_value_ref[...].T.astype(jnp.bfloat16)

def attend_backward(qkv, out, totals, grad, groups, heads):
    tokens = qkv.shape[1]
    blocks = tokens // QB
    rows = (heads + 2) * HEAD_SIZE
    flops = groups * heads * tokens * tokens * HEAD_SIZE * 5
    return pl.pallas_call(
        functools.partial(backward_kernel, heads),
        grid=(groups, blocks),
        in_specs=[pl.BlockSpec((rows, tokens), lambda g, i: (g, 0)),
                  pl.BlockSpec((heads * HEAD_SIZE, QB), lambda g, i: (g, i)),
                  pl.BlockSpec((1, 1, 1, heads * QB), lambda g, i: (g, i, 0, 0)),
                  pl.BlockSpec((heads * HEAD_SIZE, QB), lambda g, i: (g, i))],
        out_specs=pl.BlockSpec((rows, tokens), lambda g, i: (g, 0)),
        out_shape=jax.ShapeDtypeStruct((groups * rows, tokens), jnp.bfloat16),
        scratch_shapes=[pltpu.VMEM((tokens, HEAD_SIZE), jnp.bfloat16), pltpu.VMEM((tokens, HEAD_SIZE), jnp.bfloat16),
                        pltpu.VMEM((tokens, HEAD_SIZE), jnp.float32), pltpu.VMEM((tokens, HEAD_SIZE), jnp.float32)],
        cost_estimate=pl.CostEstimate(flops=flops * 7, bytes_accessed=qkv.size * 8, transcendentals=0),
        compiler_params=pltpu.CompilerParams(vmem_limit_bytes=40 << 20),
    )(qkv, out, totals, grad)


def arrange(experts_of):
    tokens = experts_of.shape[0]
    assigned = tokens * TOPK
    flat_ids = experts_of.reshape(assigned)
    one_hot = (flat_ids[:, None] == jnp.arange(E, dtype=jnp.int32)[None, :]).astype(jnp.int32)
    counts = jnp.sum(one_hot, axis=0, dtype=jnp.int32)
    blocks = jnp.maximum((counts + BLOCK - 1) // BLOCK, 1)
    block_ends = jnp.cumsum(blocks, dtype=jnp.int32)
    starts = (block_ends - blocks) * BLOCK
    before = jnp.cumsum(one_hot, axis=0, dtype=jnp.int32) - one_hot
    slot_of = jnp.sum((before + starts[None, :]) * one_hot, axis=1, dtype=jnp.int32)
    slots = assigned + E * BLOCK
    slot_token = (
        jnp.full((slots,), tokens, jnp.int32)
        .at[slot_of]
        .set(jnp.arange(assigned, dtype=jnp.int32) // TOPK)
    )
    firsts = jnp.arange(slots // BLOCK, dtype=jnp.int32)
    later = (firsts[:, None] >= block_ends[None, :]).astype(jnp.int32)
    block_expert = jnp.minimum(jnp.sum(later, axis=1, dtype=jnp.int32), E - 1)
    return slot_token, block_expert, block_ends


def row_at(index):
    return pl.ds(index * PITCH, PITCH)


def dispatch_kernel(blocks, gated, token_ref, expert_ref, live_ref, me_ref, *refs):
    sources, refs = refs[:blocks], refs[blocks:]
    if gated:
        gain_ref, router_ref, route_ref, out_ref, gate_ref, held, moved = refs
    else:
        out_ref, held, moved = refs
    step = pl.program_id(0)
    rows, width = sources[0].shape
    tokens = rows * blocks
    parts = width // LANES
    lanes = lax.broadcasted_iota(jnp.int32, (BLOCK, LANES), 1)

    def hold(number, source_ref):
        def part_of(piece, carry):
            start = pl.multiple_of(piece * BLOCK, BLOCK)
            first = pl.multiple_of((me_ref[0] ^ number) * rows + start, BLOCK)
            value = source_ref[pl.ds(start, BLOCK), :].astype(F32)
            if gated:
                scale = lax.rsqrt(jnp.mean(value * value, axis=1, keepdims=True) + EPSILON)
                low = (value * scale * gain_ref[...]).astype(BF16)
                logits = jnp.dot(low, router_ref[...], preferred_element_type=F32)
                routes = route_ref[pl.ds(first, BLOCK), :]
                picks = [lanes == routes[:, slot : slot + 1] for slot in range(TOPK)]
                chosen = [
                    jnp.sum(jnp.where(pick, logits, 0.0), axis=1, keepdims=True) for pick in picks
                ]
                highest = jnp.maximum(chosen[0], chosen[1])
                raised = [jnp.exp(value - highest) for value in chosen]
                total = raised[0] + raised[1]
                held[pl.ds(first * PITCH + parts, BLOCK, stride=PITCH), :] = jnp.where(
                    picks[0],
                    raised[0] / total,
                    jnp.where(picks[1], raised[1] / total, 0.0),
                )
                value = low.astype(F32)
            for part in range(parts):
                held[pl.ds(first * PITCH + part, BLOCK, stride=PITCH), :] = value[
                    :, part * LANES : (part + 1) * LANES
                ]
            return carry

        lax.fori_loop(0, rows // BLOCK, part_of, 0)

    @pl.when(step == 0)
    def _():
        held[tokens * PITCH : (tokens + 1) * PITCH, :] = jnp.zeros((PITCH, LANES), F32)
        for number, source_ref in enumerate(sources):
            hold(number, source_ref)

    @pl.when(step < live_ref[0])
    def _():
        def move(group, carry):
            base = group * UNROLL
            for j in range(UNROLL):
                moved[row_at(base + j), :] = held[row_at(token_ref[step * BLOCK + base + j]), :]
            return carry

        lax.fori_loop(0, BLOCK // UNROLL, move, 0)
        for part in range(parts):
            out_ref[:, part * LANES : (part + 1) * LANES] = moved[
                pl.ds(part, BLOCK, stride=PITCH), :
            ].astype(BF16)
        if gated:
            spare = moved[pl.ds(parts, BLOCK, stride=PITCH), :]
            own = jnp.where(lanes == expert_ref[step], spare, 0.0)
            gate_ref[...] = jnp.sum(own, axis=1, keepdims=True)


def dispatch(sources, extras, slot_token, block_expert, live):
    rows, width = sources[0].shape
    tokens = rows * len(sources)
    slots = slot_token.shape[0]
    gated = bool(extras)
    at = lambda i, t, e, n, m: (jnp.minimum(i, n[0] - 1), 0)

    def whole(value):
        return pl.BlockSpec(
            value.shape, lambda i, t, e, n, m: (0, 0), pipeline_mode=pl.Buffered(1)
        )

    out_specs = [pl.BlockSpec((BLOCK, width), at), pl.BlockSpec((BLOCK, 1), at)]
    out_shape = [
        jax.ShapeDtypeStruct((slots, width), BF16),
        jax.ShapeDtypeStruct((slots, 1), F32),
    ]
    me = lax.axis_index("narrow").astype(jnp.int32)[None]
    if len(sources) == 1:
        me = jnp.zeros((1,), jnp.int32)
    return pl.pallas_call(
        functools.partial(dispatch_kernel, len(sources), gated),
        grid_spec=pltpu.PrefetchScalarGridSpec(
            num_scalar_prefetch=4,
            grid=(slots // BLOCK,),
            in_specs=[whole(value) for value in (*sources, *extras)],
            out_specs=out_specs if gated else out_specs[:1],
            scratch_shapes=[
                pltpu.VMEM(((tokens + 1) * PITCH, LANES), F32),
                pltpu.VMEM((BLOCK * PITCH, LANES), F32),
            ],
        ),
        out_shape=out_shape if gated else out_shape[:1],
        cost_estimate=pl.CostEstimate(
            flops=42 * 10**9, bytes_accessed=24 * BLOCK * width * 2, transcendentals=0
        ),
        compiler_params=pltpu.CompilerParams(vmem_limit_bytes=48 << 20),
    )(slot_token, block_expert, live, me, *sources, *extras)


def expert_kernel(
    span_ref,
    expert_ref,
    token_ref,
    row_ref,
    cot_ref,
    gate_ref,
    weight_ref,
    out_ref,
    back_ref,
    score_ref,
    grad_ref,
    gate_sum,
    up_sum,
    down_sum,
    out_sum,
    back_sum,
    moved,
    staging,
    sems,
):
    step = pl.program_id(0)
    total = span_ref[1]
    block = span_ref[0] + jnp.minimum(step, total - 1)
    expert = expert_ref[block]
    width = row_ref.shape[1]
    parts = width // LANES
    tokens = out_sum.shape[0] // PITCH - 1
    following = expert_ref[jnp.minimum(block + 1, expert_ref.shape[0] - 1)]
    closing = jnp.logical_or(step == total - 1, following != expert)

    @pl.when(step == 0)
    def _():
        for ref in (out_sum, back_sum, moved, gate_sum, up_sum, down_sum):
            ref[...] = jnp.zeros_like(ref)

    @pl.when(step < total)
    def _():
        rows = row_ref[...]
        cots = cot_ref[...]
        gates = gate_ref[...]
        gate_weight = weight_ref[0, 0]
        up_weight = weight_ref[1, 0]
        down_weight = weight_ref[2, 0]
        gate_val = jnp.dot(rows, gate_weight, preferred_element_type=F32)
        up_val = jnp.dot(rows, up_weight, preferred_element_type=F32)
        raw_grad = jnp.dot(cots, down_weight, preferred_element_type=F32)
        sigma = jax.nn.sigmoid(gate_val)
        silu_val = gate_val * sigma
        active = (silu_val * up_val).astype(BF16).astype(F32)
        scores = jnp.sum(active * raw_grad, axis=1, keepdims=True)
        act_grad = raw_grad * gates
        gate_d = (act_grad * up_val * sigma * (1.0 + gate_val * (1.0 - sigma))).astype(BF16)
        up_d = (act_grad * silu_val).astype(BF16)
        weighted = (active * gates).astype(BF16)
        over_rows = (((0,), (0,)), ((), ()))
        over_hidden = (((1,), (1,)), ((), ()))
        gate_sum[...] += lax.dot_general(gate_d, rows, over_rows, preferred_element_type=F32)
        up_sum[...] += lax.dot_general(up_d, rows, over_rows, preferred_element_type=F32)
        down_sum[...] += lax.dot_general(weighted, cots, over_rows, preferred_element_type=F32)

        def spread(value):
            for part in range(parts):
                moved[pl.ds(part, BLOCK, stride=PITCH), :] = value[:, part * LANES : (part + 1) * LANES]

        def combine(sum_ref):
            def add(group, carry):
                base = group * UNROLL
                at = [row_at(token_ref[block * BLOCK + base + j]) for j in range(UNROLL)]
                new = [sum_ref[at[j], :] + moved[row_at(base + j), :] for j in range(UNROLL)]
                for j in range(UNROLL):
                    sum_ref[at[j], :] = new[j]
                return carry

            lax.fori_loop(0, BLOCK // UNROLL, add, 0)

        spread(lax.dot_general(weighted, down_weight, over_hidden, preferred_element_type=F32))
        combine(out_sum)
        spread(
            lax.dot_general(gate_d, gate_weight, over_hidden, preferred_element_type=F32)
            + lax.dot_general(up_d, up_weight, over_hidden, preferred_element_type=F32)
        )
        lanes = lax.broadcasted_iota(jnp.int32, (BLOCK, LANES), 1)
        moved[pl.ds(parts, BLOCK, stride=PITCH), :] = jnp.where(lanes == expert, scores, 0.0)
        combine(back_sum)

        @pl.when(closing)
        def _():
            for index, ref in enumerate((gate_sum, up_sum, down_sum)):
                grad_ref[index, 0] = ref[...].T.astype(BF16)
                ref[...] = jnp.zeros_like(ref)

    @pl.when(step == total - 1)
    def _():
        for first in range(0, tokens, BLOCK):
            score_ref[first : first + BLOCK, :] = back_sum[
                pl.ds(first * PITCH + parts, BLOCK, stride=PITCH), :
            ]

        jobs = [
            (first, source, target)
            for first in range(0, tokens, BLOCK)
            for source, target in ((out_sum, out_ref), (back_sum, back_ref))
        ]

        def copy(number):
            first, _, target = jobs[number]
            slot = number % 2
            return pltpu.make_async_copy(
                staging.at[slot], target.at[pl.ds(first, BLOCK), :], sems.at[slot]
            )

        for number, (first, source, _) in enumerate(jobs):
            if number >= 2:
                copy(number - 2).wait()
            for part in range(parts):
                staging[number % 2, :, part * LANES : (part + 1) * LANES] = source[
                    pl.ds(first * PITCH + part, BLOCK, stride=PITCH), :
                ].astype(BF16)
            copy(number).start()
        copy(len(jobs) - 2).wait()
        copy(len(jobs) - 1).wait()


def run_experts(span, slot_token, block_expert, rows, cots, gates, weights, tokens):
    width = rows.shape[1]
    experts, hidden = weights.shape[1], weights.shape[3]
    index = lambda i, s: s[0] + jnp.minimum(i, s[1] - 1)
    at = lambda i, s, e, t: (index(i, s), 0)
    pick = pl.BlockSpec(
        (3, 1, width, hidden), lambda i, s, e, t: (0, e[index(i, s)] - s[2], 0, 0)
    )
    anywhere = pl.BlockSpec(memory_space=pl.ANY)
    block_count = experts * 3 // 2
    return pl.pallas_call(
        expert_kernel,
        grid_spec=pltpu.PrefetchScalarGridSpec(
            num_scalar_prefetch=3,
            grid=(tokens * TOPK // BLOCK + experts,),
            in_specs=[
                pl.BlockSpec((BLOCK, width), at),
                pl.BlockSpec((BLOCK, width), at),
                pl.BlockSpec((BLOCK, 1), at),
                pick,
            ],
            out_specs=[
                anywhere,
                anywhere,
                pl.BlockSpec((tokens, LANES), lambda i, s, e, t: (0, 0)),
                pick,
            ],
            scratch_shapes=[pltpu.VMEM((hidden, width), F32)] * 3
            + [pltpu.VMEM(((tokens + 1) * PITCH, LANES), F32)] * 2
            + [
                pltpu.VMEM((BLOCK * PITCH, LANES), F32),
                pltpu.VMEM((2, BLOCK, width), BF16),
                pltpu.SemaphoreType.DMA((2,)),
            ],
        ),
        out_shape=[
            jax.ShapeDtypeStruct((tokens, width), BF16),
            jax.ShapeDtypeStruct((tokens, width), BF16),
            jax.ShapeDtypeStruct((tokens, LANES), F32),
            jax.ShapeDtypeStruct(weights.shape, BF16),
        ],
        cost_estimate=pl.CostEstimate(
            flops=block_count * 2 * BLOCK * width * hidden * 9 * 6,
            bytes_accessed=weights.size * 4 + block_count * BLOCK * width * 4,
            transcendentals=0,
        ),
        compiler_params=pltpu.CompilerParams(vmem_limit_bytes=62 << 20),
    )(span, block_expert, slot_token, rows, cots, gates, weights)


def swap(value, bit):
    count = lax.axis_size("narrow")
    return lax.ppermute(value, "narrow", [(index, index ^ bit) for index in range(count)])


def ordered(pieces, axis):
    me = lax.axis_index("narrow")
    count = len(pieces)
    return jnp.concatenate(
        [lax.select_n(me ^ index, *pieces) for index in range(count)], axis=axis
    )


def gather_blocks(value):
    half = value.shape[0] // 2
    one = swap(value, 1)
    two = swap(value, 2)
    before = yield
    low, high = (two[:half], one[half:]) if before is None else after((two[:half], one[half:]), before)
    far = jnp.concatenate([swap(low, 1), swap(high, 2)], axis=0)
    yield [value, one, two, far]


def gather_start(value, axis=0):
    if lax.axis_size("narrow") != 4:
        return [lax.all_gather(value, "narrow", axis=axis, tiled=True)]
    rounds = gather_blocks(value)
    next(rounds)
    return rounds


def gather_end(rounds, before=None):
    return rounds if isinstance(rounds, list) else rounds.send(before)


def gather_rows_end(rounds, before=None):
    blocks = gather_end(rounds, before)
    return ordered(blocks, 0) if len(blocks) > 1 else blocks[0]


def gather_rows(value):
    return gather_rows_end(gather_start(value))


def sum_rows(parts, turned):
    count = lax.axis_size("narrow")
    if count != 4:
        low = sum(part.astype(F32) for part in parts).astype(BF16)
        return lax.psum_scatter(low, "narrow", scatter_dimension=0, tiled=True).astype(F32)
    me = lax.axis_index("narrow")
    rows = parts[0].shape[0] // count
    half = rows // 2

    def block(other, offset):
        if turned:
            first = other * rows + offset
            pieces = [lax.slice_in_dim(part, first, first + half) for part in parts]
        else:
            first = (me ^ other) * rows + offset
            pieces = [lax.dynamic_slice_in_dim(part, first, half, 0) for part in parts]
        return sum(piece.astype(F32) for piece in pieces)

    def send(low_blocks, low_bit, high_blocks, high_bit):
        both = [
            jnp.concatenate([piece.astype(BF16) for piece in blocks], axis=0)
            for blocks in (low_blocks, high_blocks)
        ]
        low_send, high_send = lax.optimization_barrier(both)
        return swap(low_send, low_bit).astype(F32), swap(high_send, high_bit).astype(F32)

    low, high = send([block(1, 0), block(3, 0)], 1, [block(2, half), block(3, half)], 2)
    low_far, high_far = send(
        [block(2, 0) + low[half:]], 2, [block(1, half) + high[half:]], 1
    )
    return jnp.concatenate(
        [block(0, 0) + low[:half] + low_far, block(0, half) + high[:half] + high_far], axis=0
    )


def to_rows(value):
    count = lax.axis_size("narrow")
    if count != 4:
        return [lax.all_to_all(value, "narrow", split_axis=1, concat_axis=0, tiled=True)]
    me = lax.axis_index("narrow")
    size = value.shape[1] // count
    pieces = [
        lax.dynamic_slice_in_dim(value, (me ^ step) * size, size, 1) for step in range(count)
    ]
    return [swap(piece, step) if step else piece for step, piece in enumerate(pieces)]


def product_sum(equation, lefts, rights):
    return sum(
        jnp.einsum(equation, left, right, preferred_element_type=F32)
        for left, right in zip(lefts, rights)
    )


def to_heads(value):
    if len(value) == 1:
        return lax.all_to_all(value[0], "narrow", split_axis=0, concat_axis=1, tiled=True)
    pieces = value
    return ordered([swap(piece, step) if step else piece for step, piece in enumerate(pieces)], 1)


def gather_columns(value):
    count = lax.axis_size("narrow")
    return ordered([value] + [swap(value, step) for step in range(1, count)], 1)


def sum_columns(part):
    count = lax.axis_size("narrow")
    me = lax.axis_index("narrow")
    columns = part.shape[1] // count
    result = lax.dynamic_slice_in_dim(part, me * columns, columns, 1)
    for step in range(1, count):
        piece = lax.dynamic_slice_in_dim(part, (me ^ step) * columns, columns, 1)
        result = result + swap(piece, step)
    return result


def sum_all(value):
    for axis in ("wide", "narrow"):
        count = lax.axis_size(axis)
        bit = 1
        while bit < count:
            value = value + lax.ppermute(value, axis, [(index, index ^ bit) for index in range(count)])
            bit *= 2
    return value


def after(value, *others):
    return lax.optimization_barrier((value,) + others)[0]


def local(
    block_input,
    routes,
    first_gain,
    query_key_value_weight,
    output_weight,
    second_gain,
    router_weight,
    gate_weight,
    up_weight,
    down_weight,
    cotangent,
):
    row_part, width = block_input.shape
    me = lax.axis_index("narrow")
    row_offset = me * row_part
    gain_part = first_gain.shape[0]
    tokens = routes.shape[0]
    heads = QUERY_HEADS // KEY_VALUE_HEADS
    head_columns = query_key_value_weight.shape[1]
    groups = head_columns // ((heads + 2) * HEAD_SIZE)

    def own_rows(value):
        return lax.dynamic_slice_in_dim(value, row_offset, row_part, 0)

    inputs = gather_rows(block_input)
    gains = gather_columns(jnp.stack([first_gain, second_gain])).astype(F32)
    gain_one, gain_two = gains[0], gains[1]
    packed = lax.all_gather(
        jnp.concatenate(
            [
                query_key_value_weight,
                jnp.pad(router_weight, ((0, 0), (0, LANES - E))),
                output_weight.T,
            ],
            axis=1,
        ),
        "wide",
        axis=0,
        tiled=True,
    )
    input_full = packed[:, :head_columns]
    router_padded = packed[:, head_columns : head_columns + LANES]
    router_full = router_padded[:, :E]
    output_part = packed[:, head_columns + LANES :]
    lows = [sum(CHUNKS[:index]) for index in range(len(CHUNKS))]
    chunk_weights = []
    for low, size in zip(lows, CHUNKS):
        packed = jnp.stack([w[low : low + size] for w in (gate_weight, up_weight, down_weight)])
        chunk_weights.append(lax.all_gather(packed, "wide", axis=2, tiled=True))
    slot_token, block_expert, block_ends = arrange(routes)

    x_full = inputs.astype(F32)
    scale_one = lax.rsqrt(jnp.mean(x_full * x_full, axis=1, keepdims=True) + EPSILON)
    attn_in = (x_full * scale_one * gain_one).astype(BF16)
    projected = jnp.einsum(
        "td,dc->ct", attn_in, input_full, preferred_element_type=F32
    ).astype(BF16)
    output_rounds = gather_start(after(output_part, projected), 1)
    cot_rounds = gather_start(after(cotangent, projected))
    mixed, log_totals = attend_forward(projected, groups, heads)
    mixed_own = to_rows(mixed)
    output_blocks = gather_end(output_rounds, mixed)
    middle_own = block_input.astype(F32) + product_sum("ct,dc->td", mixed_own, output_blocks)
    middle_low = middle_own.astype(BF16)
    cot_blocks = gather_end(cot_rounds, middle_low)
    live = block_ends[E - 1 :]
    (cot_rows,) = dispatch(cot_blocks, (), slot_token, block_expert, live)
    middle_blocks = gather_end(gather_start(middle_low))
    rows, slot_gates = dispatch(
        middle_blocks, (gain_two[None], router_padded, routes), slot_token, block_expert, live
    )

    outs, backs, scores, grads = [], [], [], []
    for low, size, weights in zip(lows, CHUNKS, chunk_weights):
        first = block_ends[low - 1 : low] if low else jnp.zeros((1,), jnp.int32)
        count = block_ends[low + size - 1 : low + size] - first
        out, back, score, grad = run_experts(
            jnp.concatenate([first, count, jnp.full((1,), low, jnp.int32)]),
            slot_token, block_expert, rows, cot_rows, slot_gates, weights, tokens
        )
        outs.append(out)
        backs.append(back)
        scores.append(score)
        grads.append(lax.psum_scatter(grad, "wide", scatter_dimension=2, tiled=True))

    def total(values):
        return sum(value.astype(F32) for value in values)

    expert_sum = sum_rows(backs, False)
    picked = (routes[:, :, None] == jnp.arange(E, dtype=jnp.int32)[None, None, :]).astype(F32)
    score_part = jnp.sum(picked * total(scores)[:, None, :E], axis=2)
    score_sum = sum_columns(score_part.T).T

    middle_back = after(middle_low, rows).astype(F32)
    scale_two_own = lax.rsqrt(jnp.mean(middle_back * middle_back, axis=1, keepdims=True) + EPSILON)
    normed_two_own = middle_back * scale_two_own
    expert_in_own = (normed_two_own * gain_two).astype(BF16)
    picked_own = own_rows(picked)
    logits_own = jnp.dot(expert_in_own, router_full, preferred_element_type=F32)
    gates_own = jax.nn.softmax(jnp.sum(picked_own * logits_own[:, None, :], axis=2), axis=1)
    centre = jnp.sum(gates_own * score_sum, axis=1, keepdims=True)
    logit_part = gates_own * (score_sum - centre)
    logit_grad = jnp.sum(picked_own * logit_part[:, :, None], axis=1).astype(BF16)
    norm_grad = expert_sum + jnp.einsum(
        "te,de->td", logit_grad, router_full, preferred_element_type=F32
    )
    row_dot = jnp.sum(norm_grad * normed_two_own * gain_two, axis=1, keepdims=True)
    gain_two_part = jnp.sum(norm_grad * normed_two_own, axis=0)
    mid_grad = cotangent.astype(F32) + scale_two_own * (
        gain_two * norm_grad - normed_two_own * row_dot / width
    )
    branch_grad = mid_grad.astype(BF16)
    mixed_grad_own = [
        jnp.einsum("td,dc->ct", branch_grad, block, preferred_element_type=F32).astype(BF16)
        for block in output_blocks
    ]
    mixed_grad = to_heads(mixed_grad_own)
    projected_grad = attend_backward(projected, mixed, log_totals, mixed_grad, groups, heads)
    grad_input_w = jnp.einsum(
        "td,ct->dc", attn_in, projected_grad, preferred_element_type=F32
    ).astype(BF16)
    input_part = jnp.einsum(
        "ct,dc->td", after(projected_grad, grads[0]), input_full, preferred_element_type=F32
    ).astype(BF16)
    input_sum = sum_rows([input_part], False)
    grad_output_w = sum_rows(
        [
            jnp.concatenate(
                [
                    jnp.einsum("ct,td->cd", block, branch_grad, preferred_element_type=F32).astype(
                        BF16
                    )
                    for block in after(mixed_own, input_sum)
                ],
                axis=0,
            )
        ],
        True,
    ).astype(BF16)
    block_output = (
        middle_own + sum_rows(after(outs, input_sum), False)
    ).astype(BF16)
    grad_router = jnp.einsum(
        "te,td->ed", logit_grad, expert_in_own, preferred_element_type=F32
    )
    x_own = after(block_input, projected_grad).astype(F32)
    scale_one_own = lax.rsqrt(jnp.mean(x_own * x_own, axis=1, keepdims=True) + EPSILON)
    normed_one_own = x_own * scale_one_own
    gain_one_part = jnp.sum(input_sum * normed_one_own, axis=0)
    small_sum = sum_all(
        jnp.concatenate([grad_router, gain_one_part[None], gain_two_part[None]], axis=0)
    )
    gain_own = lax.dynamic_slice_in_dim(small_sum[E:], me * gain_part, gain_part, 1)
    router_part = router_weight.shape[0]
    router_grad = lax.dynamic_slice_in_dim(
        small_sum[:E], lax.axis_index("wide") * router_part, router_part, 1
    ).T
    input_dot = jnp.sum(input_sum * normed_one_own * gain_one, axis=1, keepdims=True)
    input_grad = mid_grad + scale_one_own * (
        gain_one * input_sum - normed_one_own * input_dot / width
    )
    packed_grad = lax.psum_scatter(
        after(
            jnp.concatenate([grad_input_w, grad_output_w.T], axis=1), grads[1], input_grad
        ),
        "wide",
        scatter_dimension=0,
        tiled=True,
    ).astype(F32)
    input_w_grad = packed_grad[:, :head_columns]
    output_w_grad = packed_grad[:, head_columns:].T
    grads = after(grads, block_output, small_sum, grad_output_w, input_grad)
    gate_grad, up_grad, down_grad = (
        jnp.concatenate([grad[index] for grad in grads], axis=0).astype(F32) for index in range(3)
    )
    return (
        block_output,
        input_grad,
        gain_own[0],
        input_w_grad,
        output_w_grad,
        gain_own[1],
        router_grad,
        gate_grad,
        up_grad,
        down_grad,
    )


def solution(mesh):
    placed = (
        P(("wide", "narrow"), None),
        P("wide", None),
        P("narrow"),
        P("wide", "narrow"),
        P("narrow", "wide"),
        P("narrow"),
        P("wide", None),
        P(None, "wide", "narrow"),
        P(None, "wide", "narrow"),
        P(None, "wide", "narrow"),
        P(("wide", "narrow"), None),
    )
    return jax.shard_map(
        local,
        mesh=mesh,
        in_specs=placed,
        out_specs=(
            P(("wide", "narrow"), None),
            P(("wide", "narrow"), None),
            P("narrow"),
            P("wide", "narrow"),
            P("narrow", "wide"),
            P("narrow"),
            P("wide", None),
            P(None, "wide", "narrow"),
            P(None, "wide", "narrow"),
            P(None, "wide", "narrow"),
        ),
        check_vma=False,
    )
```

```python
import functools

import jax
import jax.numpy as jnp
from jax import lax
from jax.experimental import pallas as pl
from jax.experimental.pallas import tpu as pltpu
from jax.sharding import PartitionSpec as P

QUERY_HEADS = 24
KEY_VALUE_HEADS = 8
HEAD_SIZE = 64
E = 16
TOPK = 2
SEQUENCE_LENGTH = 2048
BLOCK = 256
QB = 256
KB = 256
LANES = 128
PITCH = 13
UNROLL = 8
CHUNKS = (4, 6, 6)
EPSILON = 1e-05
F32 = jnp.float32
BF16 = jnp.bfloat16

def stack_heads(ref, row, first, heads):
    return jnp.concatenate(
        [ref[row + h * HEAD_SIZE : row + (h + 1) * HEAD_SIZE, pl.ds(first, QB)] for h in range(heads)], axis=1
    )

def rows_of(block):
    return block.astype(jnp.float32).T.astype(jnp.bfloat16)

def forward_kernel(heads, qkv_ref, out_ref, total_ref, key_ref):
    index = pl.program_id(1)
    first = pl.multiple_of(index * QB, QB)
    key_row = heads * HEAD_SIZE
    value_row = key_row + HEAD_SIZE
    @pl.when(index == 0)
    def _():
        key_ref[...] = rows_of(qkv_ref[key_row:value_row, :])
    queries = stack_heads(qkv_ref, 0, first, heads) * jnp.bfloat16(0.125)
    lanes = heads * QB

    def step(block, carry, masked):
        highest, denominator, mixed = carry
        start = pl.multiple_of(block * KB, KB)
        scores = jnp.dot(key_ref[pl.ds(start, KB), :], queries, preferred_element_type=jnp.float32)
        if masked:
            key_at = lax.broadcasted_iota(jnp.int32, (KB, QB), 0)
            query_at = lax.broadcasted_iota(jnp.int32, (KB, QB), 1)
            seen = jnp.concatenate([key_at <= query_at] * heads, axis=1)
            scores = jnp.where(seen, scores, -1e30)
        raised_to = jnp.maximum(highest, jnp.max(scores, axis=0, keepdims=True))
        shrink = jnp.exp(highest - raised_to)
        raised = jnp.exp(scores - raised_to)
        denominator = denominator * shrink + jnp.sum(raised, axis=0, keepdims=True)
        mixed = mixed * shrink + jnp.dot(
            qkv_ref[value_row : value_row + HEAD_SIZE, pl.ds(start, KB)], raised.astype(jnp.bfloat16),
            preferred_element_type=jnp.float32)
        return raised_to, denominator, mixed

    carry = (jnp.full((1, lanes), -1e30, jnp.float32), jnp.zeros((1, lanes), jnp.float32), jnp.zeros((HEAD_SIZE, lanes), jnp.float32))
    carry = lax.fori_loop(0, index, lambda b, c: step(b, c, False), carry)
    highest, denominator, mixed = step(index, carry, True)
    mixed = (mixed / denominator).astype(jnp.bfloat16)
    for h in range(heads):
        out_ref[h * HEAD_SIZE : (h + 1) * HEAD_SIZE, :] = mixed[:, h * QB : (h + 1) * QB]
    total_ref[0, 0] = highest + jnp.log(denominator)

def attend_forward(qkv, groups, heads):
    tokens = qkv.shape[1]
    blocks = tokens // QB
    rows = (heads + 2) * HEAD_SIZE
    flops = groups * heads * tokens * tokens * HEAD_SIZE * 2
    return pl.pallas_call(
        functools.partial(forward_kernel, heads),
        grid=(groups, blocks),
        in_specs=[pl.BlockSpec((rows, tokens), lambda g, i: (g, 0))],
        out_specs=[pl.BlockSpec((heads * HEAD_SIZE, QB), lambda g, i: (g, i)),
                   pl.BlockSpec((1, 1, 1, heads * QB), lambda g, i: (g, i, 0, 0))],
        out_shape=[jax.ShapeDtypeStruct((groups * heads * HEAD_SIZE, tokens), jnp.bfloat16),
                   jax.ShapeDtypeStruct((groups, blocks, 1, heads * QB), jnp.float32)],
        scratch_shapes=[pltpu.VMEM((tokens, HEAD_SIZE), jnp.bfloat16)],
        cost_estimate=pl.CostEstimate(flops=flops * 14, bytes_accessed=qkv.size * 4, transcendentals=0),
        compiler_params=pltpu.CompilerParams(vmem_limit_bytes=32 << 20),
    )(qkv)

def backward_kernel(heads, qkv_ref, out_ref, total_ref, grad_ref, result_ref, key_ref, value_ref, grad_key_ref, grad_value_ref):
    index = pl.program_id(1)
    first = pl.multiple_of(index * QB, QB)
    key_row = heads * HEAD_SIZE
    value_row = key_row + HEAD_SIZE
    @pl.when(index == 0)
    def _():
        key_ref[...] = rows_of(qkv_ref[key_row:value_row, :])
        value_ref[...] = rows_of(qkv_ref[value_row : value_row + HEAD_SIZE, :])
        grad_key_ref[...] = jnp.zeros_like(grad_key_ref)
        grad_value_ref[...] = jnp.zeros_like(grad_value_ref)
    queries = stack_heads(qkv_ref, 0, first, heads) * jnp.bfloat16(0.125)
    grads = stack_heads(grad_ref, 0, 0, heads)
    outs = stack_heads(out_ref, 0, 0, heads)
    centre = jnp.sum(grads.astype(jnp.float32) * outs.astype(jnp.float32), axis=0, keepdims=True)
    totals = total_ref[0, 0]
    query_rows = rows_of(queries)
    grad_rows = rows_of(grads)

    def step(block, grad_query, masked):
        start = pl.multiple_of(block * KB, KB)
        keys = key_ref[pl.ds(start, KB), :]
        scores = jnp.dot(keys, queries, preferred_element_type=jnp.float32)
        probs = jnp.exp(scores - totals)
        if masked:
            key_at = lax.broadcasted_iota(jnp.int32, (KB, QB), 0)
            query_at = lax.broadcasted_iota(jnp.int32, (KB, QB), 1)
            seen = jnp.concatenate([key_at <= query_at] * heads, axis=1)
            probs = jnp.where(seen, probs, 0.0)
        grad_probs = jnp.dot(value_ref[pl.ds(start, KB), :], grads, preferred_element_type=jnp.float32)
        grad_scores = (probs * (grad_probs - centre)).astype(jnp.bfloat16)
        grad_value_ref[pl.ds(start, KB), :] += jnp.dot(probs.astype(jnp.bfloat16), grad_rows, preferred_element_type=jnp.float32)
        grad_key_ref[pl.ds(start, KB), :] += jnp.dot(grad_scores, query_rows, preferred_element_type=jnp.float32)
        return grad_query + jnp.dot(qkv_ref[key_row:value_row, pl.ds(start, KB)], grad_scores, preferred_element_type=jnp.float32)

    grad_query = lax.fori_loop(0, index, lambda b, c: step(b, c, False), jnp.zeros((HEAD_SIZE, heads * QB), jnp.float32))
    grad_query = (step(index, grad_query, True) * 0.125).astype(jnp.bfloat16)
    for h in range(heads):
        result_ref[h * HEAD_SIZE : (h + 1) * HEAD_SIZE, pl.ds(first, QB)] = grad_query[:, h * QB : (h + 1) * QB]
    @pl.when(index == pl.num_programs(1) - 1)
    def _():
        result_ref[key_row:value_row, :] = grad_key_ref[...].T.astype(jnp.bfloat16)
        result_ref[value_row : value_row + HEAD_SIZE, :] = grad_value_ref[...].T.astype(jnp.bfloat16)

def attend_backward(qkv, out, totals, grad, groups, heads):
    tokens = qkv.shape[1]
    blocks = tokens // QB
    rows = (heads + 2) * HEAD_SIZE
    flops = groups * heads * tokens * tokens * HEAD_SIZE * 5
    return pl.pallas_call(
        functools.partial(backward_kernel, heads),
        grid=(groups, blocks),
        in_specs=[pl.BlockSpec((rows, tokens), lambda g, i: (g, 0)),
                  pl.BlockSpec((heads * HEAD_SIZE, QB), lambda g, i: (g, i)),
                  pl.BlockSpec((1, 1, 1, heads * QB), lambda g, i: (g, i, 0, 0)),
                  pl.BlockSpec((heads * HEAD_SIZE, QB), lambda g, i: (g, i))],
        out_specs=pl.BlockSpec((rows, tokens), lambda g, i: (g, 0)),
        out_shape=jax.ShapeDtypeStruct((groups * rows, tokens), jnp.bfloat16),
        scratch_shapes=[pltpu.VMEM((tokens, HEAD_SIZE), jnp.bfloat16), pltpu.VMEM((tokens, HEAD_SIZE), jnp.bfloat16),
                        pltpu.VMEM((tokens, HEAD_SIZE), jnp.float32), pltpu.VMEM((tokens, HEAD_SIZE), jnp.float32)],
        cost_estimate=pl.CostEstimate(flops=flops * 7, bytes_accessed=qkv.size * 8, transcendentals=0),
        compiler_params=pltpu.CompilerParams(vmem_limit_bytes=40 << 20),
    )(qkv, out, totals, grad)


def arrange(experts_of):
    tokens = experts_of.shape[0]
    assigned = tokens * TOPK
    flat_ids = experts_of.reshape(assigned)
    one_hot = (flat_ids[:, None] == jnp.arange(E, dtype=jnp.int32)[None, :]).astype(jnp.int32)
    counts = jnp.sum(one_hot, axis=0, dtype=jnp.int32)
    blocks = jnp.maximum((counts + BLOCK - 1) // BLOCK, 1)
    block_ends = jnp.cumsum(blocks, dtype=jnp.int32)
    starts = (block_ends - blocks) * BLOCK
    before = jnp.cumsum(one_hot, axis=0, dtype=jnp.int32) - one_hot
    slot_of = jnp.sum((before + starts[None, :]) * one_hot, axis=1, dtype=jnp.int32)
    slots = assigned + E * BLOCK
    slot_token = (
        jnp.full((slots,), tokens, jnp.int32)
        .at[slot_of]
        .set(jnp.arange(assigned, dtype=jnp.int32) // TOPK)
    )
    firsts = jnp.arange(slots // BLOCK, dtype=jnp.int32)
    later = (firsts[:, None] >= block_ends[None, :]).astype(jnp.int32)
    block_expert = jnp.minimum(jnp.sum(later, axis=1, dtype=jnp.int32), E - 1)
    return slot_token, block_expert, block_ends


def row_at(index):
    return pl.ds(index * PITCH, PITCH)


def dispatch_kernel(blocks, gated, token_ref, expert_ref, live_ref, me_ref, *refs):
    sources, refs = refs[:blocks], refs[blocks:]
    if gated:
        gain_ref, router_ref, route_ref, out_ref, gate_ref, held, moved = refs
    else:
        out_ref, held, moved = refs
    step = pl.program_id(0)
    rows, width = sources[0].shape
    tokens = rows * blocks
    parts = width // LANES
    lanes = lax.broadcasted_iota(jnp.int32, (BLOCK, LANES), 1)

    def hold(number, source_ref):
        def part_of(piece, carry):
            start = pl.multiple_of(piece * BLOCK, BLOCK)
            first = pl.multiple_of((me_ref[0] ^ number) * rows + start, BLOCK)
            value = source_ref[pl.ds(start, BLOCK), :].astype(F32)
            if gated:
                scale = lax.rsqrt(jnp.mean(value * value, axis=1, keepdims=True) + EPSILON)
                low = (value * scale * gain_ref[...]).astype(BF16)
                logits = jnp.dot(low, router_ref[...], preferred_element_type=F32)
                routes = route_ref[pl.ds(first, BLOCK), :]
                picks = [lanes == routes[:, slot : slot + 1] for slot in range(TOPK)]
                chosen = [
                    jnp.sum(jnp.where(pick, logits, 0.0), axis=1, keepdims=True) for pick in picks
                ]
                highest = jnp.maximum(chosen[0], chosen[1])
                raised = [jnp.exp(value - highest) for value in chosen]
                total = raised[0] + raised[1]
                held[pl.ds(first * PITCH + parts, BLOCK, stride=PITCH), :] = jnp.where(
                    picks[0],
                    raised[0] / total,
                    jnp.where(picks[1], raised[1] / total, 0.0),
                )
                value = low.astype(F32)
            for part in range(parts):
                held[pl.ds(first * PITCH + part, BLOCK, stride=PITCH), :] = value[
                    :, part * LANES : (part + 1) * LANES
                ]
            return carry

        lax.fori_loop(0, rows // BLOCK, part_of, 0)

    @pl.when(step == 0)
    def _():
        held[tokens * PITCH : (tokens + 1) * PITCH, :] = jnp.zeros((PITCH, LANES), F32)
        for number, source_ref in enumerate(sources):
            hold(number, source_ref)

    @pl.when(step < live_ref[0])
    def _():
        def move(group, carry):
            base = group * UNROLL
            for j in range(UNROLL):
                moved[row_at(base + j), :] = held[row_at(token_ref[step * BLOCK + base + j]), :]
            return carry

        lax.fori_loop(0, BLOCK // UNROLL, move, 0)
        for part in range(parts):
            out_ref[:, part * LANES : (part + 1) * LANES] = moved[
                pl.ds(part, BLOCK, stride=PITCH), :
            ].astype(BF16)
        if gated:
            spare = moved[pl.ds(parts, BLOCK, stride=PITCH), :]
            own = jnp.where(lanes == expert_ref[step], spare, 0.0)
            gate_ref[...] = jnp.sum(own, axis=1, keepdims=True)


def dispatch(sources, extras, slot_token, block_expert, live):
    rows, width = sources[0].shape
    tokens = rows * len(sources)
    slots = slot_token.shape[0]
    gated = bool(extras)
    at = lambda i, t, e, n, m: (jnp.minimum(i, n[0] - 1), 0)

    def whole(value):
        return pl.BlockSpec(
            value.shape, lambda i, t, e, n, m: (0, 0), pipeline_mode=pl.Buffered(1)
        )

    out_specs = [pl.BlockSpec((BLOCK, width), at), pl.BlockSpec((BLOCK, 1), at)]
    out_shape = [
        jax.ShapeDtypeStruct((slots, width), BF16),
        jax.ShapeDtypeStruct((slots, 1), F32),
    ]
    me = lax.axis_index("narrow").astype(jnp.int32)[None]
    if len(sources) == 1:
        me = jnp.zeros((1,), jnp.int32)
    return pl.pallas_call(
        functools.partial(dispatch_kernel, len(sources), gated),
        grid_spec=pltpu.PrefetchScalarGridSpec(
            num_scalar_prefetch=4,
            grid=(slots // BLOCK,),
            in_specs=[whole(value) for value in (*sources, *extras)],
            out_specs=out_specs if gated else out_specs[:1],
            scratch_shapes=[
                pltpu.VMEM(((tokens + 1) * PITCH, LANES), F32),
                pltpu.VMEM((BLOCK * PITCH, LANES), F32),
            ],
        ),
        out_shape=out_shape if gated else out_shape[:1],
        cost_estimate=pl.CostEstimate(
            flops=42 * 10**9, bytes_accessed=24 * BLOCK * width * 2, transcendentals=0
        ),
        compiler_params=pltpu.CompilerParams(vmem_limit_bytes=48 << 20),
    )(slot_token, block_expert, live, me, *sources, *extras)


def expert_kernel(
    shards,
    span_ref,
    expert_ref,
    token_ref,
    row_ref,
    cot_ref,
    gate_ref,
    weight_ref,
    out_ref,
    back_ref,
    score_ref,
    *refs,
):
    *grad_refs, gate_sum, up_sum, down_sum, out_sum, back_sum, moved, staging, sems = refs
    step = pl.program_id(0)
    total = span_ref[1]
    block = span_ref[0] + jnp.minimum(step, total - 1)
    expert = expert_ref[block]
    width = row_ref.shape[1]
    parts = width // LANES
    tokens = out_sum.shape[0] // PITCH - 1
    following = expert_ref[jnp.minimum(block + 1, expert_ref.shape[0] - 1)]
    closing = jnp.logical_or(step == total - 1, following != expert)

    @pl.when(step == 0)
    def _():
        for ref in (out_sum, back_sum, moved, gate_sum, up_sum, down_sum):
            ref[...] = jnp.zeros_like(ref)

    @pl.when(step < total)
    def _():
        rows = row_ref[...]
        cots = cot_ref[...]
        gates = gate_ref[...]
        gate_weight = weight_ref[0, 0]
        up_weight = weight_ref[1, 0]
        down_weight = weight_ref[2, 0]
        gate_val = jnp.dot(rows, gate_weight, preferred_element_type=F32)
        up_val = jnp.dot(rows, up_weight, preferred_element_type=F32)
        raw_grad = jnp.dot(cots, down_weight, preferred_element_type=F32)
        sigma = jax.nn.sigmoid(gate_val)
        silu_val = gate_val * sigma
        active = (silu_val * up_val).astype(BF16).astype(F32)
        scores = jnp.sum(active * raw_grad, axis=1, keepdims=True)
        act_grad = raw_grad * gates
        gate_d = (act_grad * up_val * sigma * (1.0 + gate_val * (1.0 - sigma))).astype(BF16)
        up_d = (act_grad * silu_val).astype(BF16)
        weighted = (active * gates).astype(BF16)
        over_rows = (((0,), (0,)), ((), ()))
        over_hidden = (((1,), (1,)), ((), ()))
        gate_sum[...] += lax.dot_general(gate_d, rows, over_rows, preferred_element_type=F32)
        up_sum[...] += lax.dot_general(up_d, rows, over_rows, preferred_element_type=F32)
        down_sum[...] += lax.dot_general(weighted, cots, over_rows, preferred_element_type=F32)

        def spread(value):
            for part in range(parts):
                moved[pl.ds(part, BLOCK, stride=PITCH), :] = value[:, part * LANES : (part + 1) * LANES]

        def combine(sum_ref):
            def add(group, carry):
                base = group * UNROLL
                at = [row_at(token_ref[block * BLOCK + base + j]) for j in range(UNROLL)]
                new = [sum_ref[at[j], :] + moved[row_at(base + j), :] for j in range(UNROLL)]
                for j in range(UNROLL):
                    sum_ref[at[j], :] = new[j]
                return carry

            lax.fori_loop(0, BLOCK // UNROLL, add, 0)

        spread(lax.dot_general(weighted, down_weight, over_hidden, preferred_element_type=F32))
        combine(out_sum)
        spread(
            lax.dot_general(gate_d, gate_weight, over_hidden, preferred_element_type=F32)
            + lax.dot_general(up_d, up_weight, over_hidden, preferred_element_type=F32)
        )
        lanes = lax.broadcasted_iota(jnp.int32, (BLOCK, LANES), 1)
        moved[pl.ds(parts, BLOCK, stride=PITCH), :] = jnp.where(lanes == expert, scores, 0.0)
        combine(back_sum)

        @pl.when(closing)
        def _():
            rows_each = width // shards
            for index, ref in enumerate((gate_sum, up_sum, down_sum)):
                grad = ref[...].T.astype(BF16)
                ref[...] = jnp.zeros_like(ref)
                if len(grad_refs) == 1:
                    grad_refs[0][index, 0] = grad
                    continue
                keep_ref, send_ref = grad_refs
                for core in range(2):

                    @pl.when(span_ref[3] == core)
                    def _():
                        for shard in range(shards):
                            target = keep_ref if shard % 2 == core else send_ref
                            first = shard // 2 * rows_each
                            target[index, 0, first : first + rows_each, :] = grad[
                                shard * rows_each : (shard + 1) * rows_each
                            ]

    @pl.when(step == total - 1)
    def _():
        for first in range(0, tokens, BLOCK):
            score_ref[first : first + BLOCK, :] = back_sum[
                pl.ds(first * PITCH + parts, BLOCK, stride=PITCH), :
            ]

        jobs = [
            (first, source, target)
            for first in range(0, tokens, BLOCK)
            for source, target in ((out_sum, out_ref), (back_sum, back_ref))
        ]

        def copy(number):
            first, _, target = jobs[number]
            slot = number % 2
            return pltpu.make_async_copy(
                staging.at[slot], target.at[pl.ds(first, BLOCK), :], sems.at[slot]
            )

        for number, (first, source, _) in enumerate(jobs):
            if number >= 2:
                copy(number - 2).wait()
            for part in range(parts):
                staging[number % 2, :, part * LANES : (part + 1) * LANES] = source[
                    pl.ds(first * PITCH + part, BLOCK, stride=PITCH), :
                ].astype(BF16)
            copy(number).start()
        copy(len(jobs) - 2).wait()
        copy(len(jobs) - 1).wait()


def run_experts(span, slot_token, block_expert, rows, cots, gates, weights, tokens, shards, halved):
    width = rows.shape[1]
    experts, hidden = weights.shape[1], weights.shape[3]
    index = lambda i, s: s[0] + jnp.minimum(i, s[1] - 1)
    at = lambda i, s, e, t: (index(i, s), 0)
    pick = pl.BlockSpec(
        (3, 1, width, hidden), lambda i, s, e, t: (0, e[index(i, s)] - s[2], 0, 0)
    )
    half = pl.BlockSpec(
        (3, 1, width // 2, hidden), lambda i, s, e, t: (0, e[index(i, s)] - s[2], 0, 0)
    )
    anywhere = pl.BlockSpec(memory_space=pl.ANY)
    block_count = experts * 3 // 2
    return pl.pallas_call(
        functools.partial(expert_kernel, shards),
        grid_spec=pltpu.PrefetchScalarGridSpec(
            num_scalar_prefetch=3,
            grid=(tokens * TOPK // BLOCK + experts,),
            in_specs=[
                pl.BlockSpec((BLOCK, width), at),
                pl.BlockSpec((BLOCK, width), at),
                pl.BlockSpec((BLOCK, 1), at),
                pick,
            ],
            out_specs=[
                anywhere,
                anywhere,
                pl.BlockSpec((tokens, LANES), lambda i, s, e, t: (0, 0)),
            ]
            + ([half, half] if halved else [pick]),
            scratch_shapes=[pltpu.VMEM((hidden, width), F32)] * 3
            + [pltpu.VMEM(((tokens + 1) * PITCH, LANES), F32)] * 2
            + [
                pltpu.VMEM((BLOCK * PITCH, LANES), F32),
                pltpu.VMEM((2, BLOCK, width), BF16),
                pltpu.SemaphoreType.DMA((2,)),
            ],
        ),
        out_shape=[
            jax.ShapeDtypeStruct((tokens, width), BF16),
            jax.ShapeDtypeStruct((tokens, width), BF16),
            jax.ShapeDtypeStruct((tokens, LANES), F32),
        ]
        + (
            [jax.ShapeDtypeStruct((3, experts, width // 2, hidden), BF16)] * 2
            if halved
            else [jax.ShapeDtypeStruct(weights.shape, BF16)]
        ),
        cost_estimate=pl.CostEstimate(
            flops=block_count * 2 * BLOCK * width * hidden * 9 * 6,
            bytes_accessed=weights.size * 4 + block_count * BLOCK * width * 4,
            transcendentals=0,
        ),
        compiler_params=pltpu.CompilerParams(vmem_limit_bytes=62 << 20),
    )(span, block_expert, slot_token, rows, cots, gates, weights)


def swap(value, bit):
    count = lax.axis_size("narrow")
    return lax.ppermute(value, "narrow", [(index, index ^ bit) for index in range(count)])


def ordered(pieces, axis):
    me = lax.axis_index("narrow")
    count = len(pieces)
    return jnp.concatenate(
        [lax.select_n(me ^ index, *pieces) for index in range(count)], axis=axis
    )


def gather_blocks(value):
    half = value.shape[0] // 2
    one = swap(value, 1)
    two = swap(value, 2)
    before = yield
    low, high = (two[:half], one[half:]) if before is None else after((two[:half], one[half:]), before)
    far = jnp.concatenate([swap(low, 1), swap(high, 2)], axis=0)
    yield [value, one, two, far]


def gather_start(value, axis=0):
    if lax.axis_size("narrow") != 4:
        return [lax.all_gather(value, "narrow", axis=axis, tiled=True)]
    rounds = gather_blocks(value)
    next(rounds)
    return rounds


def gather_end(rounds, before=None):
    return rounds if isinstance(rounds, list) else rounds.send(before)


def gather_rows_end(rounds, before=None):
    blocks = gather_end(rounds, before)
    return ordered(blocks, 0) if len(blocks) > 1 else blocks[0]


def gather_rows(value):
    return gather_rows_end(gather_start(value))


def sum_rows(parts, turned):
    return sum_rows_end(sum_rows_start(parts, turned))


def sum_rows_end(rounds, before=None):
    return rounds if isinstance(rounds, jax.Array) else rounds[1](rounds[0], before)


def sum_rows_start(parts, turned):
    count = lax.axis_size("narrow")
    if count != 4:
        low = sum(part.astype(F32) for part in parts).astype(BF16)
        return lax.psum_scatter(low, "narrow", scatter_dimension=0, tiled=True).astype(F32)
    me = lax.axis_index("narrow")
    rows = parts[0].shape[0] // count
    half = rows // 2

    def block(other, offset):
        if turned:
            first = other * rows + offset
            pieces = [lax.slice_in_dim(part, first, first + half) for part in parts]
        else:
            first = (me ^ other) * rows + offset
            pieces = [lax.dynamic_slice_in_dim(part, first, half, 0) for part in parts]
        return sum(piece.astype(F32) for piece in pieces)

    def send(low_blocks, low_bit, high_blocks, high_bit):
        both = [
            jnp.concatenate([piece.astype(BF16) for piece in blocks], axis=0)
            for blocks in (low_blocks, high_blocks)
        ]
        low_send, high_send = lax.optimization_barrier(both)
        return swap(low_send, low_bit).astype(F32), swap(high_send, high_bit).astype(F32)

    def finish(came, before):
        low, high = came if before is None else after(came, before)
        low_far, high_far = send(
            [block(2, 0) + low[half:]], 2, [block(1, half) + high[half:]], 1
        )
        return jnp.concatenate(
            [block(0, 0) + low[:half] + low_far, block(0, half) + high[:half] + high_far], axis=0
        )

    first = send([block(1, 0), block(3, 0)], 1, [block(2, half), block(3, half)], 2)
    return first, finish


def to_rows(value):
    count = lax.axis_size("narrow")
    if count != 4:
        return [lax.all_to_all(value, "narrow", split_axis=1, concat_axis=0, tiled=True)]
    me = lax.axis_index("narrow")
    size = value.shape[1] // count
    pieces = [
        lax.dynamic_slice_in_dim(value, (me ^ step) * size, size, 1) for step in range(count)
    ]
    return [swap(piece, step) if step else piece for step, piece in enumerate(pieces)]


def product_sum(equation, lefts, rights):
    return sum(
        jnp.einsum(equation, left, right, preferred_element_type=F32)
        for left, right in zip(lefts, rights)
    )


def to_heads(value):
    if len(value) == 1:
        return lax.all_to_all(value[0], "narrow", split_axis=0, concat_axis=1, tiled=True)
    pieces = value
    return ordered([swap(piece, step) if step else piece for step, piece in enumerate(pieces)], 1)


def gather_columns(value):
    count = lax.axis_size("narrow")
    return ordered([value] + [swap(value, step) for step in range(1, count)], 1)


def sum_columns(part):
    count = lax.axis_size("narrow")
    me = lax.axis_index("narrow")
    columns = part.shape[1] // count
    result = lax.dynamic_slice_in_dim(part, me * columns, columns, 1)
    for step in range(1, count):
        piece = lax.dynamic_slice_in_dim(part, (me ^ step) * columns, columns, 1)
        result = result + swap(piece, step)
    return result


def sum_all(value):
    for axis in ("wide", "narrow"):
        count = lax.axis_size(axis)
        bit = 1
        while bit < count:
            value = value + lax.ppermute(value, axis, [(index, index ^ bit) for index in range(count)])
            bit *= 2
    return value


def after(value, *others):
    return lax.optimization_barrier((value,) + others)[0]


def local(
    block_input,
    routes,
    first_gain,
    query_key_value_weight,
    output_weight,
    second_gain,
    router_weight,
    gate_weight,
    up_weight,
    down_weight,
    cotangent,
):
    row_part, width = block_input.shape
    me = lax.axis_index("narrow")
    row_offset = me * row_part
    gain_part = first_gain.shape[0]
    tokens = routes.shape[0]
    heads = QUERY_HEADS // KEY_VALUE_HEADS
    head_columns = query_key_value_weight.shape[1]
    groups = head_columns // ((heads + 2) * HEAD_SIZE)

    def own_rows(value):
        return lax.dynamic_slice_in_dim(value, row_offset, row_part, 0)

    inputs = gather_rows(block_input)
    gains = gather_columns(jnp.stack([first_gain, second_gain])).astype(F32)
    gain_one, gain_two = gains[0], gains[1]
    packed = lax.all_gather(
        jnp.concatenate(
            [
                query_key_value_weight,
                jnp.pad(router_weight, ((0, 0), (0, LANES - E))),
                output_weight.T,
            ],
            axis=1,
        ),
        "wide",
        axis=0,
        tiled=True,
    )
    input_full = packed[:, :head_columns]
    router_padded = packed[:, head_columns : head_columns + LANES]
    router_full = router_padded[:, :E]
    output_part = packed[:, head_columns + LANES :]
    lows = [sum(CHUNKS[:index]) for index in range(len(CHUNKS))]
    chunk_weights = []
    for low, size in zip(lows, CHUNKS):
        packed = jnp.stack([w[low : low + size] for w in (gate_weight, up_weight, down_weight)])
        chunk_weights.append(lax.all_gather(packed, "wide", axis=2, tiled=True))
    slot_token, block_expert, block_ends = arrange(routes)

    x_full = inputs.astype(F32)
    scale_one = lax.rsqrt(jnp.mean(x_full * x_full, axis=1, keepdims=True) + EPSILON)
    attn_in = (x_full * scale_one * gain_one).astype(BF16)
    projected = jnp.einsum(
        "td,dc->ct", attn_in, input_full, preferred_element_type=F32
    ).astype(BF16)
    output_rounds = gather_start(after(output_part, projected), 1)
    cot_rounds = gather_start(after(cotangent, projected))
    mixed, log_totals = attend_forward(projected, groups, heads)
    mixed_own = to_rows(mixed)
    output_blocks = gather_end(output_rounds, mixed)
    middle_own = block_input.astype(F32) + product_sum("ct,dc->td", mixed_own, output_blocks)
    middle_low = middle_own.astype(BF16)
    cot_blocks = gather_end(cot_rounds, middle_low)
    live = block_ends[E - 1 :]
    (cot_rows,) = dispatch(cot_blocks, (), slot_token, block_expert, live)
    middle_blocks = gather_end(gather_start(middle_low))
    rows, slot_gates = dispatch(
        middle_blocks, (gain_two[None], router_padded, routes), slot_token, block_expert, live
    )

    shards = lax.axis_size("wide")
    core = lax.rem(lax.axis_index("wide"), 2).astype(jnp.int32)[None]
    mates = [(index, index ^ 1) for index in range(shards)]
    parities = [list(range(parity, shards, 2)) for parity in range(2)]
    outs, backs, scores, kept = [], [], [], []
    for low, size, weights in zip(lows, CHUNKS, chunk_weights):
        first = block_ends[low - 1 : low] if low else jnp.zeros((1,), jnp.int32)
        count = block_ends[low + size - 1 : low + size] - first
        halved = len(outs) == len(CHUNKS) - 1
        if outs:
            first = after(first, scores[-1])
        out, back, score, *halves = run_experts(
            jnp.concatenate([first, count, jnp.full((1,), low, jnp.int32), core]),
            slot_token, block_expert, rows, cot_rows, slot_gates, weights, tokens, shards, halved
        )
        outs.append(out)
        backs.append(back)
        scores.append(score)
        kept.append(halves)

    def sum_cores(keep, send):
        return (keep.astype(F32) + lax.ppermute(send, "wide", mates).astype(F32)).astype(BF16)

    def sum_chips(value):
        return lax.psum_scatter(
            value, "wide", scatter_dimension=2, tiled=True, axis_index_groups=parities
        )

    grads = [
        lax.psum_scatter(grad, "wide", scatter_dimension=2, tiled=True) for (grad,) in kept[:-1]
    ]

    def total(values):
        return sum(value.astype(F32) for value in values)

    expert_sum = sum_rows(backs, False)
    picked = (routes[:, :, None] == jnp.arange(E, dtype=jnp.int32)[None, None, :]).astype(F32)
    score_part = jnp.sum(picked * total(scores)[:, None, :E], axis=2)
    score_sum = sum_columns(score_part.T).T

    middle_back = after(middle_low, rows).astype(F32)
    scale_two_own = lax.rsqrt(jnp.mean(middle_back * middle_back, axis=1, keepdims=True) + EPSILON)
    normed_two_own = middle_back * scale_two_own
    expert_in_own = (normed_two_own * gain_two).astype(BF16)
    picked_own = own_rows(picked)
    logits_own = jnp.dot(expert_in_own, router_full, preferred_element_type=F32)
    gates_own = jax.nn.softmax(jnp.sum(picked_own * logits_own[:, None, :], axis=2), axis=1)
    centre = jnp.sum(gates_own * score_sum, axis=1, keepdims=True)
    logit_part = gates_own * (score_sum - centre)
    logit_grad = jnp.sum(picked_own * logit_part[:, :, None], axis=1).astype(BF16)
    norm_grad = expert_sum + jnp.einsum(
        "te,de->td", logit_grad, router_full, preferred_element_type=F32
    )
    row_dot = jnp.sum(norm_grad * normed_two_own * gain_two, axis=1, keepdims=True)
    gain_two_part = jnp.sum(norm_grad * normed_two_own, axis=0)
    mid_grad = cotangent.astype(F32) + scale_two_own * (
        gain_two * norm_grad - normed_two_own * row_dot / width
    )
    branch_grad = mid_grad.astype(BF16)
    mixed_grad_own = [
        jnp.einsum("td,dc->ct", branch_grad, block, preferred_element_type=F32).astype(BF16)
        for block in output_blocks
    ]
    third = sum_cores(*after(kept[-1], branch_grad))
    grads.append(sum_chips(third))
    mixed_grad = after(to_heads(mixed_grad_own), third)
    projected_grad = attend_backward(projected, mixed, log_totals, mixed_grad, groups, heads)
    grad_input_w = jnp.einsum(
        "td,ct->dc", attn_in, projected_grad, preferred_element_type=F32
    ).astype(BF16)
    block_rounds = sum_rows_start(after(outs, mixed_grad), False)
    came = block_rounds if isinstance(block_rounds, jax.Array) else block_rounds[0]
    input_part = jnp.einsum(
        "ct,dc->td", after(projected_grad, grads[0], came), input_full, preferred_element_type=F32
    ).astype(BF16)
    input_sum = sum_rows_end(sum_rows_start([input_part], False), grads[1])
    grad_output_w = sum_rows(
        [
            jnp.concatenate(
                [
                    jnp.einsum("ct,td->cd", block, branch_grad, preferred_element_type=F32).astype(
                        BF16
                    )
                    for block in after(mixed_own, input_sum)
                ],
                axis=0,
            )
        ],
        True,
    ).astype(BF16)
    block_output = (middle_own + sum_rows_end(block_rounds, input_sum)).astype(BF16)
    grad_router = jnp.einsum(
        "te,td->ed", logit_grad, expert_in_own, preferred_element_type=F32
    )
    x_own = after(block_input, projected_grad).astype(F32)
    scale_one_own = lax.rsqrt(jnp.mean(x_own * x_own, axis=1, keepdims=True) + EPSILON)
    normed_one_own = x_own * scale_one_own
    gain_one_part = jnp.sum(input_sum * normed_one_own, axis=0)
    small_sum = sum_all(
        after(
            jnp.concatenate([grad_router, gain_one_part[None], gain_two_part[None]], axis=0),
            grads[2],
        )
    )
    gain_own = lax.dynamic_slice_in_dim(small_sum[E:], me * gain_part, gain_part, 1)
    router_part = router_weight.shape[0]
    router_grad = lax.dynamic_slice_in_dim(
        small_sum[:E], lax.axis_index("wide") * router_part, router_part, 1
    ).T
    input_dot = jnp.sum(input_sum * normed_one_own * gain_one, axis=1, keepdims=True)
    input_grad = mid_grad + scale_one_own * (
        gain_one * input_sum - normed_one_own * input_dot / width
    )
    packed_grad = lax.psum_scatter(
        after(
            jnp.concatenate([grad_input_w, grad_output_w.T], axis=1), input_grad
        ),
        "wide",
        scatter_dimension=0,
        tiled=True,
    ).astype(F32)
    input_w_grad = packed_grad[:, :head_columns]
    output_w_grad = packed_grad[:, head_columns:].T
    grads = after(grads, block_output, small_sum, grad_output_w, input_grad)
    gate_grad, up_grad, down_grad = (
        jnp.concatenate([grad[index] for grad in grads], axis=0).astype(F32) for index in range(3)
    )
    return (
        block_output,
        input_grad,
        gain_own[0],
        input_w_grad,
        output_w_grad,
        gain_own[1],
        router_grad,
        gate_grad,
        up_grad,
        down_grad,
    )


def solution(mesh):
    placed = (
        P(("wide", "narrow"), None),
        P("wide", None),
        P("narrow"),
        P("wide", "narrow"),
        P("narrow", "wide"),
        P("narrow"),
        P("wide", None),
        P(None, "wide", "narrow"),
        P(None, "wide", "narrow"),
        P(None, "wide", "narrow"),
        P(("wide", "narrow"), None),
    )
    return jax.shard_map(
        local,
        mesh=mesh,
        in_specs=placed,
        out_specs=(
            P(("wide", "narrow"), None),
            P(("wide", "narrow"), None),
            P("narrow"),
            P("wide", "narrow"),
            P("narrow", "wide"),
            P("narrow"),
            P("wide", None),
            P(None, "wide", "narrow"),
            P(None, "wide", "narrow"),
            P(None, "wide", "narrow"),
        ),
        check_vma=False,
    )
```

```python
import functools

import jax
import jax.numpy as jnp
from jax import lax
from jax.experimental import pallas as pl
from jax.experimental.pallas import tpu as pltpu
from jax.sharding import PartitionSpec as P

QUERY_HEADS = 24
KEY_VALUE_HEADS = 8
HEAD_SIZE = 64
E = 16
TOPK = 2
SEQUENCE_LENGTH = 2048
BLOCK = 256
QB = 512
KB = 512
LANES = 128
PITCH = 13
UNROLL = 8
CHUNKS = (4, 6, 6)
EPSILON = 1e-05
F32 = jnp.float32
BF16 = jnp.bfloat16

def stack_heads(ref, row, first, heads):
    return jnp.concatenate(
        [ref[row + h * HEAD_SIZE : row + (h + 1) * HEAD_SIZE, pl.ds(first, QB)] for h in range(heads)], axis=1
    )

def rows_of(block):
    return block.astype(jnp.float32).T.astype(jnp.bfloat16)

def forward_kernel(heads, qkv_ref, out_ref, total_ref, key_ref):
    index = pl.program_id(1)
    first = pl.multiple_of(index * QB, QB)
    key_row = heads * HEAD_SIZE
    value_row = key_row + HEAD_SIZE
    @pl.when(index == 0)
    def _():
        key_ref[...] = rows_of(qkv_ref[key_row:value_row, :])
    queries = stack_heads(qkv_ref, 0, first, heads) * jnp.bfloat16(0.125)
    lanes = heads * QB

    def step(block, carry, masked):
        highest, denominator, mixed = carry
        start = pl.multiple_of(block * KB, KB)
        scores = jnp.dot(key_ref[pl.ds(start, KB), :], queries, preferred_element_type=jnp.float32)
        if masked:
            key_at = lax.broadcasted_iota(jnp.int32, (KB, QB), 0)
            query_at = lax.broadcasted_iota(jnp.int32, (KB, QB), 1)
            seen = jnp.concatenate([key_at <= query_at] * heads, axis=1)
            scores = jnp.where(seen, scores, -1e30)
        raised_to = jnp.maximum(highest, jnp.max(scores, axis=0, keepdims=True))
        shrink = jnp.exp(highest - raised_to)
        raised = jnp.exp(scores - raised_to)
        denominator = denominator * shrink + jnp.sum(raised, axis=0, keepdims=True)
        mixed = mixed * shrink + jnp.dot(
            qkv_ref[value_row : value_row + HEAD_SIZE, pl.ds(start, KB)], raised.astype(jnp.bfloat16),
            preferred_element_type=jnp.float32)
        return raised_to, denominator, mixed

    carry = (jnp.full((1, lanes), -1e30, jnp.float32), jnp.zeros((1, lanes), jnp.float32), jnp.zeros((HEAD_SIZE, lanes), jnp.float32))
    carry = lax.fori_loop(0, index, lambda b, c: step(b, c, False), carry)
    highest, denominator, mixed = step(index, carry, True)
    mixed = (mixed / denominator).astype(jnp.bfloat16)
    for h in range(heads):
        out_ref[h * HEAD_SIZE : (h + 1) * HEAD_SIZE, :] = mixed[:, h * QB : (h + 1) * QB]
    total_ref[0, 0] = highest + jnp.log(denominator)

def attend_forward(qkv, groups, heads):
    tokens = qkv.shape[1]
    blocks = tokens // QB
    rows = (heads + 2) * HEAD_SIZE
    flops = groups * heads * tokens * tokens * HEAD_SIZE * 2
    return pl.pallas_call(
        functools.partial(forward_kernel, heads),
        grid=(groups, blocks),
        in_specs=[pl.BlockSpec((rows, tokens), lambda g, i: (g, 0))],
        out_specs=[pl.BlockSpec((heads * HEAD_SIZE, QB), lambda g, i: (g, i)),
                   pl.BlockSpec((1, 1, 1, heads * QB), lambda g, i: (g, i, 0, 0))],
        out_shape=[jax.ShapeDtypeStruct((groups * heads * HEAD_SIZE, tokens), jnp.bfloat16),
                   jax.ShapeDtypeStruct((groups, blocks, 1, heads * QB), jnp.float32)],
        scratch_shapes=[pltpu.VMEM((tokens, HEAD_SIZE), jnp.bfloat16)],
        cost_estimate=pl.CostEstimate(flops=flops * 14, bytes_accessed=qkv.size * 4, transcendentals=0),
        compiler_params=pltpu.CompilerParams(vmem_limit_bytes=32 << 20),
    )(qkv)

def backward_kernel(heads, qkv_ref, out_ref, total_ref, grad_ref, result_ref, key_ref, value_ref, grad_key_ref, grad_value_ref):
    index = pl.program_id(1)
    first = pl.multiple_of(index * QB, QB)
    key_row = heads * HEAD_SIZE
    value_row = key_row + HEAD_SIZE
    @pl.when(index == 0)
    def _():
        key_ref[...] = rows_of(qkv_ref[key_row:value_row, :])
        value_ref[...] = rows_of(qkv_ref[value_row : value_row + HEAD_SIZE, :])
        grad_key_ref[...] = jnp.zeros_like(grad_key_ref)
        grad_value_ref[...] = jnp.zeros_like(grad_value_ref)
    queries = stack_heads(qkv_ref, 0, first, heads) * jnp.bfloat16(0.125)
    grads = stack_heads(grad_ref, 0, 0, heads)
    outs = stack_heads(out_ref, 0, 0, heads)
    centre = jnp.sum(grads.astype(jnp.float32) * outs.astype(jnp.float32), axis=0, keepdims=True)
    totals = total_ref[0, 0]
    query_rows = rows_of(queries)
    grad_rows = rows_of(grads)

    def step(block, grad_query, masked):
        start = pl.multiple_of(block * KB, KB)
        keys = key_ref[pl.ds(start, KB), :]
        scores = jnp.dot(keys, queries, preferred_element_type=jnp.float32)
        probs = jnp.exp(scores - totals)
        if masked:
            key_at = lax.broadcasted_iota(jnp.int32, (KB, QB), 0)
            query_at = lax.broadcasted_iota(jnp.int32, (KB, QB), 1)
            seen = jnp.concatenate([key_at <= query_at] * heads, axis=1)
            probs = jnp.where(seen, probs, 0.0)
        grad_probs = jnp.dot(value_ref[pl.ds(start, KB), :], grads, preferred_element_type=jnp.float32)
        grad_scores = (probs * (grad_probs - centre)).astype(jnp.bfloat16)
        grad_value_ref[pl.ds(start, KB), :] += jnp.dot(probs.astype(jnp.bfloat16), grad_rows, preferred_element_type=jnp.float32)
        grad_key_ref[pl.ds(start, KB), :] += jnp.dot(grad_scores, query_rows, preferred_element_type=jnp.float32)
        return grad_query + jnp.dot(qkv_ref[key_row:value_row, pl.ds(start, KB)], grad_scores, preferred_element_type=jnp.float32)

    grad_query = lax.fori_loop(0, index, lambda b, c: step(b, c, False), jnp.zeros((HEAD_SIZE, heads * QB), jnp.float32))
    grad_query = (step(index, grad_query, True) * 0.125).astype(jnp.bfloat16)
    for h in range(heads):
        result_ref[h * HEAD_SIZE : (h + 1) * HEAD_SIZE, pl.ds(first, QB)] = grad_query[:, h * QB : (h + 1) * QB]
    @pl.when(index == pl.num_programs(1) - 1)
    def _():
        result_ref[key_row:value_row, :] = grad_key_ref[...].T.astype(jnp.bfloat16)
        result_ref[value_row : value_row + HEAD_SIZE, :] = grad_value_ref[...].T.astype(jnp.bfloat16)

def attend_backward(qkv, out, totals, grad, groups, heads):
    tokens = qkv.shape[1]
    blocks = tokens // QB
    rows = (heads + 2) * HEAD_SIZE
    flops = groups * heads * tokens * tokens * HEAD_SIZE * 5
    return pl.pallas_call(
        functools.partial(backward_kernel, heads),
        grid=(groups, blocks),
        in_specs=[pl.BlockSpec((rows, tokens), lambda g, i: (g, 0)),
                  pl.BlockSpec((heads * HEAD_SIZE, QB), lambda g, i: (g, i)),
                  pl.BlockSpec((1, 1, 1, heads * QB), lambda g, i: (g, i, 0, 0)),
                  pl.BlockSpec((heads * HEAD_SIZE, QB), lambda g, i: (g, i))],
        out_specs=pl.BlockSpec((rows, tokens), lambda g, i: (g, 0)),
        out_shape=jax.ShapeDtypeStruct((groups * rows, tokens), jnp.bfloat16),
        scratch_shapes=[pltpu.VMEM((tokens, HEAD_SIZE), jnp.bfloat16), pltpu.VMEM((tokens, HEAD_SIZE), jnp.bfloat16),
                        pltpu.VMEM((tokens, HEAD_SIZE), jnp.float32), pltpu.VMEM((tokens, HEAD_SIZE), jnp.float32)],
        cost_estimate=pl.CostEstimate(flops=flops * 7, bytes_accessed=qkv.size * 8, transcendentals=0),
        compiler_params=pltpu.CompilerParams(vmem_limit_bytes=40 << 20),
    )(qkv, out, totals, grad)


def arrange(experts_of):
    tokens = experts_of.shape[0]
    assigned = tokens * TOPK
    flat_ids = experts_of.reshape(assigned)
    one_hot = (flat_ids[:, None] == jnp.arange(E, dtype=jnp.int32)[None, :]).astype(jnp.int32)
    counts = jnp.sum(one_hot, axis=0, dtype=jnp.int32)
    blocks = jnp.maximum((counts + BLOCK - 1) // BLOCK, 1)
    block_ends = jnp.cumsum(blocks, dtype=jnp.int32)
    starts = (block_ends - blocks) * BLOCK
    before = jnp.cumsum(one_hot, axis=0, dtype=jnp.int32) - one_hot
    slot_of = jnp.sum((before + starts[None, :]) * one_hot, axis=1, dtype=jnp.int32)
    slots = assigned + E * BLOCK
    slot_token = (
        jnp.full((slots,), tokens, jnp.int32)
        .at[slot_of]
        .set(jnp.arange(assigned, dtype=jnp.int32) // TOPK)
    )
    firsts = jnp.arange(slots // BLOCK, dtype=jnp.int32)
    later = (firsts[:, None] >= block_ends[None, :]).astype(jnp.int32)
    block_expert = jnp.minimum(jnp.sum(later, axis=1, dtype=jnp.int32), E - 1)
    return slot_token, block_expert, block_ends


def row_at(index):
    return pl.ds(index * PITCH, PITCH)


def dispatch_kernel(blocks, gated, token_ref, expert_ref, live_ref, me_ref, *refs):
    sources, refs = refs[:blocks], refs[blocks:]
    if gated:
        gain_ref, router_ref, route_ref, out_ref, gate_ref, held, moved = refs
    else:
        out_ref, held, moved = refs
    step = pl.program_id(0)
    rows, width = sources[0].shape
    tokens = rows * blocks
    parts = width // LANES
    lanes = lax.broadcasted_iota(jnp.int32, (BLOCK, LANES), 1)

    def hold(number, source_ref):
        def part_of(piece, carry):
            start = pl.multiple_of(piece * BLOCK, BLOCK)
            first = pl.multiple_of((me_ref[0] ^ number) * rows + start, BLOCK)
            value = source_ref[pl.ds(start, BLOCK), :].astype(F32)
            if gated:
                scale = lax.rsqrt(jnp.mean(value * value, axis=1, keepdims=True) + EPSILON)
                low = (value * scale * gain_ref[...]).astype(BF16)
                logits = jnp.dot(low, router_ref[...], preferred_element_type=F32)
                routes = route_ref[pl.ds(first, BLOCK), :]
                picks = [lanes == routes[:, slot : slot + 1] for slot in range(TOPK)]
                chosen = [
                    jnp.sum(jnp.where(pick, logits, 0.0), axis=1, keepdims=True) for pick in picks
                ]
                highest = jnp.maximum(chosen[0], chosen[1])
                raised = [jnp.exp(value - highest) for value in chosen]
                total = raised[0] + raised[1]
                held[pl.ds(first * PITCH + parts, BLOCK, stride=PITCH), :] = jnp.where(
                    picks[0],
                    raised[0] / total,
                    jnp.where(picks[1], raised[1] / total, 0.0),
                )
                value = low.astype(F32)
            for part in range(parts):
                held[pl.ds(first * PITCH + part, BLOCK, stride=PITCH), :] = value[
                    :, part * LANES : (part + 1) * LANES
                ]
            return carry

        lax.fori_loop(0, rows // BLOCK, part_of, 0)

    @pl.when(step == 0)
    def _():
        held[tokens * PITCH : (tokens + 1) * PITCH, :] = jnp.zeros((PITCH, LANES), F32)
        for number, source_ref in enumerate(sources):
            hold(number, source_ref)

    @pl.when(step < live_ref[0])
    def _():
        def move(group, carry):
            base = group * UNROLL
            for j in range(UNROLL):
                moved[row_at(base + j), :] = held[row_at(token_ref[step * BLOCK + base + j]), :]
            return carry

        lax.fori_loop(0, BLOCK // UNROLL, move, 0)
        for part in range(parts):
            out_ref[:, part * LANES : (part + 1) * LANES] = moved[
                pl.ds(part, BLOCK, stride=PITCH), :
            ].astype(BF16)
        if gated:
            spare = moved[pl.ds(parts, BLOCK, stride=PITCH), :]
            own = jnp.where(lanes == expert_ref[step], spare, 0.0)
            gate_ref[...] = jnp.sum(own, axis=1, keepdims=True)


def dispatch(sources, extras, slot_token, block_expert, live):
    rows, width = sources[0].shape
    tokens = rows * len(sources)
    slots = slot_token.shape[0]
    gated = bool(extras)
    at = lambda i, t, e, n, m: (jnp.minimum(i, n[0] - 1), 0)

    def whole(value):
        return pl.BlockSpec(
            value.shape, lambda i, t, e, n, m: (0, 0), pipeline_mode=pl.Buffered(1)
        )

    out_specs = [pl.BlockSpec((BLOCK, width), at), pl.BlockSpec((BLOCK, 1), at)]
    out_shape = [
        jax.ShapeDtypeStruct((slots, width), BF16),
        jax.ShapeDtypeStruct((slots, 1), F32),
    ]
    me = lax.axis_index("narrow").astype(jnp.int32)[None]
    if len(sources) == 1:
        me = jnp.zeros((1,), jnp.int32)
    return pl.pallas_call(
        functools.partial(dispatch_kernel, len(sources), gated),
        grid_spec=pltpu.PrefetchScalarGridSpec(
            num_scalar_prefetch=4,
            grid=(slots // BLOCK,),
            in_specs=[whole(value) for value in (*sources, *extras)],
            out_specs=out_specs if gated else out_specs[:1],
            scratch_shapes=[
                pltpu.VMEM(((tokens + 1) * PITCH, LANES), F32),
                pltpu.VMEM((BLOCK * PITCH, LANES), F32),
            ],
        ),
        out_shape=out_shape if gated else out_shape[:1],
        cost_estimate=pl.CostEstimate(
            flops=42 * 10**9, bytes_accessed=24 * BLOCK * width * 2, transcendentals=0
        ),
        compiler_params=pltpu.CompilerParams(vmem_limit_bytes=48 << 20),
    )(slot_token, block_expert, live, me, *sources, *extras)


def expert_kernel(
    shards,
    span_ref,
    expert_ref,
    token_ref,
    row_ref,
    cot_ref,
    gate_ref,
    weight_ref,
    out_ref,
    back_ref,
    score_ref,
    *refs,
):
    *grad_refs, gate_sum, up_sum, down_sum, out_sum, back_sum, moved, staging, sems = refs
    step = pl.program_id(0)
    total = span_ref[1]
    block = span_ref[0] + jnp.minimum(step, total - 1)
    expert = expert_ref[block]
    width = row_ref.shape[1]
    parts = width // LANES
    tokens = out_sum.shape[0] // PITCH - 1
    following = expert_ref[jnp.minimum(block + 1, expert_ref.shape[0] - 1)]
    closing = jnp.logical_or(step == total - 1, following != expert)

    @pl.when(step == 0)
    def _():
        for ref in (out_sum, back_sum, moved, gate_sum, up_sum, down_sum):
            ref[...] = jnp.zeros_like(ref)

    @pl.when(step < total)
    def _():
        rows = row_ref[...]
        cots = cot_ref[...]
        gates = gate_ref[...]
        gate_weight = weight_ref[0, 0]
        up_weight = weight_ref[1, 0]
        down_weight = weight_ref[2, 0]
        gate_val = jnp.dot(rows, gate_weight, preferred_element_type=F32)
        up_val = jnp.dot(rows, up_weight, preferred_element_type=F32)
        raw_grad = jnp.dot(cots, down_weight, preferred_element_type=F32)
        sigma = jax.nn.sigmoid(gate_val)
        silu_val = gate_val * sigma
        active = (silu_val * up_val).astype(BF16).astype(F32)
        scores = jnp.sum(active * raw_grad, axis=1, keepdims=True)
        act_grad = raw_grad * gates
        gate_d = (act_grad * up_val * sigma * (1.0 + gate_val * (1.0 - sigma))).astype(BF16)
        up_d = (act_grad * silu_val).astype(BF16)
        weighted = (active * gates).astype(BF16)
        over_rows = (((0,), (0,)), ((), ()))
        over_hidden = (((1,), (1,)), ((), ()))
        gate_sum[...] += lax.dot_general(gate_d, rows, over_rows, preferred_element_type=F32)
        up_sum[...] += lax.dot_general(up_d, rows, over_rows, preferred_element_type=F32)
        down_sum[...] += lax.dot_general(weighted, cots, over_rows, preferred_element_type=F32)

        def spread(value):
            for part in range(parts):
                moved[pl.ds(part, BLOCK, stride=PITCH), :] = value[:, part * LANES : (part + 1) * LANES]

        def combine(sum_ref):
            def add(group, carry):
                base = group * UNROLL
                at = [row_at(token_ref[block * BLOCK + base + j]) for j in range(UNROLL)]
                new = [sum_ref[at[j], :] + moved[row_at(base + j), :] for j in range(UNROLL)]
                for j in range(UNROLL):
                    sum_ref[at[j], :] = new[j]
                return carry

            lax.fori_loop(0, BLOCK // UNROLL, add, 0)

        spread(lax.dot_general(weighted, down_weight, over_hidden, preferred_element_type=F32))
        combine(out_sum)
        spread(
            lax.dot_general(gate_d, gate_weight, over_hidden, preferred_element_type=F32)
            + lax.dot_general(up_d, up_weight, over_hidden, preferred_element_type=F32)
        )
        lanes = lax.broadcasted_iota(jnp.int32, (BLOCK, LANES), 1)
        moved[pl.ds(parts, BLOCK, stride=PITCH), :] = jnp.where(lanes == expert, scores, 0.0)
        combine(back_sum)

        @pl.when(closing)
        def _():
            rows_each = width // shards
            for index, ref in enumerate((gate_sum, up_sum, down_sum)):
                grad = ref[...].T.astype(BF16)
                ref[...] = jnp.zeros_like(ref)
                if len(grad_refs) == 1:
                    grad_refs[0][index, 0] = grad
                    continue
                keep_ref, send_ref = grad_refs
                for core in range(2):

                    @pl.when(span_ref[3] == core)
                    def _():
                        for shard in range(shards):
                            target = keep_ref if shard % 2 == core else send_ref
                            first = shard // 2 * rows_each
                            target[index, 0, first : first + rows_each, :] = grad[
                                shard * rows_each : (shard + 1) * rows_each
                            ]

    @pl.when(step == total - 1)
    def _():
        for first in range(0, tokens, BLOCK):
            score_ref[first : first + BLOCK, :] = back_sum[
                pl.ds(first * PITCH + parts, BLOCK, stride=PITCH), :
            ]

        jobs = [
            (first, source, target)
            for first in range(0, tokens, BLOCK)
            for source, target in ((out_sum, out_ref), (back_sum, back_ref))
        ]

        def copy(number):
            first, _, target = jobs[number]
            slot = number % 2
            return pltpu.make_async_copy(
                staging.at[slot], target.at[pl.ds(first, BLOCK), :], sems.at[slot]
            )

        for number, (first, source, _) in enumerate(jobs):
            if number >= 2:
                copy(number - 2).wait()
            for part in range(parts):
                staging[number % 2, :, part * LANES : (part + 1) * LANES] = source[
                    pl.ds(first * PITCH + part, BLOCK, stride=PITCH), :
                ].astype(BF16)
            copy(number).start()
        copy(len(jobs) - 2).wait()
        copy(len(jobs) - 1).wait()


def run_experts(span, slot_token, block_expert, rows, cots, gates, weights, tokens, shards, halved):
    width = rows.shape[1]
    experts, hidden = weights.shape[1], weights.shape[3]
    index = lambda i, s: s[0] + jnp.minimum(i, s[1] - 1)
    at = lambda i, s, e, t: (index(i, s), 0)
    pick = pl.BlockSpec(
        (3, 1, width, hidden), lambda i, s, e, t: (0, e[index(i, s)] - s[2], 0, 0)
    )
    half = pl.BlockSpec(
        (3, 1, width // 2, hidden), lambda i, s, e, t: (0, e[index(i, s)] - s[2], 0, 0)
    )
    anywhere = pl.BlockSpec(memory_space=pl.ANY)
    block_count = experts * 3 // 2
    return pl.pallas_call(
        functools.partial(expert_kernel, shards),
        grid_spec=pltpu.PrefetchScalarGridSpec(
            num_scalar_prefetch=3,
            grid=(tokens * TOPK // BLOCK + experts,),
            in_specs=[
                pl.BlockSpec((BLOCK, width), at),
                pl.BlockSpec((BLOCK, width), at),
                pl.BlockSpec((BLOCK, 1), at),
                pick,
            ],
            out_specs=[
                anywhere,
                anywhere,
                pl.BlockSpec((tokens, LANES), lambda i, s, e, t: (0, 0)),
            ]
            + ([half, half] if halved else [pick]),
            scratch_shapes=[pltpu.VMEM((hidden, width), F32)] * 3
            + [pltpu.VMEM(((tokens + 1) * PITCH, LANES), F32)] * 2
            + [
                pltpu.VMEM((BLOCK * PITCH, LANES), F32),
                pltpu.VMEM((2, BLOCK, width), BF16),
                pltpu.SemaphoreType.DMA((2,)),
            ],
        ),
        out_shape=[
            jax.ShapeDtypeStruct((tokens, width), BF16),
            jax.ShapeDtypeStruct((tokens, width), BF16),
            jax.ShapeDtypeStruct((tokens, LANES), F32),
        ]
        + (
            [jax.ShapeDtypeStruct((3, experts, width // 2, hidden), BF16)] * 2
            if halved
            else [jax.ShapeDtypeStruct(weights.shape, BF16)]
        ),
        cost_estimate=pl.CostEstimate(
            flops=block_count * 2 * BLOCK * width * hidden * 9 * 6,
            bytes_accessed=weights.size * 4 + block_count * BLOCK * width * 4,
            transcendentals=0,
        ),
        compiler_params=pltpu.CompilerParams(vmem_limit_bytes=62 << 20),
    )(span, block_expert, slot_token, rows, cots, gates, weights)


def swap(value, bit):
    count = lax.axis_size("narrow")
    return lax.ppermute(value, "narrow", [(index, index ^ bit) for index in range(count)])


def ordered(pieces, axis):
    me = lax.axis_index("narrow")
    count = len(pieces)
    return jnp.concatenate(
        [lax.select_n(me ^ index, *pieces) for index in range(count)], axis=axis
    )


def gather_blocks(value):
    half = value.shape[0] // 2
    one = swap(value, 1)
    two = swap(value, 2)
    before = yield
    low, high = (two[:half], one[half:]) if before is None else after((two[:half], one[half:]), before)
    far = jnp.concatenate([swap(low, 1), swap(high, 2)], axis=0)
    yield [value, one, two, far]


def gather_start(value, axis=0):
    if lax.axis_size("narrow") != 4:
        return [lax.all_gather(value, "narrow", axis=axis, tiled=True)]
    rounds = gather_blocks(value)
    next(rounds)
    return rounds


def gather_end(rounds, before=None):
    return rounds if isinstance(rounds, list) else rounds.send(before)


def gather_rows_end(rounds, before=None):
    blocks = gather_end(rounds, before)
    return ordered(blocks, 0) if len(blocks) > 1 else blocks[0]


def gather_rows(value):
    return gather_rows_end(gather_start(value))


def sum_rows(parts, turned):
    return sum_rows_end(sum_rows_start(parts, turned))


def sum_rows_end(rounds, before=None):
    return rounds if isinstance(rounds, jax.Array) else rounds[1](rounds[0], before)


def sum_rows_start(parts, turned):
    count = lax.axis_size("narrow")
    if count != 4:
        low = sum(part.astype(F32) for part in parts).astype(BF16)
        return lax.psum_scatter(low, "narrow", scatter_dimension=0, tiled=True).astype(F32)
    me = lax.axis_index("narrow")
    rows = parts[0].shape[0] // count
    half = rows // 2

    def block(other, offset):
        if turned:
            first = other * rows + offset
            pieces = [lax.slice_in_dim(part, first, first + half) for part in parts]
        else:
            first = (me ^ other) * rows + offset
            pieces = [lax.dynamic_slice_in_dim(part, first, half, 0) for part in parts]
        return sum(piece.astype(F32) for piece in pieces)

    def send(low_blocks, low_bit, high_blocks, high_bit):
        both = [
            jnp.concatenate([piece.astype(BF16) for piece in blocks], axis=0)
            for blocks in (low_blocks, high_blocks)
        ]
        low_send, high_send = lax.optimization_barrier(both)
        return swap(low_send, low_bit).astype(F32), swap(high_send, high_bit).astype(F32)

    def finish(came, before):
        low, high = came if before is None else after(came, before)
        low_far, high_far = send(
            [block(2, 0) + low[half:]], 2, [block(1, half) + high[half:]], 1
        )
        return jnp.concatenate(
            [block(0, 0) + low[:half] + low_far, block(0, half) + high[:half] + high_far], axis=0
        )

    first = send([block(1, 0), block(3, 0)], 1, [block(2, half), block(3, half)], 2)
    return first, finish


def to_rows(value):
    count = lax.axis_size("narrow")
    if count != 4:
        return [lax.all_to_all(value, "narrow", split_axis=1, concat_axis=0, tiled=True)]
    me = lax.axis_index("narrow")
    size = value.shape[1] // count
    pieces = [
        lax.dynamic_slice_in_dim(value, (me ^ step) * size, size, 1) for step in range(count)
    ]
    return [swap(piece, step) if step else piece for step, piece in enumerate(pieces)]


def product_sum(equation, lefts, rights):
    return sum(
        jnp.einsum(equation, left, right, preferred_element_type=F32)
        for left, right in zip(lefts, rights)
    )


def to_heads(value):
    if len(value) == 1:
        return lax.all_to_all(value[0], "narrow", split_axis=0, concat_axis=1, tiled=True)
    pieces = value
    return ordered([swap(piece, step) if step else piece for step, piece in enumerate(pieces)], 1)


def gather_columns(value):
    count = lax.axis_size("narrow")
    return ordered([value] + [swap(value, step) for step in range(1, count)], 1)


def sum_columns(part):
    count = lax.axis_size("narrow")
    me = lax.axis_index("narrow")
    columns = part.shape[1] // count
    result = lax.dynamic_slice_in_dim(part, me * columns, columns, 1)
    for step in range(1, count):
        piece = lax.dynamic_slice_in_dim(part, (me ^ step) * columns, columns, 1)
        result = result + swap(piece, step)
    return result


def sum_along(value, axis):
    count = lax.axis_size(axis)
    bit = 1
    while bit < count:
        value = value + lax.ppermute(value, axis, [(index, index ^ bit) for index in range(count)])
        bit *= 2
    return value


def after(value, *others):
    return lax.optimization_barrier((value,) + others)[0]


def local(
    block_input,
    routes,
    first_gain,
    query_key_value_weight,
    output_weight,
    second_gain,
    router_weight,
    gate_weight,
    up_weight,
    down_weight,
    cotangent,
):
    row_part, width = block_input.shape
    me = lax.axis_index("narrow")
    row_offset = me * row_part
    gain_part = first_gain.shape[0]
    tokens = routes.shape[0]
    heads = QUERY_HEADS // KEY_VALUE_HEADS
    head_columns = query_key_value_weight.shape[1]
    groups = head_columns // ((heads + 2) * HEAD_SIZE)

    def own_rows(value):
        return lax.dynamic_slice_in_dim(value, row_offset, row_part, 0)

    inputs = gather_rows(block_input)
    gains = gather_columns(jnp.stack([first_gain, second_gain])).astype(F32)
    gain_one, gain_two = gains[0], gains[1]
    packed = lax.all_gather(
        jnp.concatenate(
            [
                query_key_value_weight,
                jnp.pad(router_weight, ((0, 0), (0, LANES - E))),
                output_weight.T,
            ],
            axis=1,
        ),
        "wide",
        axis=0,
        tiled=True,
    )
    input_full = packed[:, :head_columns]
    router_padded = packed[:, head_columns : head_columns + LANES]
    router_full = router_padded[:, :E]
    output_part = packed[:, head_columns + LANES :]
    lows = [sum(CHUNKS[:index]) for index in range(len(CHUNKS))]
    chunk_weights = []
    for low, size in zip(lows, CHUNKS):
        packed = jnp.stack([w[low : low + size] for w in (gate_weight, up_weight, down_weight)])
        chunk_weights.append(lax.all_gather(packed, "wide", axis=2, tiled=True))
    slot_token, block_expert, block_ends = arrange(routes)

    x_full = inputs.astype(F32)
    scale_one = lax.rsqrt(jnp.mean(x_full * x_full, axis=1, keepdims=True) + EPSILON)
    attn_in = (x_full * scale_one * gain_one).astype(BF16)
    projected = jnp.einsum(
        "td,dc->ct", attn_in, input_full, preferred_element_type=F32
    ).astype(BF16)
    output_rounds = gather_start(after(output_part, projected), 1)
    cot_rounds = gather_start(after(cotangent, projected))
    mixed, log_totals = attend_forward(projected, groups, heads)
    mixed_own = to_rows(mixed)
    output_blocks = gather_end(output_rounds, mixed)
    middle_own = block_input.astype(F32) + product_sum("ct,dc->td", mixed_own, output_blocks)
    middle_low = middle_own.astype(BF16)
    cot_blocks = gather_end(cot_rounds, middle_low)
    live = block_ends[E - 1 :]
    (cot_rows,) = dispatch(cot_blocks, (), slot_token, block_expert, live)
    middle_blocks = gather_end(gather_start(middle_low))
    rows, slot_gates = dispatch(
        middle_blocks, (gain_two[None], router_padded, routes), slot_token, block_expert, live
    )

    shards = lax.axis_size("wide")
    core = lax.rem(lax.axis_index("wide"), 2).astype(jnp.int32)[None]
    mates = [(index, index ^ 1) for index in range(shards)]
    parities = [list(range(parity, shards, 2)) for parity in range(2)]
    outs, backs, scores, kept = [], [], [], []
    for low, size, weights in zip(lows, CHUNKS, chunk_weights):
        first = block_ends[low - 1 : low] if low else jnp.zeros((1,), jnp.int32)
        count = block_ends[low + size - 1 : low + size] - first
        halved = len(outs) == len(CHUNKS) - 1
        if outs:
            first = after(first, scores[-1])
        out, back, score, *halves = run_experts(
            jnp.concatenate([first, count, jnp.full((1,), low, jnp.int32), core]),
            slot_token, block_expert, rows, cot_rows, slot_gates, weights, tokens, shards, halved
        )
        outs.append(out)
        backs.append(back)
        scores.append(score)
        kept.append(halves)

    def sum_cores(keep, send):
        return (keep.astype(F32) + lax.ppermute(send, "wide", mates).astype(F32)).astype(BF16)

    def sum_chips(value):
        return lax.psum_scatter(
            value, "wide", scatter_dimension=2, tiled=True, axis_index_groups=parities
        )

    grads = [
        lax.psum_scatter(grad, "wide", scatter_dimension=2, tiled=True) for (grad,) in kept[:-1]
    ]

    def total(values):
        return sum(value.astype(F32) for value in values)

    expert_sum = sum_rows(backs, False)
    picked = (routes[:, :, None] == jnp.arange(E, dtype=jnp.int32)[None, None, :]).astype(F32)
    score_part = jnp.sum(picked * total(scores)[:, None, :E], axis=2)
    score_sum = sum_columns(score_part.T).T

    middle_back = after(middle_low, rows).astype(F32)
    scale_two_own = lax.rsqrt(jnp.mean(middle_back * middle_back, axis=1, keepdims=True) + EPSILON)
    normed_two_own = middle_back * scale_two_own
    expert_in_own = (normed_two_own * gain_two).astype(BF16)
    picked_own = own_rows(picked)
    logits_own = jnp.dot(expert_in_own, router_full, preferred_element_type=F32)
    gates_own = jax.nn.softmax(jnp.sum(picked_own * logits_own[:, None, :], axis=2), axis=1)
    centre = jnp.sum(gates_own * score_sum, axis=1, keepdims=True)
    logit_part = gates_own * (score_sum - centre)
    logit_grad = jnp.sum(picked_own * logit_part[:, :, None], axis=1).astype(BF16)
    norm_grad = expert_sum + jnp.einsum(
        "te,de->td", logit_grad, router_full, preferred_element_type=F32
    )
    row_dot = jnp.sum(norm_grad * normed_two_own * gain_two, axis=1, keepdims=True)
    gain_two_part = jnp.sum(norm_grad * normed_two_own, axis=0)
    mid_grad = cotangent.astype(F32) + scale_two_own * (
        gain_two * norm_grad - normed_two_own * row_dot / width
    )
    branch_grad = mid_grad.astype(BF16)
    mixed_grad_own = [
        jnp.einsum("td,dc->ct", branch_grad, block, preferred_element_type=F32).astype(BF16)
        for block in output_blocks
    ]
    third = sum_cores(*after(kept[-1], branch_grad))
    grads.append(sum_chips(third))
    mixed_grad = after(to_heads(mixed_grad_own), third)
    projected_grad = attend_backward(projected, mixed, log_totals, mixed_grad, groups, heads)
    grad_input_w = jnp.einsum(
        "td,ct->dc", attn_in, projected_grad, preferred_element_type=F32
    ).astype(BF16)
    block_rounds = sum_rows_start(after(outs, mixed_grad), False)
    came = block_rounds if isinstance(block_rounds, jax.Array) else block_rounds[0]
    input_part = jnp.einsum(
        "ct,dc->td", after(projected_grad, grads[0], came), input_full, preferred_element_type=F32
    ).astype(BF16)
    input_sum = sum_rows_end(sum_rows_start([input_part], False), grads[1])
    grad_output_w = sum_rows(
        [
            jnp.concatenate(
                [
                    jnp.einsum("ct,td->cd", block, branch_grad, preferred_element_type=F32).astype(
                        BF16
                    )
                    for block in after(mixed_own, input_sum)
                ],
                axis=0,
            )
        ],
        True,
    ).astype(BF16)
    block_output = (middle_own + sum_rows_end(block_rounds, input_sum)).astype(BF16)
    grad_router = jnp.einsum(
        "te,td->ed", logit_grad, expert_in_own, preferred_element_type=F32
    )
    x_own = after(block_input, projected_grad).astype(F32)
    scale_one_own = lax.rsqrt(jnp.mean(x_own * x_own, axis=1, keepdims=True) + EPSILON)
    normed_one_own = x_own * scale_one_own
    gain_one_part = jnp.sum(input_sum * normed_one_own, axis=0)
    small_part = jnp.concatenate([grad_router, gain_one_part[None], gain_two_part[None]], axis=0)
    small_sum = sum_along(after(sum_along(small_part, "wide"), grads[2]), "narrow")
    gain_own = lax.dynamic_slice_in_dim(small_sum[E:], me * gain_part, gain_part, 1)
    router_part = router_weight.shape[0]
    router_grad = lax.dynamic_slice_in_dim(
        small_sum[:E], lax.axis_index("wide") * router_part, router_part, 1
    ).T
    input_dot = jnp.sum(input_sum * normed_one_own * gain_one, axis=1, keepdims=True)
    input_grad = mid_grad + scale_one_own * (
        gain_one * input_sum - normed_one_own * input_dot / width
    )
    packed_grad = lax.psum_scatter(
        after(
            jnp.concatenate([grad_input_w, grad_output_w.T], axis=1), input_grad
        ),
        "wide",
        scatter_dimension=0,
        tiled=True,
    ).astype(F32)
    input_w_grad = packed_grad[:, :head_columns]
    output_w_grad = packed_grad[:, head_columns:].T
    grads = after(grads, input_grad)
    gate_grad, up_grad, down_grad = (
        jnp.concatenate([grad[index] for grad in grads], axis=0).astype(F32) for index in range(3)
    )
    return (
        block_output,
        input_grad,
        gain_own[0],
        input_w_grad,
        output_w_grad,
        gain_own[1],
        router_grad,
        gate_grad,
        up_grad,
        down_grad,
    )


def solution(mesh):
    placed = (
        P(("wide", "narrow"), None),
        P("wide", None),
        P("narrow"),
        P("wide", "narrow"),
        P("narrow", "wide"),
        P("narrow"),
        P("wide", None),
        P(None, "wide", "narrow"),
        P(None, "wide", "narrow"),
        P(None, "wide", "narrow"),
        P(("wide", "narrow"), None),
    )
    return jax.shard_map(
        local,
        mesh=mesh,
        in_specs=placed,
        out_specs=(
            P(("wide", "narrow"), None),
            P(("wide", "narrow"), None),
            P("narrow"),
            P("wide", "narrow"),
            P("narrow", "wide"),
            P("narrow"),
            P("wide", None),
            P(None, "wide", "narrow"),
            P(None, "wide", "narrow"),
            P(None, "wide", "narrow"),
        ),
        check_vma=False,
    )
```
